512 devices in a mesh: guide: 2 (over core), blk: 64 (over y, z), batch: 4 (over x).
Axes of the slice: x: 4, y: 8, z: 8, core: 2. Of those that a mesh axis runs over, the one named last changes fastest.
Arguments:
- hidden: bfloat16 [2, 64, 1536], P('guide', 'batch'), may hold values from -6 to 6
- w_qkv: bfloat16 [1536, 2560], P('blk'), may hold values from -0.15625 to 0.15625
- key_cache: bfloat16 [2, 64, 1024, 512], P('guide', 'batch', 'blk'), may hold values from -700 to 700
- value_cache: bfloat16 [2, 64, 1024, 512], P('guide', 'batch', 'blk'), may hold values from -6 to 6
- lengths: int32 [2, 64], P('guide', 'batch'), may hold values from 128 to 1024, as said below
- w_out: bfloat16 [1536, 1536], P('blk'), may hold values from -0.15625 to 0.15625
- router: bfloat16 [1536, 16], replicated, may hold values from -0.15625 to 0.15625
- routes: int32 [2, 64, 2], P('guide', 'batch'), may hold values from 0 to 15, all different within a row
- w_gate: bfloat16 [1536, 16384], P(None, 'blk'), may hold values from -0.15625 to 0.15625
- w_up: bfloat16 [1536, 16384], P(None, 'blk'), may hold values from -0.15625 to 0.15625
- w_down: bfloat16 [16384, 1536], P('blk'), may hold values from -0.125 to 0.125
- w_vocab: bfloat16 [1536, 65536], P(None, ('blk', 'batch')), may hold values from -0.15625 to 0.15625
- group_ids: int32 [64], replicated, may hold values from 0 to 7, never falling along the last dimension, each value on 1 to 16 neighbouring positions
- weight_index: int32 [8], replicated, may hold values from 0 to 7
- guidance_levels: float32 [8], replicated, may hold values from 1 to 5
Outputs:
- logits: float32 [64, 65536], P('guide', ('blk', 'batch'))
- new_keys: bfloat16 [2, 64, 512], P('guide', 'batch')
- new_values: bfloat16 [2, 64, 512], P('guide', 'batch')
The draws below stay inside these ranges and needn't reach their ends.
Inputs may be any that keep to these rules, and one draw needn't show every extreme that they name: `lengths`: every stream and index of batch has a request whose cache is full.
All inputs are finite; a program needn't handle non-finite values.
Results may differ from the reference program's by a relative error of at most 0.008.
Values may be sent and summed in bfloat16 or wider, within the bound.
No kernel may reach another device: no remote copies, remote signals or barrier semaphores. Data moves between devices by JAX's collectives and lax.ppermute only.
A program may use at most 64 MiB of HBM per device.

```python
import math
import jax
import jax.numpy as jnp
import numpy as np
from jax import lax

D = 1536
HEADS = 24
KV_HEADS = 8
HEAD_DIM = 64
EXPERTS = 16
EXPERT_UNITS = 1024
VOCAB = 65536
REQ_DEV = 16
LEVELS = 8
REQUESTS = 64
GROUPS = 8
CACHE = 1024


def draw_lengths(key, part):
    drawn = jax.random.randint(key, (2, REQUESTS), CACHE // 8, CACHE + 1)
    column = jnp.arange(REQUESTS)[None, :]
    block_start = column % REQ_DEV == 0
    return jnp.where(block_start, CACHE, drawn).astype(jnp.int32)


def draw_key_cache(key, part):
    key_base = jax.random.fold_in(key, 0)
    shape = (2, REQUESTS, CACHE, KV_HEADS * HEAD_DIM)
    base = jnp.clip(jax.random.normal(key_base, shape, jnp.float32), -4.0, 4.0)
    return base.astype(jnp.bfloat16)


def with_ends(entries, rng, low, high):
    longest = entries.shape.index(max(entries.shape))
    spots = []
    for shift in (0, 1):
        where = [jax.random.randint(jax.random.fold_in(rng, axis), (), 0, length) for axis, length in enumerate(entries.shape)]
        where[longest] = (where[longest] + shift) % entries.shape[longest]
        spots.append(tuple(where))
    return entries.at[spots[0]].set(low).at[spots[1]].set(high)


def block_levels(own_key, dims, cuts, smallest, high):
    loudness = 1.0
    for dim, blocks in cuts:
        steps = jax.random.uniform(jax.random.fold_in(jax.random.fold_in(own_key, 6), dim), (blocks,), jnp.float32, smallest / len(cuts), high / len(cuts))
        loudness = loudness * jnp.repeat(jnp.exp(steps), dims[dim] // blocks).reshape((-1,) + (1,) * (len(dims) - 1 - dim))
    return loudness


def choose_distinct(rng, rows, number_of, top, lift):
    order = jax.random.permutation(jax.random.fold_in(rng, 1), number_of)
    boost = order
    for power in range(3):
        boost = boost * boost // number_of
    boost = boost * lift // number_of
    lots = jax.random.randint(jax.random.fold_in(rng, 2), (rows, number_of), 0, 4096) + boost
    holders = jax.random.permutation(jax.random.fold_in(rng, 3), rows)[jnp.arange(number_of) % rows]
    lots = jnp.where(jnp.arange(rows)[:, None] == holders[None, :], 1 << 14, lots)
    priority = lots * number_of + jnp.arange(number_of)
    return lax.top_k(priority.astype(jnp.int32), top)[1].astype(jnp.int32)


def split_up(number_of, total, bound, skew):
    loads = [(1 << 20) // math.isqrt(grade ** skew) + 1 for grade in range(2, number_of + 1)]
    spare, holding = total - bound - (number_of - 1), [1] * (number_of - 1)
    while spare > 0:
        free = [i for i in range(number_of - 1) if holding[i] < bound]
        whole, budget = sum([loads[i] for i in free]), spare
        for i in free:
            extra = min(bound - holding[i], max(1, budget * loads[i] // whole), spare)
            holding[i] = holding[i] + extra
            spare = spare - extra
    return np.array([bound] + holding)


def ragged_sizes(rng, count, total, reach, lean):
    if count == 2:
        one = jax.random.randint(rng, (), max(1, total - reach), min(reach, total - 1) + 1)
        return jnp.stack([one, total - one])
    tallies = jnp.asarray(split_up(count, total, reach, lean), jnp.int32)
    couples = (count - 1) // 2
    giver, receiver = tallies[1:1 + 2 * couples:2], tallies[2:2 + 2 * couples:2]
    margin = jnp.minimum(giver - 1, reach - receiver)
    moved = jax.random.randint(jax.random.fold_in(rng, 1), (couples,), 0, 1 << 20) % (margin + 1)
    tallies = tallies.at[1:1 + 2 * couples:2].set(giver - moved).at[2:2 + 2 * couples:2].set(receiver + moved)
    return tallies[jax.random.permutation(jax.random.fold_in(rng, 2), count)]


def centred(own_key, dims, width, reach, shards=(), held_as=jnp.bfloat16):
    entries = jax.random.normal(own_key, dims, jnp.float32) * width
    if len(shards) > 0:
        entries = block_levels(own_key, dims, shards, -0.22, 0.18) * entries
    return jnp.clip(entries, min=-reach, max=reach).astype(held_as)


def setup_inputs(seed: int = 0) -> dict:
    key_list = jax.random.split(jax.random.key(seed), 16)
    hidden = centred(key_list[0], (2, REQUESTS, D), 1.0, 6.0, ((0, 2), (1, 4)))
    w_qkv = centred(key_list[1], (D, (HEADS + 2 * KV_HEADS) * HEAD_DIM), D ** -0.5, 0.15625, ((0, 64),))
    key_cache = draw_key_cache(jax.random.fold_in(key_list[15], 71), 0)
    value_cache = centred(key_list[3], (2, REQUESTS, CACHE, KV_HEADS * HEAD_DIM), 1.0, 6.0, ((0, 2), (1, 4), (2, 64)))
    lengths = draw_lengths(jax.random.fold_in(key_list[15], 71), 0)
    w_out = centred(key_list[5], (HEADS * HEAD_DIM, D), (HEADS * HEAD_DIM) ** -0.5, 0.15625, ((0, 64),))
    router = centred(key_list[6], (D, EXPERTS), D ** -0.5, 0.15625)
    routes = choose_distinct(key_list[7], 2 * REQUESTS, EXPERTS, 2, 1024).reshape((2, REQUESTS, 2))
    w_gate = centred(key_list[8], (D, EXPERTS * EXPERT_UNITS), D ** -0.5, 0.15625, ((1, 64),))
    w_up = centred(key_list[9], (D, EXPERTS * EXPERT_UNITS), D ** -0.5, 0.15625, ((1, 64),))
    w_down = centred(key_list[10], (EXPERTS * EXPERT_UNITS, D), (2 * EXPERT_UNITS) ** -0.5, 0.125, ((0, 64),))
    w_vocab = centred(key_list[11], (D, VOCAB), D ** -0.5, 0.15625, ((1, 256),))
    group_ids = jnp.searchsorted(jnp.cumsum(ragged_sizes(key_list[12], GROUPS, REQUESTS, 16, 0)), jnp.arange(REQUESTS), side="right").astype(jnp.int32)
    weight_index = with_ends(jax.random.randint(key_list[13], (GROUPS,), 0, LEVELS), jax.random.fold_in(key_list[13], 1), 0, LEVELS - 1).astype(jnp.int32)
    guidance_levels = jnp.clip(jax.random.uniform(key_list[14], (LEVELS,), jnp.float32, 1.0, 5.0), 1.0, 5.0)
    return {"hidden": hidden, "w_qkv": w_qkv, "key_cache": key_cache, "value_cache": value_cache, "lengths": lengths, "w_out": w_out, "router": router, "routes": routes, "w_gate": w_gate, "w_up": w_up, "w_down": w_down, "w_vocab": w_vocab, "group_ids": group_ids, "weight_index": weight_index, "guidance_levels": guidance_levels}


EPS = 1e-05

def rms(values):
    return values * lax.rsqrt(lax.optimization_barrier(jnp.mean(values * values, axis=-1, keepdims=True)) + EPS)

def stream_pass(x_in, key_c, value_c, lens, w_qkv, w_out, router, routes_s, w_gate, w_up, w_down, w_vocab):
    width_q = HEADS * HEAD_DIM
    width_k = KV_HEADS * HEAD_DIM
    group = HEADS // KV_HEADS
    count = x_in.shape[0]
    x = x_in.astype(jnp.float32)
    normed = rms(x).astype(jnp.bfloat16)
    qkv = jnp.dot(normed, w_qkv, preferred_element_type=jnp.float32)
    query = qkv[:, :width_q].astype(jnp.bfloat16)
    new_key = qkv[:, width_q:width_q + width_k].astype(jnp.bfloat16)
    new_value = qkv[:, width_q + width_k:].astype(jnp.bfloat16)
    qf = query.astype(jnp.float32).reshape(count, KV_HEADS, group, HEAD_DIM)
    kf = key_c.astype(jnp.float32).reshape(count, CACHE, KV_HEADS, HEAD_DIM)
    vf = value_c.astype(jnp.float32).reshape(count, CACHE, KV_HEADS, HEAD_DIM)
    scale = HEAD_DIM ** (-0.5)
    scores = jnp.einsum('rkgd,rckd->rkgc', qf, kf) * scale
    own = jnp.einsum('rkgd,rkd->rkg', qf, new_key.astype(jnp.float32).reshape(count, KV_HEADS, HEAD_DIM)) * scale
    valid = (jnp.arange(CACHE)[None, :] < lens[:, None])[:, None, None, :]
    top = jnp.maximum(lax.optimization_barrier(jnp.max(jnp.where(valid, scores, -1e+30), axis=-1)), own)
    probs = jnp.exp(jnp.where(valid, scores - top[..., None], -1e+30))
    own_prob = jnp.exp(own - top)
    total = lax.optimization_barrier(jnp.sum(probs, axis=-1)) + own_prob
    probs_r = lax.optimization_barrier(probs.astype(jnp.bfloat16)).astype(jnp.float32)
    own_r = lax.optimization_barrier(own_prob.astype(jnp.bfloat16)).astype(jnp.float32)
    acc = jnp.einsum('rkgc,rckd->rkgd', probs_r, vf)
    acc = acc + own_r[..., None] * new_value.astype(jnp.float32).reshape(count, KV_HEADS, 1, HEAD_DIM)
    attn = (acc / total[..., None]).reshape(count, width_q).astype(jnp.bfloat16)
    mixed = x + jnp.dot(attn, w_out, preferred_element_type=jnp.float32)
    expert_in = rms(mixed).astype(jnp.bfloat16)
    choice_logits = jnp.dot(expert_in, router, preferred_element_type=jnp.float32)
    picks = (routes_s[:, :, None] == jnp.arange(EXPERTS)[None, None, :]).astype(jnp.float32)
    chosen = lax.optimization_barrier(jnp.sum(picks * choice_logits[:, None, :], axis=-1))
    first = jax.nn.sigmoid(chosen[:, 0] - chosen[:, 1])
    shares = jnp.stack([first, 1.0 - first], axis=1)
    per_expert = lax.optimization_barrier(jnp.sum(picks * shares[:, :, None], axis=1))
    unit_weight = jnp.repeat(per_expert, EXPERT_UNITS, axis=1)
    gate = jnp.dot(expert_in, w_gate, preferred_element_type=jnp.float32)
    upper = jnp.dot(expert_in, w_up, preferred_element_type=jnp.float32)
    act = (jax.nn.silu(gate) * upper * unit_weight).astype(jnp.bfloat16)
    outgoing = mixed + jnp.dot(act, w_down, preferred_element_type=jnp.float32)
    final_in = rms(outgoing).astype(jnp.bfloat16)
    stream_logits = jnp.dot(final_in, w_vocab, preferred_element_type=jnp.float32).astype(jnp.bfloat16)
    return (stream_logits, new_key, new_value)

def reference(hidden, w_qkv, key_cache, value_cache, lengths, w_out, router, routes, w_gate, w_up, w_down, w_vocab, group_ids, weight_index, guidance_levels):
    results = []
    for stream in range(2):
        results.append(stream_pass(hidden[stream], key_cache[stream], value_cache[stream], lengths[stream], w_qkv, w_out, router, routes[stream], w_gate, w_up, w_down, w_vocab))
    cond = results[0][0].astype(jnp.float32)
    uncond = results[1][0].astype(jnp.float32)
    member = (group_ids[:, None] == jnp.arange(GROUPS)[None, :]).astype(jnp.float32)
    level_pick = (weight_index[:, None] == jnp.arange(LEVELS)[None, :]).astype(jnp.float32)
    group_weight = lax.optimization_barrier(jnp.sum(level_pick * guidance_levels[None, :], axis=1))
    request_weight = lax.optimization_barrier(jnp.sum(member * group_weight[None, :], axis=1))
    logits = uncond + request_weight[:, None] * (cond - uncond)
    new_keys = jnp.stack([results[0][1], results[1][1]], axis=0)
    new_values = jnp.stack([results[0][2], results[1][2]], axis=0)
    return (logits, new_keys, new_values)
```

```python
import jax
import jax.numpy as jnp
from jax import lax
from jax.sharding import Mesh, PartitionSpec as P

HEADS = 24
KV_HEADS = 8
HEAD_DIM = 64
EXPERTS = 16
EXPERT_UNITS = 1024
EPS = 1e-05
F32 = jnp.float32
BF16 = jnp.bfloat16
BLK = ("y", "z")


def rms(values):
    return values * lax.rsqrt(jnp.mean(values * values, axis=-1, keepdims=True) + EPS)


def exchange(value, axes):
    return lax.all_to_all(value, axes, 0, 0, tiled=True)


def halves(value):
    high = lax.reduce_precision(value, 8, 7)
    return high.astype(BF16), (value - high).astype(BF16)


def local(
    hidden,
    w_qkv,
    key_cache,
    value_cache,
    lengths,
    w_out,
    router,
    routes,
    w_gate,
    w_up,
    w_down,
    w_vocab,
    group_ids,
    weight_index,
    guidance_levels,
):
    group = HEADS // KV_HEADS
    y, z = lax.axis_index("y"), lax.axis_index("z")
    ny, nz = lax.axis_size("y"), lax.axis_size("z")
    blocks = ny * nz
    block = y * nz + z
    count = hidden.shape[1]
    pair = count // nz
    width = hidden.shape[2]
    width_q = HEADS * HEAD_DIM
    width_k = KV_HEADS * HEAD_DIM
    head_w = gathered_rows(w_out)

    x = hidden[0].astype(F32)
    normed = rms(x).astype(BF16)
    rows = w_qkv.shape[0]
    part = lax.dynamic_slice_in_dim(normed, block * rows, rows, 1)
    qkv = jnp.dot(part, w_qkv, preferred_element_type=F32)
    q = qkv[:, :width_q].reshape(pair, nz, KV_HEADS, group, HEAD_DIM)
    k = qkv[:, width_q : width_q + width_k].reshape(pair, nz, KV_HEADS, 1, HEAD_DIM)
    v = qkv[:, width_q + width_k :].reshape(pair, nz, KV_HEADS, 1, HEAD_DIM)
    upper = jnp.concatenate([k, v, jnp.zeros_like(k)], axis=3)
    lines = jnp.concatenate([q, upper], axis=4).transpose(2, 1, 0, 3, 4)
    lines = lines.reshape(blocks, pair * group, 2 * HEAD_DIM)
    high, low = halves(lines)
    span = key_cache.shape[2]
    kc = key_cache[0].reshape(pair, nz, span, KV_HEADS, HEAD_DIM)
    vc = value_cache[0].reshape(pair, nz, span, KV_HEADS, HEAD_DIM)
    kv = jnp.concatenate([kc, vc], axis=4).transpose(3, 1, 0, 2, 4)
    kv = kv.reshape(blocks, pair * span, 2 * HEAD_DIM)
    fill = jnp.zeros((blocks, 4, 2 * HEAD_DIM), BF16)
    got = exchange(jnp.concatenate([kv, high, low, fill], axis=1), BLK)

    n_kv, n_l = pair * span, pair * group
    kv = got[:, :n_kv].reshape(blocks, pair, span, 2 * HEAD_DIM).transpose(1, 0, 2, 3)
    kv = kv.reshape(pair, blocks * span, 2 * HEAD_DIM)
    sums = jnp.sum(
        got[:, n_kv : n_kv + n_l].astype(F32) + got[:, n_kv + n_l : n_kv + 2 * n_l].astype(F32), axis=0
    )
    sums = sums.reshape(pair, group, 2 * HEAD_DIM).astype(BF16)
    query, new_k, new_v = sums[:, :, :HEAD_DIM], sums[:, 0, HEAD_DIM:], sums[:, 1, HEAD_DIM:]
    scale = HEAD_DIM ** (-0.5)
    scores = jnp.einsum("ihd,ipd->ihp", query, kv[:, :, :HEAD_DIM], preferred_element_type=F32) * scale
    own = jnp.sum(query.astype(F32) * new_k.astype(F32)[:, None, :], axis=-1) * scale
    lens = lax.dynamic_index_in_dim(lengths[0].reshape(pair, nz), z, 1, False)
    valid = (jnp.arange(blocks * span)[None, :] < lens[:, None])[:, None, :]
    top = jnp.maximum(jnp.max(jnp.where(valid, scores, -1e30), axis=-1), own)
    probs = jnp.exp(jnp.where(valid, scores - top[..., None], -1e30))
    own_prob = jnp.exp(own - top)
    total = jnp.sum(probs, axis=-1) + own_prob
    acc = jnp.einsum("ihp,ipd->ihd", probs.astype(BF16), kv[:, :, HEAD_DIM:], preferred_element_type=F32)
    own_r = lax.reduce_precision(own_prob, 8, 7)
    acc = acc + own_r[..., None] * new_v.astype(F32)[:, None, :]
    attn = (acc / total[..., None]).astype(BF16).reshape(pair, group * HEAD_DIM)
    part = jnp.dot(attn, head_w, preferred_element_type=F32).astype(BF16)
    part = part.reshape(pair * width // 128, 128)
    got = exchange(jnp.broadcast_to(part[None], (blocks,) + part.shape), BLK)

    got = jnp.sum(got.reshape(ny, nz, pair, width).astype(F32), axis=0)
    mixed = x + got.transpose(1, 0, 2).reshape(count, width)
    expert_in = rms(mixed).astype(BF16)
    choice_logits = jnp.dot(expert_in, router, preferred_element_type=F32)
    picks = (routes[0][:, :, None] == jnp.arange(EXPERTS)[None, None, :]).astype(F32)
    chosen = jnp.sum(picks * choice_logits[:, None, :], axis=-1)
    first = jax.nn.sigmoid(chosen[:, 0] - chosen[:, 1])
    shares = jnp.stack([first, 1.0 - first], axis=1)
    per_expert = jnp.sum(picks * shares[:, :, None], axis=1)
    units = w_gate.shape[1]
    owner = (block * units + jnp.arange(units)) // EXPERT_UNITS
    member = (owner[None, :] == jnp.arange(EXPERTS)[:, None]).astype(F32)
    unit_weight = jnp.sum(per_expert[:, :, None] * member[None, :, :], axis=1)
    gate = jnp.dot(expert_in, w_gate, preferred_element_type=F32)
    upper = jnp.dot(expert_in, w_up, preferred_element_type=F32)
    act = (jax.nn.silu(gate) * upper * unit_weight).astype(BF16)
    expert_out = jnp.dot(act, w_down, preferred_element_type=F32)
    own_lines = count * width // blocks // 128
    high, low = halves(expert_out.reshape(blocks, own_lines, 128))
    fresh = jnp.concatenate([new_k, new_v], axis=1)
    fresh = jnp.broadcast_to(fresh[None], (blocks,) + fresh.shape)
    got = exchange(jnp.concatenate([high, low, fresh], axis=1), BLK)

    piece = jnp.sum(got[:, :own_lines].astype(F32) + got[:, own_lines : 2 * own_lines].astype(F32), axis=0)
    mixed_piece = lax.dynamic_index_in_dim(mixed.reshape(blocks, own_lines, 128), block, 0, False)
    piece = (mixed_piece + piece).astype(BF16)
    piece = jnp.concatenate([piece, jnp.zeros((1, 128), BF16)], axis=0)
    everyone = blocks * lax.axis_size("batch")
    fresh = got[:, 2 * own_lines :].reshape(ny, nz, pair, 2, HEAD_DIM).transpose(3, 2, 1, 0, 4)
    fresh = fresh.reshape(2, count, width_k)
    got = exchange(jnp.broadcast_to(piece[None], (everyone,) + piece.shape), ("batch",) + BLK)
    outgoing = got[:, :own_lines].reshape(-1, width).astype(F32)
    final_in = rms(outgoing).astype(BF16)
    stream_logits = jnp.dot(final_in, w_vocab, preferred_element_type=F32).astype(BF16)
    stream = lax.axis_index("guide")
    half_rows = stream_logits.shape[0] // 2
    kept = lax.dynamic_slice_in_dim(stream_logits, stream * half_rows, half_rows, 0)
    sent = lax.dynamic_slice_in_dim(stream_logits, (1 - stream) * half_rows, half_rows, 0)
    partner = lax.ppermute(sent, "guide", [(0, 1), (1, 0)])
    is_first = stream == 0
    cond = jnp.where(is_first, kept, partner).astype(F32)
    uncond = jnp.where(is_first, partner, kept).astype(F32)
    group_count = weight_index.shape[0]
    level_count = guidance_levels.shape[0]
    in_group = (group_ids[:, None] == jnp.arange(group_count)[None, :]).astype(F32)
    level_pick = (weight_index[:, None] == jnp.arange(level_count)[None, :]).astype(F32)
    group_weight = jnp.sum(level_pick * guidance_levels[None, :], axis=1)
    request_weight = jnp.sum(in_group * group_weight[None, :], axis=1)
    weight_rows = lax.dynamic_slice_in_dim(request_weight, stream * half_rows, half_rows, 0)
    logits = uncond + weight_rows[:, None] * (cond - uncond)
    return (logits, fresh[0][None], fresh[1][None])


def gathered_rows(w_out):
    return lax.all_gather(w_out, "z", axis=0, tiled=True)


def solution(mesh):
    guide, blk, batch = (mesh.shape[a] for a in ("guide", "blk", "batch"))
    ny = KV_HEADS
    mesh = Mesh(mesh.devices.reshape(guide, ny, blk // ny, batch), ("guide",) + BLK + ("batch",))
    placed = (
        P("guide", "batch", None),
        P(BLK, None),
        P("guide", "batch", BLK, None),
        P("guide", "batch", BLK, None),
        P("guide", "batch"),
        P(BLK, None),
        P(),
        P("guide", "batch", None),
        P(None, BLK),
        P(None, BLK),
        P(BLK, None),
        P(None, BLK + ("batch",)),
        P(),
        P(),
        P(),
    )
    return jax.shard_map(
        local,
        mesh=mesh,
        in_specs=placed,
        out_specs=(
            P("guide", BLK + ("batch",)),
            P("guide", "batch", None),
            P("guide", "batch", None),
        ),
        check_vma=False,
    )
```

```python
import jax
import jax.numpy as jnp
from jax import lax
from jax.sharding import Mesh, PartitionSpec as P

HEADS = 24
KV_HEADS = 8
HEAD_DIM = 64
EXPERTS = 16
EXPERT_UNITS = 1024
EPS = 1e-05
F32 = jnp.float32
BF16 = jnp.bfloat16
BLK = ("y", "z")


def rms(values):
    return values * lax.rsqrt(jnp.mean(values * values, axis=-1, keepdims=True) + EPS)


def exchange(value, axes):
    return lax.all_to_all(value, axes, 0, 0, tiled=True)


def halves(value):
    high = lax.reduce_precision(value, 8, 7)
    return high.astype(BF16), (value - high).astype(BF16)


def local(
    hidden,
    w_qkv,
    key_cache,
    value_cache,
    lengths,
    w_out,
    router,
    routes,
    w_gate,
    w_up,
    w_down,
    w_vocab,
    group_ids,
    weight_index,
    guidance_levels,
):
    group = HEADS // KV_HEADS
    y, z = lax.axis_index("y"), lax.axis_index("z")
    ny, nz = lax.axis_size("y"), lax.axis_size("z")
    blocks = ny * nz
    block = y * nz + z
    count = hidden.shape[1]
    pair = count // nz
    width = hidden.shape[2]
    width_q = HEADS * HEAD_DIM
    width_k = KV_HEADS * HEAD_DIM
    head_w = gathered_rows(w_out)

    x = hidden[0].astype(F32)
    normed = rms(x).astype(BF16)
    rows = w_qkv.shape[0]
    part = lax.dynamic_slice_in_dim(normed, block * rows, rows, 1)
    qkv = jnp.dot(part, w_qkv, preferred_element_type=F32)
    q = qkv[:, :width_q].reshape(pair, nz, KV_HEADS, group, HEAD_DIM)
    k = qkv[:, width_q : width_q + width_k].reshape(pair, nz, KV_HEADS, 1, HEAD_DIM)
    v = qkv[:, width_q + width_k :].reshape(pair, nz, KV_HEADS, 1, HEAD_DIM)
    upper = jnp.concatenate([k, v, jnp.zeros_like(k)], axis=3)
    lines = jnp.concatenate([q, upper], axis=4).transpose(2, 1, 0, 3, 4)
    lines = lines.reshape(blocks, pair * group, 2 * HEAD_DIM)
    high, low = halves(lines)
    span = key_cache.shape[2]
    kc = key_cache[0].reshape(pair, nz, span, KV_HEADS, HEAD_DIM)
    vc = value_cache[0].reshape(pair, nz, span, KV_HEADS, HEAD_DIM)
    kv = jnp.concatenate([kc, vc], axis=4).transpose(3, 1, 0, 2, 4)
    kv = kv.reshape(blocks, pair * span, 2 * HEAD_DIM)
    fill = jnp.zeros((blocks, 4, 2 * HEAD_DIM), BF16)
    got = exchange(jnp.concatenate([kv, high, low, fill], axis=1), BLK)

    n_kv, n_l = pair * span, pair * group
    kv = got[:, :n_kv].reshape(blocks, pair, span, 2 * HEAD_DIM).transpose(1, 0, 2, 3)
    kv = kv.reshape(pair, blocks * span, 2 * HEAD_DIM)
    sums = jnp.sum(
        got[:, n_kv : n_kv + n_l].astype(F32) + got[:, n_kv + n_l : n_kv + 2 * n_l].astype(F32), axis=0
    )
    sums = sums.reshape(pair, group, 2 * HEAD_DIM).astype(BF16)
    query, new_k, new_v = sums[:, :, :HEAD_DIM], sums[:, 0, HEAD_DIM:], sums[:, 1, HEAD_DIM:]
    scale = HEAD_DIM ** (-0.5)
    scores = jnp.einsum("ihd,ipd->ihp", query, kv[:, :, :HEAD_DIM], preferred_element_type=F32) * scale
    own = jnp.sum(query.astype(F32) * new_k.astype(F32)[:, None, :], axis=-1) * scale
    lens = lax.dynamic_index_in_dim(lengths[0].reshape(pair, nz), z, 1, False)
    valid = (jnp.arange(blocks * span)[None, :] < lens[:, None])[:, None, :]
    top = jnp.maximum(jnp.max(jnp.where(valid, scores, -1e30), axis=-1), own)
    probs = jnp.exp(jnp.where(valid, scores - top[..., None], -1e30))
    own_prob = jnp.exp(own - top)
    total = jnp.sum(probs, axis=-1) + own_prob
    acc = jnp.einsum("ihp,ipd->ihd", probs.astype(BF16), kv[:, :, HEAD_DIM:], preferred_element_type=F32)
    own_r = lax.reduce_precision(own_prob, 8, 7)
    acc = acc + own_r[..., None] * new_v.astype(F32)[:, None, :]
    attn = (acc / total[..., None]).astype(BF16).reshape(pair, group * HEAD_DIM)
    part = jnp.dot(attn, head_w, preferred_element_type=F32).astype(BF16)
    part = part.reshape(pair * width // 128, 128)
    got = exchange(jnp.broadcast_to(part[None], (blocks,) + part.shape), BLK)

    got = jnp.sum(got.reshape(ny, nz, pair, width).astype(F32), axis=0)
    mixed = x + got.transpose(1, 0, 2).reshape(count, width)
    expert_in = rms(mixed).astype(BF16)
    choice_logits = jnp.dot(expert_in, router, preferred_element_type=F32)
    picks = (routes[0][:, :, None] == jnp.arange(EXPERTS)[None, None, :]).astype(F32)
    chosen = jnp.sum(picks * choice_logits[:, None, :], axis=-1)
    first = jax.nn.sigmoid(chosen[:, 0] - chosen[:, 1])
    shares = jnp.stack([first, 1.0 - first], axis=1)
    per_expert = jnp.sum(picks * shares[:, :, None], axis=1)
    units = w_gate.shape[1]
    owner = (block * units + jnp.arange(units)) // EXPERT_UNITS
    member = (owner[None, :] == jnp.arange(EXPERTS)[:, None]).astype(F32)
    unit_weight = jnp.sum(per_expert[:, :, None] * member[None, :, :], axis=1)
    gate = jnp.dot(expert_in, w_gate, preferred_element_type=F32)
    upper = jnp.dot(expert_in, w_up, preferred_element_type=F32)
    act = (jax.nn.silu(gate) * upper * unit_weight).astype(BF16)
    expert_out = jnp.dot(act, w_down, preferred_element_type=F32)
    own_lines = count * width // blocks // 128
    high, low = halves(expert_out.reshape(blocks, own_lines, 128))
    fresh = jnp.concatenate([new_k, new_v], axis=1)
    fresh = jnp.broadcast_to(fresh[None], (blocks,) + fresh.shape)
    got = exchange(jnp.concatenate([high, low, fresh], axis=1), BLK)

    piece = jnp.sum(got[:, :own_lines].astype(F32) + got[:, own_lines : 2 * own_lines].astype(F32), axis=0)
    mixed_piece = lax.dynamic_index_in_dim(mixed.reshape(blocks, own_lines, 128), block, 0, False)
    piece = (mixed_piece + piece).astype(BF16)
    piece = jnp.concatenate([piece, jnp.zeros((1, 128), BF16)], axis=0)
    everyone = blocks * lax.axis_size("batch")
    fresh = got[:, 2 * own_lines :].reshape(ny, nz, pair, 2, HEAD_DIM).transpose(3, 2, 1, 0, 4)
    fresh = fresh.reshape(2, count, width_k)
    got = exchange(jnp.broadcast_to(piece[None], (everyone,) + piece.shape), ("batch",) + BLK)
    outgoing = got[:, :own_lines].reshape(-1, width).astype(F32)
    final_in = rms(outgoing).astype(BF16)
    stream_logits = jnp.dot(final_in, w_vocab, preferred_element_type=F32).astype(BF16)
    stream = lax.axis_index("guide")
    half_rows = stream_logits.shape[0] // 2
    kept = lax.dynamic_slice_in_dim(stream_logits, stream * half_rows, half_rows, 0)
    sent = lax.dynamic_slice_in_dim(stream_logits, (1 - stream) * half_rows, half_rows, 0)
    partner = lax.ppermute(sent, "guide", [(0, 1), (1, 0)])
    is_first = stream == 0
    cond = jnp.where(is_first, kept, partner).astype(F32)
    uncond = jnp.where(is_first, partner, kept).astype(F32)
    group_count = weight_index.shape[0]
    level_count = guidance_levels.shape[0]
    in_group = (group_ids[:, None] == jnp.arange(group_count)[None, :]).astype(F32)
    level_pick = (weight_index[:, None] == jnp.arange(level_count)[None, :]).astype(F32)
    group_weight = jnp.sum(level_pick * guidance_levels[None, :], axis=1)
    request_weight = jnp.sum(in_group * group_weight[None, :], axis=1)
    weight_rows = lax.dynamic_slice_in_dim(request_weight, stream * half_rows, half_rows, 0)
    logits = uncond + weight_rows[:, None] * (cond - uncond)
    return (logits, fresh[0][None], fresh[1][None])


def gathered_rows(w_out):
    rows, width = w_out.shape
    size = lax.axis_size("z") * width * 2
    want = -(-(2**20) // size)
    want += -want % 4
    padded = jnp.concatenate([w_out, w_out[: want - rows]], axis=0)
    gathered = lax.all_gather(padded, "z", axis=0, tiled=False)
    return gathered[:, :rows].reshape(-1, width)


def solution(mesh):
    guide, blk, batch = (mesh.shape[a] for a in ("guide", "blk", "batch"))
    ny = KV_HEADS
    mesh = Mesh(mesh.devices.reshape(guide, ny, blk // ny, batch), ("guide",) + BLK + ("batch",))
    placed = (
        P("guide", "batch", None),
        P(BLK, None),
        P("guide", "batch", BLK, None),
        P("guide", "batch", BLK, None),
        P("guide", "batch"),
        P(BLK, None),
        P(),
        P("guide", "batch", None),
        P(None, BLK),
        P(None, BLK),
        P(BLK, None),
        P(None, BLK + ("batch",)),
        P(),
        P(),
        P(),
    )
    return jax.shard_map(
        local,
        mesh=mesh,
        in_specs=placed,
        out_specs=(
            P("guide", BLK + ("batch",)),
            P("guide", "batch", None),
            P("guide", "batch", None),
        ),
        check_vma=False,
    )
```

```python
import jax
import jax.numpy as jnp
from jax import lax
from jax.sharding import Mesh, PartitionSpec as P

HEADS = 24
KV_HEADS = 8
HEAD_DIM = 64
EXPERTS = 16
EXPERT_UNITS = 1024
EPS = 1e-05
F32 = jnp.float32
BF16 = jnp.bfloat16
BLK = ("y", "z")


def rms(values):
    return values * lax.rsqrt(jnp.mean(values * values, axis=-1, keepdims=True) + EPS)


def exchange(value, axes):
    return lax.all_to_all(value, axes, 0, 0, tiled=True)


def halves(value):
    high = lax.reduce_precision(value, 8, 7)
    return high.astype(BF16), (value - high).astype(BF16)


def local(
    hidden,
    w_qkv,
    key_cache,
    value_cache,
    lengths,
    w_out,
    router,
    routes,
    w_gate,
    w_up,
    w_down,
    w_vocab,
    group_ids,
    weight_index,
    guidance_levels,
):
    group = HEADS // KV_HEADS
    y, z = lax.axis_index("y"), lax.axis_index("z")
    ny, nz = lax.axis_size("y"), lax.axis_size("z")
    blocks = ny * nz
    block = y * nz + z
    count = hidden.shape[1]
    pair = count // nz
    width = hidden.shape[2]
    width_q = HEADS * HEAD_DIM
    width_k = KV_HEADS * HEAD_DIM
    head_w = gathered_rows(w_out)

    x = hidden[0].astype(F32)
    normed = rms(x).astype(BF16)
    rows = w_qkv.shape[0]
    part = lax.dynamic_slice_in_dim(normed, block * rows, rows, 1)
    qkv = jnp.dot(part, w_qkv, preferred_element_type=F32)
    q = qkv[:, :width_q].reshape(pair, nz, KV_HEADS, group, HEAD_DIM)
    k = qkv[:, width_q : width_q + width_k].reshape(pair, nz, KV_HEADS, 1, HEAD_DIM)
    v = qkv[:, width_q + width_k :].reshape(pair, nz, KV_HEADS, 1, HEAD_DIM)
    upper = jnp.concatenate([k, v, jnp.zeros_like(k)], axis=3)
    lines = jnp.concatenate([q, upper], axis=4).transpose(2, 1, 0, 3, 4)
    lines = lines.reshape(blocks, pair * group, 2 * HEAD_DIM)
    high, low = halves(lines)
    span = key_cache.shape[2]
    kc = key_cache[0].reshape(pair, nz, span, KV_HEADS, HEAD_DIM)
    vc = value_cache[0].reshape(pair, nz, span, KV_HEADS, HEAD_DIM)
    kv = jnp.concatenate([kc, vc], axis=4).transpose(3, 1, 0, 2, 4)
    kv = kv.reshape(blocks, pair * span, 2 * HEAD_DIM)
    fill = jnp.zeros((blocks, 4, 2 * HEAD_DIM), BF16)
    got = exchange(jnp.concatenate([kv, high, low, fill], axis=1), BLK)
    got, head_w = lax.optimization_barrier((got, head_w))

    n_kv, n_l = pair * span, pair * group
    kv = got[:, :n_kv].reshape(blocks, pair, span, 2 * HEAD_DIM).transpose(1, 0, 2, 3)
    kv = kv.reshape(pair, blocks * span, 2 * HEAD_DIM)
    sums = jnp.sum(
        got[:, n_kv : n_kv + n_l].astype(F32) + got[:, n_kv + n_l : n_kv + 2 * n_l].astype(F32), axis=0
    )
    sums = sums.reshape(pair, group, 2 * HEAD_DIM).astype(BF16)
    query, new_k, new_v = sums[:, :, :HEAD_DIM], sums[:, 0, HEAD_DIM:], sums[:, 1, HEAD_DIM:]
    scale = HEAD_DIM ** (-0.5)
    scores = jnp.einsum("ihd,ipd->ihp", query, kv[:, :, :HEAD_DIM], preferred_element_type=F32) * scale
    own = jnp.sum(query.astype(F32) * new_k.astype(F32)[:, None, :], axis=-1) * scale
    lens = lax.dynamic_index_in_dim(lengths[0].reshape(pair, nz), z, 1, False)
    valid = (jnp.arange(blocks * span)[None, :] < lens[:, None])[:, None, :]
    top = jnp.maximum(jnp.max(jnp.where(valid, scores, -1e30), axis=-1), own)
    probs = jnp.exp(jnp.where(valid, scores - top[..., None], -1e30))
    own_prob = jnp.exp(own - top)
    total = jnp.sum(probs, axis=-1) + own_prob
    acc = jnp.einsum("ihp,ipd->ihd", probs.astype(BF16), kv[:, :, HEAD_DIM:], preferred_element_type=F32)
    own_r = lax.reduce_precision(own_prob, 8, 7)
    acc = acc + own_r[..., None] * new_v.astype(F32)[:, None, :]
    attn = (acc / total[..., None]).astype(BF16).reshape(pair, group * HEAD_DIM)
    part = jnp.dot(attn, head_w, preferred_element_type=F32).astype(BF16)
    part = part.reshape(pair * width // 128, 128)
    got = exchange(jnp.broadcast_to(part[None], (blocks,) + part.shape), BLK)

    got = jnp.sum(got.reshape(ny, nz, pair, width).astype(F32), axis=0)
    mixed = x + got.transpose(1, 0, 2).reshape(count, width)
    expert_in = rms(mixed).astype(BF16)
    choice_logits = jnp.dot(expert_in, router, preferred_element_type=F32)
    picks = (routes[0][:, :, None] == jnp.arange(EXPERTS)[None, None, :]).astype(F32)
    chosen = jnp.sum(picks * choice_logits[:, None, :], axis=-1)
    first = jax.nn.sigmoid(chosen[:, 0] - chosen[:, 1])
    shares = jnp.stack([first, 1.0 - first], axis=1)
    per_expert = jnp.sum(picks * shares[:, :, None], axis=1)
    units = w_gate.shape[1]
    owner = (block * units + jnp.arange(units)) // EXPERT_UNITS
    member = (owner[None, :] == jnp.arange(EXPERTS)[:, None]).astype(F32)
    unit_weight = jnp.sum(per_expert[:, :, None] * member[None, :, :], axis=1)
    gate = jnp.dot(expert_in, w_gate, preferred_element_type=F32)
    upper = jnp.dot(expert_in, w_up, preferred_element_type=F32)
    act = (jax.nn.silu(gate) * upper * unit_weight).astype(BF16)
    expert_out = jnp.dot(act, w_down, preferred_element_type=F32)
    own_lines = count * width // blocks // 128
    high, low = halves(expert_out.reshape(blocks, own_lines, 128))
    fresh = jnp.concatenate([new_k, new_v], axis=1)
    fresh = jnp.broadcast_to(fresh[None], (blocks,) + fresh.shape)
    got = exchange(jnp.concatenate([high, low, fresh], axis=1), BLK)

    piece = jnp.sum(got[:, :own_lines].astype(F32) + got[:, own_lines : 2 * own_lines].astype(F32), axis=0)
    mixed_piece = lax.dynamic_index_in_dim(mixed.reshape(blocks, own_lines, 128), block, 0, False)
    piece = (mixed_piece + piece).astype(BF16)
    piece = jnp.concatenate([piece, jnp.zeros((1, 128), BF16)], axis=0)
    everyone = blocks * lax.axis_size("batch")
    fresh = got[:, 2 * own_lines :].reshape(ny, nz, pair, 2, HEAD_DIM).transpose(3, 2, 1, 0, 4)
    fresh = fresh.reshape(2, count, width_k)
    got = exchange(jnp.broadcast_to(piece[None], (everyone,) + piece.shape), ("batch",) + BLK)
    outgoing = got[:, :own_lines].reshape(-1, width).astype(F32)
    final_in = rms(outgoing).astype(BF16)
    stream_logits = jnp.dot(final_in, w_vocab, preferred_element_type=F32).astype(BF16)
    stream = lax.axis_index("guide")
    half_rows = stream_logits.shape[0] // 2
    kept = lax.dynamic_slice_in_dim(stream_logits, stream * half_rows, half_rows, 0)
    sent = lax.dynamic_slice_in_dim(stream_logits, (1 - stream) * half_rows, half_rows, 0)
    partner = lax.ppermute(sent, "guide", [(0, 1), (1, 0)])
    is_first = stream == 0
    cond = jnp.where(is_first, kept, partner).astype(F32)
    uncond = jnp.where(is_first, partner, kept).astype(F32)
    group_count = weight_index.shape[0]
    level_count = guidance_levels.shape[0]
    in_group = (group_ids[:, None] == jnp.arange(group_count)[None, :]).astype(F32)
    level_pick = (weight_index[:, None] == jnp.arange(level_count)[None, :]).astype(F32)
    group_weight = jnp.sum(level_pick * guidance_levels[None, :], axis=1)
    request_weight = jnp.sum(in_group * group_weight[None, :], axis=1)
    weight_rows = lax.dynamic_slice_in_dim(request_weight, stream * half_rows, half_rows, 0)
    logits = uncond + weight_rows[:, None] * (cond - uncond)
    return (logits, fresh[0][None], fresh[1][None])


def gathered_rows(w_out):
    rows, width = w_out.shape
    size = lax.axis_size("z") * width * 2
    want = -(-(2**20) // size)
    want += -want % 4
    padded = jnp.concatenate([w_out, w_out[: want - rows]], axis=0)
    gathered = lax.all_gather(padded, "z", axis=0, tiled=False)
    return gathered[:, :rows].reshape(-1, width)


def solution(mesh):
    guide, blk, batch = (mesh.shape[a] for a in ("guide", "blk", "batch"))
    ny = KV_HEADS
    mesh = Mesh(mesh.devices.reshape(guide, ny, blk // ny, batch), ("guide",) + BLK + ("batch",))
    placed = (
        P("guide", "batch", None),
        P(BLK, None),
        P("guide", "batch", BLK, None),
        P("guide", "batch", BLK, None),
        P("guide", "batch"),
        P(BLK, None),
        P(),
        P("guide", "batch", None),
        P(None, BLK),
        P(None, BLK),
        P(BLK, None),
        P(None, BLK + ("batch",)),
        P(),
        P(),
        P(),
    )
    return jax.shard_map(
        local,
        mesh=mesh,
        in_specs=placed,
        out_specs=(
            P("guide", BLK + ("batch",)),
            P("guide", "batch", None),
            P("guide", "batch", None),
        ),
        check_vma=False,
    )
```

```python
import jax
import jax.numpy as jnp
from jax import lax
from jax.sharding import Mesh, PartitionSpec as P

HEADS = 24
KV_HEADS = 8
HEAD_DIM = 64
EXPERTS = 16
EXPERT_UNITS = 1024
EPS = 1e-05
F32 = jnp.float32
BF16 = jnp.bfloat16
BLK = ("y", "z")


def rms(values):
    return values * lax.rsqrt(jnp.mean(values * values, axis=-1, keepdims=True) + EPS)


def exchange(value, axes):
    return lax.all_to_all(value, axes, 0, 0, tiled=True)


def halves(value):
    high = lax.reduce_precision(value, 8, 7)
    return high.astype(BF16), (value - high).astype(BF16)


def local(
    hidden,
    w_qkv,
    key_cache,
    value_cache,
    lengths,
    w_out,
    router,
    routes,
    w_gate,
    w_up,
    w_down,
    w_vocab,
    group_ids,
    weight_index,
    guidance_levels,
):
    group = HEADS // KV_HEADS
    y, z = lax.axis_index("y"), lax.axis_index("z")
    ny, nz = lax.axis_size("y"), lax.axis_size("z")
    blocks = ny * nz
    block = y * nz + z
    count = hidden.shape[1]
    pair = count // nz
    width = hidden.shape[2]
    width_q = HEADS * HEAD_DIM
    width_k = KV_HEADS * HEAD_DIM
    x = hidden[0].astype(F32)
    normed = rms(x).astype(BF16)
    rows = w_qkv.shape[0]
    part = lax.dynamic_slice_in_dim(normed, block * rows, rows, 1)
    qkv = jnp.dot(part, w_qkv, preferred_element_type=F32)
    q = qkv[:, :width_q].reshape(pair, nz, KV_HEADS, group * HEAD_DIM)
    k = qkv[:, width_q : width_q + width_k].reshape(pair, nz, KV_HEADS, HEAD_DIM)
    v = qkv[:, width_q + width_k :].reshape(pair, nz, KV_HEADS, HEAD_DIM)
    lines = jnp.concatenate([q, k, v], axis=3).transpose(2, 1, 0, 3)
    n_l = pair * (group + 2) * HEAD_DIM // 128
    high, low = halves(lines.reshape(blocks, n_l, 128))
    span = key_cache.shape[2]
    kc = key_cache[0].reshape(pair, nz, span, KV_HEADS, HEAD_DIM)
    vc = value_cache[0].reshape(pair, nz, span, KV_HEADS, HEAD_DIM)
    kv = jnp.concatenate([kc, vc], axis=4).transpose(3, 1, 0, 2, 4)
    kv = kv.reshape(blocks, pair * span, 2 * HEAD_DIM)
    cols = width // blocks
    w_rows = w_out.shape[0]
    n_w = -(-w_rows * cols // 128)
    w_blocks = w_out.reshape(w_rows, blocks, cols).transpose(1, 0, 2).reshape(blocks, w_rows * cols)
    w_blocks = jnp.pad(w_blocks, ((0, 0), (0, n_w * 128 - w_rows * cols))).reshape(blocks, n_w, 128)
    got = exchange(jnp.concatenate([kv, high, low, w_blocks], axis=1), BLK)

    n_kv = pair * span
    w_cols = got[:, n_kv + 2 * n_l :].reshape(blocks, n_w * 128)[:, : w_rows * cols].reshape(-1, cols)
    kv = got[:, :n_kv].reshape(blocks, pair, span, 2 * HEAD_DIM).transpose(1, 0, 2, 3)
    kv = kv.reshape(pair, blocks * span, 2 * HEAD_DIM)
    sums = jnp.sum(
        got[:, n_kv : n_kv + n_l].astype(F32) + got[:, n_kv + n_l : n_kv + 2 * n_l].astype(F32), axis=0
    )
    sums = sums.reshape(pair, group + 2, HEAD_DIM).astype(BF16)
    query, new_k, new_v = sums[:, :group], sums[:, group], sums[:, group + 1]
    scale = HEAD_DIM ** (-0.5)
    scores = jnp.einsum("ihd,ipd->ihp", query, kv[:, :, :HEAD_DIM], preferred_element_type=F32) * scale
    own = jnp.sum(query.astype(F32) * new_k.astype(F32)[:, None, :], axis=-1) * scale
    lens = lax.dynamic_index_in_dim(lengths[0].reshape(pair, nz), z, 1, False)
    valid = (jnp.arange(blocks * span)[None, :] < lens[:, None])[:, None, :]
    top = jnp.maximum(jnp.max(jnp.where(valid, scores, -1e30), axis=-1), own)
    probs = jnp.exp(jnp.where(valid, scores - top[..., None], -1e30))
    own_prob = jnp.exp(own - top)
    total = jnp.sum(probs, axis=-1) + own_prob
    acc = jnp.einsum("ihp,ipd->ihd", probs.astype(BF16), kv[:, :, HEAD_DIM:], preferred_element_type=F32)
    own_r = lax.reduce_precision(own_prob, 8, 7)
    acc = acc + own_r[..., None] * new_v.astype(F32)[:, None, :]
    attn = (acc / total[..., None]).astype(BF16)
    attn = jnp.concatenate([attn, sums[:, group:]], axis=1).reshape(n_l, 128)
    got = exchange(to_all(attn, blocks), BLK)

    got = got[:, :n_l].reshape(ny, nz, pair, (group + 2), HEAD_DIM).transpose(2, 1, 0, 3, 4)
    got = got.reshape(count, KV_HEADS, group + 2, HEAD_DIM)
    attn = got[:, :, :group].reshape(count, width_q)
    fresh_k = got[:, :, group].reshape(count, width_k)
    fresh_v = got[:, :, group + 1].reshape(count, width_k)
    part = jnp.dot(attn, w_cols, preferred_element_type=F32)
    own_lines = count * cols // 128
    high, low = halves(part.reshape(own_lines, 128))
    got = exchange(to_all(jnp.concatenate([high, low], axis=0), blocks), BLK)
    part = got[:, :own_lines].astype(F32) + got[:, own_lines : 2 * own_lines].astype(F32)
    part = part.reshape(blocks, count, cols).transpose(1, 0, 2).reshape(count, width)

    mixed = x + part
    expert_in = rms(mixed).astype(BF16)
    choice_logits = jnp.dot(expert_in, router, preferred_element_type=F32)
    picks = (routes[0][:, :, None] == jnp.arange(EXPERTS)[None, None, :]).astype(F32)
    chosen = jnp.sum(picks * choice_logits[:, None, :], axis=-1)
    first = jax.nn.sigmoid(chosen[:, 0] - chosen[:, 1])
    shares = jnp.stack([first, 1.0 - first], axis=1)
    per_expert = jnp.sum(picks * shares[:, :, None], axis=1)
    units = w_gate.shape[1]
    owner = (block * units + jnp.arange(units)) // EXPERT_UNITS
    member = (owner[None, :] == jnp.arange(EXPERTS)[:, None]).astype(F32)
    unit_weight = jnp.sum(per_expert[:, :, None] * member[None, :, :], axis=1)
    gate = jnp.dot(expert_in, w_gate, preferred_element_type=F32)
    upper = jnp.dot(expert_in, w_up, preferred_element_type=F32)
    act = (jax.nn.silu(gate) * upper * unit_weight).astype(BF16)
    expert_out = jnp.dot(act, w_down, preferred_element_type=F32)
    high, low = halves(expert_out.reshape(blocks, own_lines, 128))
    got = exchange(jnp.concatenate([high, low], axis=1), BLK)

    piece = jnp.sum(got[:, :own_lines].astype(F32) + got[:, own_lines : 2 * own_lines].astype(F32), axis=0)
    mixed_piece = lax.dynamic_index_in_dim(mixed.reshape(blocks, own_lines, 128), block, 0, False)
    piece = (mixed_piece + piece).astype(BF16)
    piece = jnp.concatenate([piece, jnp.zeros((1, 128), BF16)], axis=0)
    everyone = blocks * lax.axis_size("batch")
    got = exchange(jnp.broadcast_to(piece[None], (everyone,) + piece.shape), ("batch",) + BLK)
    outgoing = got[:, :own_lines].reshape(-1, width).astype(F32)
    final_in = rms(outgoing).astype(BF16)
    stream_logits = jnp.dot(final_in, w_vocab, preferred_element_type=F32).astype(BF16)
    stream = lax.axis_index("guide")
    half_rows = stream_logits.shape[0] // 2
    both = lax.all_gather(stream_logits, "guide", axis=0, tiled=False)
    both = lax.dynamic_slice_in_dim(both, stream * half_rows, half_rows, 1).astype(F32)
    cond, uncond = both[0], both[1]
    group_count = weight_index.shape[0]
    level_count = guidance_levels.shape[0]
    in_group = (group_ids[:, None] == jnp.arange(group_count)[None, :]).astype(F32)
    level_pick = (weight_index[:, None] == jnp.arange(level_count)[None, :]).astype(F32)
    group_weight = jnp.sum(level_pick * guidance_levels[None, :], axis=1)
    request_weight = jnp.sum(in_group * group_weight[None, :], axis=1)
    weight_rows = lax.dynamic_slice_in_dim(request_weight, stream * half_rows, half_rows, 0)
    logits = uncond + weight_rows[:, None] * (cond - uncond)
    return (logits, fresh_k[None], fresh_v[None])


def to_all(lines, number):
    fill = -lines.shape[0] % 8
    lines = jnp.concatenate([lines, jnp.zeros((fill, lines.shape[1]), lines.dtype)], axis=0)
    return jnp.broadcast_to(lines[None], (number,) + lines.shape)


def solution(mesh):
    guide, blk, batch = (mesh.shape[a] for a in ("guide", "blk", "batch"))
    ny = KV_HEADS
    mesh = Mesh(mesh.devices.reshape(guide, ny, blk // ny, batch), ("guide",) + BLK + ("batch",))
    placed = (
        P("guide", "batch", None),
        P(BLK, None),
        P("guide", "batch", BLK, None),
        P("guide", "batch", BLK, None),
        P("guide", "batch"),
        P(BLK, None),
        P(),
        P("guide", "batch", None),
        P(None, BLK),
        P(None, BLK),
        P(BLK, None),
        P(None, BLK + ("batch",)),
        P(),
        P(),
        P(),
    )
    return jax.shard_map(
        local,
        mesh=mesh,
        in_specs=placed,
        out_specs=(
            P("guide", BLK + ("batch",)),
            P("guide", "batch", None),
            P("guide", "batch", None),
        ),
        check_vma=False,
    )
```

```python
import jax
import jax.numpy as jnp
from jax import lax
from jax.experimental import pallas as pl
from jax.experimental.pallas import tpu as pltpu
from jax.sharding import Mesh, PartitionSpec as P

HEADS = 24
KV_HEADS = 8
HEAD_DIM = 64
EXPERTS = 16
EXPERT_UNITS = 1024
EPS = 1e-05
F32 = jnp.float32
BF16 = jnp.bfloat16
BLK = ("y", "z")


def rms(values):
    return values * lax.rsqrt(jnp.mean(values * values, axis=-1, keepdims=True) + EPS)


def exchange(value, axes):
    return lax.all_to_all(value, axes, 0, 0, tiled=True)


def halves(value):
    high = lax.reduce_precision(value, 8, 7)
    return high.astype(BF16), (value - high).astype(BF16)


def local(
    hidden,
    w_qkv,
    key_cache,
    value_cache,
    lengths,
    w_out,
    router,
    routes,
    w_gate,
    w_up,
    w_down,
    w_vocab,
    group_ids,
    weight_index,
    guidance_levels,
):
    group = HEADS // KV_HEADS
    y, z = lax.axis_index("y"), lax.axis_index("z")
    ny, nz = lax.axis_size("y"), lax.axis_size("z")
    blocks = ny * nz
    block = y * nz + z
    count = hidden.shape[1]
    pair = count // nz
    width = hidden.shape[2]
    width_q = HEADS * HEAD_DIM
    width_k = KV_HEADS * HEAD_DIM
    x = hidden[0].astype(F32)
    span = key_cache.shape[2]
    sent = first_payload(block, hidden[0], w_qkv, key_cache[0], value_cache[0], blocks)
    got = exchange(sent, BLK)
    cols = width // blocks
    w_rows = w_out.shape[0]
    n_w = -(-w_rows * cols // 128)
    w_blocks = w_out.reshape(w_rows, blocks, cols).transpose(1, 0, 2).reshape(blocks, w_rows * cols)
    w_blocks = jnp.pad(w_blocks, ((0, 0), (0, n_w * 128 - w_rows * cols))).reshape(blocks, n_w, 128)

    n_kv = pair * span
    kv = got[:, :n_kv].reshape(blocks, pair, span, 2 * HEAD_DIM).transpose(1, 0, 2, 3)
    kv = kv.reshape(pair, blocks * span, 2 * HEAD_DIM)
    sums = jnp.sum(got[:, n_kv:].astype(F32), axis=0)
    query = (sums[:group] + sums[group + 2 :]).reshape(group, pair, HEAD_DIM).transpose(1, 0, 2).astype(BF16)
    fresh = sums[group : group + 2].astype(BF16)
    new_k, new_v = fresh[0].reshape(pair, HEAD_DIM), fresh[1].reshape(pair, HEAD_DIM)
    scale = HEAD_DIM ** (-0.5)
    scores = jnp.einsum("ihd,ipd->ihp", query, kv[:, :, :HEAD_DIM], preferred_element_type=F32) * scale
    own = jnp.sum(query.astype(F32) * new_k.astype(F32)[:, None, :], axis=-1) * scale
    lens = lax.dynamic_index_in_dim(lengths[0].reshape(pair, nz), z, 1, False)
    valid = (jnp.arange(blocks * span)[None, :] < lens[:, None])[:, None, :]
    top = jnp.maximum(jnp.max(jnp.where(valid, scores, -1e30), axis=-1), own)
    probs = jnp.exp(jnp.where(valid, scores - top[..., None], -1e30))
    own_prob = jnp.exp(own - top)
    total = jnp.sum(probs, axis=-1) + own_prob
    acc = jnp.einsum("ihp,ipd->ihd", probs.astype(BF16), kv[:, :, HEAD_DIM:], preferred_element_type=F32)
    own_r = lax.reduce_precision(own_prob, 8, 7)
    acc = acc + own_r[..., None] * new_v.astype(F32)[:, None, :]
    attn = (acc / total[..., None]).astype(BF16)
    n_a = pair * group * HEAD_DIM // 128
    attn = jnp.broadcast_to(attn.reshape(1, n_a, 128), (blocks, n_a, 128))
    got = exchange(jnp.concatenate([attn, w_blocks], axis=1), BLK)

    w_cols = got[:, n_a:].reshape(blocks, n_w * 128)[:, : w_rows * cols].reshape(-1, cols)
    attn = got[:, :n_a].reshape(ny, nz, pair, group * HEAD_DIM).transpose(2, 1, 0, 3).reshape(count, width_q)
    part = jnp.dot(attn, w_cols, preferred_element_type=F32)
    own_lines = count * cols // 128
    high, low = halves(part.reshape(own_lines, 128))
    got = exchange(to_all(jnp.concatenate([high, low, fresh], axis=0), blocks), BLK)
    part = got[:, :own_lines].astype(F32) + got[:, own_lines : 2 * own_lines].astype(F32)
    part = part.reshape(blocks, count, cols).transpose(1, 0, 2).reshape(count, width)

    fresh = got[:, 2 * own_lines :].reshape(ny, nz, 2, pair, HEAD_DIM).transpose(2, 3, 1, 0, 4)
    fresh = fresh.reshape(2, 1, count, width_k)

    mixed = x + part
    expert_in = rms(mixed).astype(BF16)
    choice_logits = jnp.dot(expert_in, router, preferred_element_type=F32)
    picks = (routes[0][:, :, None] == jnp.arange(EXPERTS)[None, None, :]).astype(F32)
    chosen = jnp.sum(picks * choice_logits[:, None, :], axis=-1)
    first = jax.nn.sigmoid(chosen[:, 0] - chosen[:, 1])
    shares = jnp.stack([first, 1.0 - first], axis=1)
    per_expert = jnp.sum(picks * shares[:, :, None], axis=1)
    units = w_gate.shape[1]
    owner = (block * units + jnp.arange(units)) // EXPERT_UNITS
    member = (owner[None, :] == jnp.arange(EXPERTS)[:, None]).astype(F32)
    unit_weight = jnp.sum(per_expert[:, :, None] * member[None, :, :], axis=1)
    gate = jnp.dot(expert_in, w_gate, preferred_element_type=F32)
    upper = jnp.dot(expert_in, w_up, preferred_element_type=F32)
    act = (jax.nn.silu(gate) * upper * unit_weight).astype(BF16)
    expert_out = jnp.dot(act, w_down, preferred_element_type=F32)
    high, low = halves(expert_out.reshape(blocks, own_lines, 128))
    got = exchange(jnp.concatenate([high, low], axis=1), BLK)

    piece = jnp.sum(got[:, :own_lines].astype(F32) + got[:, own_lines : 2 * own_lines].astype(F32), axis=0)
    mixed_piece = lax.dynamic_index_in_dim(mixed.reshape(blocks, own_lines, 128), block, 0, False)
    piece = (mixed_piece + piece).astype(BF16)
    piece = jnp.concatenate([piece, jnp.zeros((1, 128), BF16)], axis=0)
    everyone = blocks * lax.axis_size("batch")
    got = exchange(jnp.broadcast_to(piece[None], (everyone,) + piece.shape), ("batch",) + BLK)
    outgoing = got[:, :own_lines].reshape(-1, width).astype(F32)
    final_in = rms(outgoing).astype(BF16)
    stream_logits = jnp.dot(final_in, w_vocab, preferred_element_type=F32).astype(BF16)
    stream = lax.axis_index("guide")
    half_rows = stream_logits.shape[0] // 2
    both = lax.all_gather(stream_logits, "guide", axis=0, tiled=False)
    both = lax.dynamic_slice_in_dim(both, stream * half_rows, half_rows, 1).astype(F32)
    cond, uncond = both[0], both[1]
    group_count = weight_index.shape[0]
    level_count = guidance_levels.shape[0]
    in_group = (group_ids[:, None] == jnp.arange(group_count)[None, :]).astype(F32)
    level_pick = (weight_index[:, None] == jnp.arange(level_count)[None, :]).astype(F32)
    group_weight = jnp.sum(level_pick * guidance_levels[None, :], axis=1)
    request_weight = jnp.sum(in_group * group_weight[None, :], axis=1)
    weight_rows = lax.dynamic_slice_in_dim(request_weight, stream * half_rows, half_rows, 0)
    logits = uncond + weight_rows[:, None] * (cond - uncond)
    return (logits, fresh[0], fresh[1])


def to_all(lines, number):
    fill = -lines.shape[0] % 8
    lines = jnp.concatenate([lines, jnp.zeros((fill, lines.shape[1]), lines.dtype)], axis=0)
    return jnp.broadcast_to(lines[None], (number,) + lines.shape)


def first_payload_kernel(block_ref, hidden_ref, w_ref, key_ref, value_ref, out_ref, lines):
    count, width = hidden_ref.shape
    rows, total = w_ref.shape
    span, width_k = key_ref.shape[1:]
    nz = 8
    normed = rms(hidden_ref[...].astype(F32)).astype(BF16)
    at = lax.broadcasted_iota(jnp.int32, (width, 128), 0) - block_ref[0] * rows
    pick = jnp.where(at == lax.broadcasted_iota(jnp.int32, (width, 128), 1), 1.0, 0.0)
    part = jnp.dot(normed, pick.astype(BF16), preferred_element_type=F32)[:, :rows].astype(BF16)
    qkv = jnp.dot(part, w_ref[...], preferred_element_type=F32)
    low_lane = lax.broadcasted_iota(jnp.int32, (nz, 128), 1) < 64
    heads = (total - 2 * width_k) // 64
    for v in range(total // 128):
        first, second = qkv[:nz, 128 * v : 128 * v + 128], qkv[nz:, 128 * v : 128 * v + 128]
        even = jnp.where(low_lane, first, pltpu.roll(second, 64, 1))
        odd = jnp.where(low_lane, pltpu.roll(first, 64, 1), second)
        for chunk, line in ((2 * v, even), (2 * v + 1, odd)):
            if chunk < heads:
                y, row = chunk // 3, chunk % 3
                high = line.astype(BF16).astype(F32)
                lines[nz * y : nz * y + nz, 5 + row, :] = line - high
            else:
                y, row = (chunk - heads) % 8, 3 + (chunk - heads) // 8
                high = line
            lines[nz * y : nz * y + nz, row, :] = high
    out_ref[:, 2 * span :, :] = lines[...].astype(BF16)
    low_lane = lax.broadcasted_iota(jnp.int32, (count, span, 128), 2) < 64
    for m in range(width_k // 128):
        keys = key_ref[:, :, 128 * m : 128 * m + 128].astype(F32)
        values = value_ref[:, :, 128 * m : 128 * m + 128].astype(F32)
        even = jnp.where(low_lane, keys, pltpu.roll(values, 64, 2)).astype(BF16)
        odd = jnp.where(low_lane, pltpu.roll(keys, 64, 2), values).astype(BF16)
        for y, pair in ((2 * m, even), (2 * m + 1, odd)):
            for i in range(count // nz):
                out_ref[nz * y : nz * y + nz, span * i : span * i + span, :] = pair[nz * i : nz * i + nz]

def first_payload(block, hidden, w_qkv, keys, values, blocks):
    span = keys.shape[1]
    vmem = pl.BlockSpec(memory_space=pltpu.VMEM)
    return pl.pallas_call(
        first_payload_kernel,
        out_shape=jax.ShapeDtypeStruct((blocks, 2 * span + 8, 128), BF16),
        in_specs=[pl.BlockSpec(memory_space=pltpu.SMEM)] + [vmem] * 4,
        out_specs=vmem,
        scratch_shapes=[pltpu.VMEM((blocks, 8, 128), F32)],
        compiler_params=pltpu.CompilerParams(vmem_limit_bytes=32 << 20),
    )(block.reshape(1), hidden, w_qkv, keys, values)


def solution(mesh):
    guide, blk, batch = (mesh.shape[a] for a in ("guide", "blk", "batch"))
    ny = KV_HEADS
    mesh = Mesh(mesh.devices.reshape(guide, ny, blk // ny, batch), ("guide",) + BLK + ("batch",))
    placed = (
        P("guide", "batch", None),
        P(BLK, None),
        P("guide", "batch", BLK, None),
        P("guide", "batch", BLK, None),
        P("guide", "batch"),
        P(BLK, None),
        P(),
        P("guide", "batch", None),
        P(None, BLK),
        P(None, BLK),
        P(BLK, None),
        P(None, BLK + ("batch",)),
        P(),
        P(),
        P(),
    )
    return jax.shard_map(
        local,
        mesh=mesh,
        in_specs=placed,
        out_specs=(
            P("guide", BLK + ("batch",)),
            P("guide", "batch", None),
            P("guide", "batch", None),
        ),
        check_vma=False,
    )
```

```python
import jax
import jax.numpy as jnp
from jax import lax
from jax.experimental import pallas as pl
from jax.experimental.pallas import tpu as pltpu
from jax.sharding import Mesh, PartitionSpec as P

HEADS = 24
KV_HEADS = 8
HEAD_DIM = 64
EXPERTS = 16
EXPERT_UNITS = 1024
EPS = 1e-05
F32 = jnp.float32
BF16 = jnp.bfloat16
BLK = ("y", "z")
HBM = pl.BlockSpec(memory_space=pltpu.HBM)
VMEM = pl.BlockSpec(memory_space=pltpu.VMEM)
SMEM = pl.BlockSpec(memory_space=pltpu.SMEM)


def rms(values):
    return values * lax.rsqrt(jnp.mean(values * values, axis=-1, keepdims=True) + EPS)


def exchange(value, axes):
    return lax.all_to_all(value, axes, 0, 0, tiled=True)


def halves(value):
    high = lax.reduce_precision(value, 8, 7)
    return high.astype(BF16), (value - high).astype(BF16)


def local(
    hidden,
    w_qkv,
    key_cache,
    value_cache,
    lengths,
    w_out,
    router,
    routes,
    w_gate,
    w_up,
    w_down,
    w_vocab,
    group_ids,
    weight_index,
    guidance_levels,
):
    group = HEADS // KV_HEADS
    y, z = lax.axis_index("y"), lax.axis_index("z")
    ny, nz = lax.axis_size("y"), lax.axis_size("z")
    blocks = ny * nz
    block = y * nz + z
    count = hidden.shape[1]
    pair = count // nz
    width = hidden.shape[2]
    width_q = HEADS * HEAD_DIM
    width_k = KV_HEADS * HEAD_DIM
    span = key_cache.shape[2]
    sent = first_payload(block, hidden[0], w_qkv, key_cache[0], value_cache[0], blocks)
    got = exchange(sent, BLK)
    cols = width // blocks
    w_rows = w_out.shape[0]
    n_w = -(-w_rows * cols // 128)
    w_blocks = w_out.reshape(w_rows, blocks, cols).transpose(1, 0, 2).reshape(blocks, w_rows * cols)
    w_blocks = jnp.pad(w_blocks, ((0, 0), (0, n_w * 128 - w_rows * cols))).reshape(blocks, n_w, 128)

    n_kv = pair * span
    kv = got[:, :n_kv].reshape(blocks, pair, span, 2 * HEAD_DIM).transpose(1, 0, 2, 3)
    kv = kv.reshape(pair, blocks * span, 2 * HEAD_DIM)
    sums = jnp.sum(got[:, n_kv:].astype(F32), axis=0)
    query = (sums[:group] + sums[group + 2 :]).reshape(group, pair, HEAD_DIM).transpose(1, 0, 2).astype(BF16)
    fresh = sums[group : group + 2].astype(BF16)
    new_k, new_v = fresh[0].reshape(pair, HEAD_DIM), fresh[1].reshape(pair, HEAD_DIM)
    scale = HEAD_DIM ** (-0.5)
    scores = jnp.einsum("ihd,ipd->ihp", query, kv[:, :, :HEAD_DIM], preferred_element_type=F32) * scale
    own = jnp.sum(query.astype(F32) * new_k.astype(F32)[:, None, :], axis=-1) * scale
    lens = lax.dynamic_index_in_dim(lengths[0].reshape(pair, nz), z, 1, False)
    valid = (jnp.arange(blocks * span)[None, :] < lens[:, None])[:, None, :]
    top = jnp.maximum(jnp.max(jnp.where(valid, scores, -1e30), axis=-1), own)
    probs = jnp.exp(jnp.where(valid, scores - top[..., None], -1e30))
    own_prob = jnp.exp(own - top)
    total = jnp.sum(probs, axis=-1) + own_prob
    acc = jnp.einsum("ihp,ipd->ihd", probs.astype(BF16), kv[:, :, HEAD_DIM:], preferred_element_type=F32)
    own_r = lax.reduce_precision(own_prob, 8, 7)
    acc = acc + own_r[..., None] * new_v.astype(F32)[:, None, :]
    attn = (acc / total[..., None]).astype(BF16)
    n_a = pair * group * HEAD_DIM // 128
    attn = jnp.broadcast_to(attn.reshape(1, n_a, 128), (blocks, n_a, 128))
    got = exchange(jnp.concatenate([attn, w_blocks], axis=1), BLK)

    w_cols = got[:, n_a:].reshape(blocks, n_w * 128)[:, : w_rows * cols].reshape(-1, cols)
    attn = got[:, :n_a].reshape(ny, nz, pair, group * HEAD_DIM).transpose(2, 1, 0, 3).reshape(count, width_q)
    part = jnp.dot(attn, w_cols, preferred_element_type=F32)
    own_lines = count * cols // 128
    high, low = halves(part.reshape(own_lines, 128))
    got = exchange(to_all(jnp.concatenate([high, low, fresh], axis=0), blocks), BLK)
    part = got[:, :own_lines].astype(F32) + got[:, own_lines : 2 * own_lines].astype(F32)
    part = part.reshape(blocks, count, cols).transpose(1, 0, 2).reshape(count, width)

    fresh = got[:, 2 * own_lines :].reshape(ny, nz, 2, pair, HEAD_DIM).transpose(2, 3, 1, 0, 4)
    fresh = fresh.reshape(2, 1, count, width_k)

    sent, mixed = expert_payload(block, hidden[0], part, router, routes[0], w_gate, w_up, w_down)
    got = exchange(sent.reshape(blocks, 2 * own_lines, 128), BLK)

    piece = jnp.sum(got[:, :own_lines].astype(F32) + got[:, own_lines : 2 * own_lines].astype(F32), axis=0)
    mixed_piece = lax.dynamic_index_in_dim(mixed.reshape(blocks, own_lines, 128), block, 0, False)
    piece = (mixed_piece + piece).astype(BF16)
    piece = jnp.concatenate([piece, jnp.zeros((1, 128), BF16)], axis=0)
    everyone = blocks * lax.axis_size("batch")
    got = exchange(jnp.broadcast_to(piece[None], (everyone,) + piece.shape), ("batch",) + BLK)
    outgoing = lax.optimization_barrier(got[:, :own_lines].astype(F32).reshape(-1, width))
    final_in = rms(outgoing).astype(BF16)
    stream_logits = jnp.dot(final_in, w_vocab, preferred_element_type=F32).astype(BF16)
    stream = lax.axis_index("guide")
    half_rows = stream_logits.shape[0] // 2
    both = lax.all_gather(stream_logits, "guide", axis=0, tiled=False)
    both = lax.dynamic_slice_in_dim(both, stream * half_rows, half_rows, 1).astype(F32)
    cond, uncond = both[0], both[1]
    group_count = weight_index.shape[0]
    level_count = guidance_levels.shape[0]
    in_group = (group_ids[:, None] == jnp.arange(group_count)[None, :]).astype(F32)
    level_pick = (weight_index[:, None] == jnp.arange(level_count)[None, :]).astype(F32)
    group_weight = jnp.sum(level_pick * guidance_levels[None, :], axis=1)
    request_weight = jnp.sum(in_group * group_weight[None, :], axis=1)
    weight_rows = lax.dynamic_slice_in_dim(request_weight, stream * half_rows, half_rows, 0)
    logits = uncond + weight_rows[:, None] * (cond - uncond)
    return (logits, fresh[0], fresh[1])


def to_all(lines, number):
    fill = -lines.shape[0] % 8
    lines = jnp.concatenate([lines, jnp.zeros((fill, lines.shape[1]), lines.dtype)], axis=0)
    return jnp.broadcast_to(lines[None], (number,) + lines.shape)


def first_payload_kernel(
    block_ref, hidden_hbm, w_hbm, key_hbm, value_hbm, out_ref, hidden_ref, w_ref, key_ref, value_ref, lines, sems
):
    copies = [
        pltpu.make_async_copy(source, target, sems.at[n])
        for n, (source, target) in enumerate(
            ((hidden_hbm, hidden_ref), (w_hbm, w_ref), (key_hbm, key_ref), (value_hbm, value_ref))
        )
    ]
    for copy in copies:
        copy.start()
    count, width = hidden_ref.shape
    rows, total = w_ref.shape
    span, width_k = key_ref.shape[1:]
    nz = count // 2
    at = lax.broadcasted_iota(jnp.int32, (width, 128), 0) - block_ref[0] * rows
    pick = jnp.where(at == lax.broadcasted_iota(jnp.int32, (width, 128), 1), 1.0, 0.0).astype(BF16)
    copies[0].wait()
    normed = rms(hidden_ref[...].astype(F32)).astype(BF16)
    part = jnp.dot(normed, pick, preferred_element_type=F32)[:, :rows].astype(BF16)
    copies[1].wait()
    qkv = jnp.dot(part, w_ref[...], preferred_element_type=F32)
    low_lane = lax.broadcasted_iota(jnp.int32, (nz, 128), 1) < 64
    heads = (total - 2 * width_k) // 64
    for v in range(total // 128):
        first, second = qkv[:nz, 128 * v : 128 * v + 128], qkv[nz:, 128 * v : 128 * v + 128]
        even = jnp.where(low_lane, first, pltpu.roll(second, 64, 1))
        odd = jnp.where(low_lane, pltpu.roll(first, 64, 1), second)
        for chunk, line in ((2 * v, even), (2 * v + 1, odd)):
            if chunk < heads:
                y, row = chunk // 3, chunk % 3
                high = line.astype(BF16).astype(F32)
                lines[nz * y : nz * y + nz, 5 + row, :] = line - high
            else:
                y, row = (chunk - heads) % 8, 3 + (chunk - heads) // 8
                high = line
            lines[nz * y : nz * y + nz, row, :] = high
    out_ref[:, 2 * span :, :] = lines[...].astype(BF16)
    copies[2].wait()
    copies[3].wait()
    low_lane = lax.broadcasted_iota(jnp.int32, (count, span, 128), 2) < 64
    for m in range(width_k // 128):
        keys = key_ref[:, :, 128 * m : 128 * m + 128].astype(F32)
        values = value_ref[:, :, 128 * m : 128 * m + 128].astype(F32)
        even = jnp.where(low_lane, keys, pltpu.roll(values, 64, 2)).astype(BF16)
        odd = jnp.where(low_lane, pltpu.roll(keys, 64, 2), values).astype(BF16)
        for y, pair in ((2 * m, even), (2 * m + 1, odd)):
            for i in range(count // nz):
                out_ref[nz * y : nz * y + nz, span * i : span * i + span, :] = pair[nz * i : nz * i + nz]


def first_payload(block, hidden, w_qkv, keys, values, blocks):
    span = keys.shape[1]
    return pl.pallas_call(
        first_payload_kernel,
        out_shape=jax.ShapeDtypeStruct((blocks, 2 * span + 8, 128), BF16),
        in_specs=[SMEM] + [HBM] * 4,
        out_specs=VMEM,
        scratch_shapes=[pltpu.VMEM(a.shape, a.dtype) for a in (hidden, w_qkv, keys, values)]
        + [pltpu.VMEM((blocks, 8, 128), F32), pltpu.SemaphoreType.DMA((4,))],
        compiler_params=pltpu.CompilerParams(vmem_limit_bytes=60 << 20),
    )(block.reshape(1), hidden, w_qkv, keys, values)


def expert_kernel(
    block_ref,
    hidden_ref,
    part_ref,
    router_ref,
    routes_ref,
    gate_hbm,
    up_hbm,
    down_hbm,
    out_ref,
    mixed_ref,
    gate_ref,
    up_ref,
    down_ref,
    lines,
    sems,
):
    copies = [
        pltpu.make_async_copy(source, target, sems.at[n])
        for n, (source, target) in enumerate(((gate_hbm, gate_ref), (up_hbm, up_ref), (down_hbm, down_ref)))
    ]
    for copy in copies:
        copy.start()
    count, width = hidden_ref.shape
    mixed = hidden_ref[...].astype(F32) + part_ref[...]
    expert_in = rms(mixed).astype(BF16)
    choice = lax.dot_general(
        router_ref[...], expert_in, (((1,), (1,)), ((), ())), preferred_element_type=F32
    )
    experts = lax.broadcasted_iota(jnp.int32, choice.shape, 0)
    routes = routes_ref[...]
    e1, e2 = routes[0:1], routes[1:2]
    zero = jnp.zeros_like(choice)
    c1 = jnp.sum(jnp.where(experts == e1, choice, zero), axis=0, keepdims=True)
    c2 = jnp.sum(jnp.where(experts == e2, choice, zero), axis=0, keepdims=True)
    first = 1.0 / (1.0 + jnp.exp(c2 - c1))
    mine = block_ref[0] * gate_ref.shape[1] // EXPERT_UNITS
    share = jnp.where(e1 == mine, first, jnp.where(e2 == mine, 1.0 - first, 0.0))
    row = lax.broadcasted_iota(jnp.int32, (count, count), 0)
    column = lax.broadcasted_iota(jnp.int32, (count, count), 1)
    share = jnp.sum(jnp.where(row == column, share, 0.0), axis=1, keepdims=True)
    copies[0].wait()
    gate = jnp.dot(expert_in, gate_ref[...], preferred_element_type=F32)
    copies[1].wait()
    upper = jnp.dot(expert_in, up_ref[...], preferred_element_type=F32)
    act = (gate / (1.0 + jnp.exp(-gate)) * upper * share).astype(BF16)
    copies[2].wait()
    out = jnp.dot(act, down_ref[...], preferred_element_type=F32)
    parts = width // 384
    for j in range(parts):
        for i in range(3):
            lanes = slice(128 * (3 * j + i), 128 * (3 * j + i) + 128)
            line = out[:, lanes]
            high = line.astype(BF16).astype(F32)
            lines[:, j, i, :] = high
            lines[:, j, 3 + i, :] = line - high
            mixed_ref[:, j, i, :] = mixed[:, lanes]
    out_ref[...] = lines[...].astype(BF16)


def expert_payload(block, hidden, part, router, routes, w_gate, w_up, w_down):
    count, width = hidden.shape
    parts = width // 384
    return pl.pallas_call(
        expert_kernel,
        out_shape=(
            jax.ShapeDtypeStruct((count, parts, 6, 128), BF16),
            jax.ShapeDtypeStruct((count, parts, 3, 128), F32),
        ),
        in_specs=[SMEM] + [VMEM] * 4 + [HBM] * 3,
        out_specs=(VMEM, VMEM),
        scratch_shapes=[pltpu.VMEM(a.shape, a.dtype) for a in (w_gate, w_up, w_down)]
        + [pltpu.VMEM((count, parts, 6, 128), F32), pltpu.SemaphoreType.DMA((3,))],
        compiler_params=pltpu.CompilerParams(vmem_limit_bytes=60 << 20),
    )(block.reshape(1), hidden, part, router.T, routes.T, w_gate, w_up, w_down)


def solution(mesh):
    guide, blk, batch = (mesh.shape[a] for a in ("guide", "blk", "batch"))
    ny = KV_HEADS
    mesh = Mesh(mesh.devices.reshape(guide, ny, blk // ny, batch), ("guide",) + BLK + ("batch",))
    placed = (
        P("guide", "batch", None),
        P(BLK, None),
        P("guide", "batch", BLK, None),
        P("guide", "batch", BLK, None),
        P("guide", "batch"),
        P(BLK, None),
        P(),
        P("guide", "batch", None),
        P(None, BLK),
        P(None, BLK),
        P(BLK, None),
        P(None, BLK + ("batch",)),
        P(),
        P(),
        P(),
    )
    return jax.shard_map(
        local,
        mesh=mesh,
        in_specs=placed,
        out_specs=(
            P("guide", BLK + ("batch",)),
            P("guide", "batch", None),
            P("guide", "batch", None),
        ),
        check_vma=False,
    )
```

```python
import jax
import jax.numpy as jnp
from jax import lax
from jax.experimental import pallas as pl
from jax.experimental.pallas import tpu as pltpu
from jax.sharding import Mesh, PartitionSpec as P

HEADS = 24
KV_HEADS = 8
HEAD_DIM = 64
EXPERTS = 16
EXPERT_UNITS = 1024
EPS = 1e-05
F32 = jnp.float32
BF16 = jnp.bfloat16
BLK = ("y", "z")
HBM = pl.BlockSpec(memory_space=pltpu.HBM)
VMEM = pl.BlockSpec(memory_space=pltpu.VMEM)
SMEM = pl.BlockSpec(memory_space=pltpu.SMEM)


def rms(values):
    return values * lax.rsqrt(jnp.mean(values * values, axis=-1, keepdims=True) + EPS)


def exchange(value, axes):
    return lax.all_to_all(value, axes, 0, 0, tiled=True)


def halves(value):
    high = lax.reduce_precision(value, 8, 7)
    return high.astype(BF16), (value - high).astype(BF16)


def local(
    hidden,
    w_qkv,
    key_cache,
    value_cache,
    lengths,
    w_out,
    router,
    routes,
    w_gate,
    w_up,
    w_down,
    w_vocab,
    group_ids,
    weight_index,
    guidance_levels,
):
    group = HEADS // KV_HEADS
    y, z = lax.axis_index("y"), lax.axis_index("z")
    ny, nz = lax.axis_size("y"), lax.axis_size("z")
    blocks = ny * nz
    block = y * nz + z
    count = hidden.shape[1]
    pair = count // nz
    width = hidden.shape[2]
    width_q = HEADS * HEAD_DIM
    width_k = KV_HEADS * HEAD_DIM
    span = key_cache.shape[2]
    sent = first_payload(block, hidden[0], w_qkv, key_cache[0], value_cache[0], blocks)
    got = exchange(sent, BLK)
    cols = width // blocks
    w_rows = w_out.shape[0]
    n_w = -(-w_rows * cols // 128)
    w_blocks = w_out.reshape(w_rows, blocks // count, cols // 8, count, 8).transpose(1, 3, 0, 2, 4)
    w_blocks = w_blocks.reshape(blocks, w_rows * cols)
    w_blocks = jnp.pad(w_blocks, ((0, 0), (0, n_w * 128 - w_rows * cols))).reshape(blocks, n_w, 128)

    n_kv = pair * span
    kv = got[:, :n_kv].reshape(blocks, pair, span, 2 * HEAD_DIM).transpose(1, 0, 2, 3)
    kv = kv.reshape(pair, blocks * span, 2 * HEAD_DIM)
    sums = jnp.sum(got[:, n_kv:].astype(F32), axis=0)
    query = (sums[:group] + sums[group + 2 :]).reshape(group, pair, HEAD_DIM).transpose(1, 0, 2).astype(BF16)
    fresh = sums[group : group + 2].astype(BF16)
    new_k, new_v = fresh[0].reshape(pair, HEAD_DIM), fresh[1].reshape(pair, HEAD_DIM)
    scale = HEAD_DIM ** (-0.5)
    scores = jnp.einsum("ihd,ipd->ihp", query, kv[:, :, :HEAD_DIM], preferred_element_type=F32) * scale
    own = jnp.sum(query.astype(F32) * new_k.astype(F32)[:, None, :], axis=-1) * scale
    lens = lax.dynamic_index_in_dim(lengths[0].reshape(pair, nz), z, 1, False)
    valid = (jnp.arange(blocks * span)[None, :] < lens[:, None])[:, None, :]
    top = jnp.maximum(jnp.max(jnp.where(valid, scores, -1e30), axis=-1), own)
    probs = jnp.exp(jnp.where(valid, scores - top[..., None], -1e30))
    own_prob = jnp.exp(own - top)
    total = jnp.sum(probs, axis=-1) + own_prob
    acc = jnp.einsum("ihp,ipd->ihd", probs.astype(BF16), kv[:, :, HEAD_DIM:], preferred_element_type=F32)
    own_r = lax.reduce_precision(own_prob, 8, 7)
    acc = acc + own_r[..., None] * new_v.astype(F32)[:, None, :]
    attn = (acc / total[..., None]).astype(BF16)
    n_a = pair * group * HEAD_DIM // 128
    attn = jnp.broadcast_to(attn.reshape(1, n_a, 128), (blocks, n_a, 128))
    got = exchange(jnp.concatenate([attn, w_blocks], axis=1), BLK)

    w_cols = got[:, n_a:].reshape(blocks, n_w * 128)[:, : w_rows * cols].reshape(-1, cols)
    attn = got[:, :n_a].reshape(ny, nz, pair, group * HEAD_DIM).transpose(2, 1, 0, 3).reshape(count, width_q)
    part = jnp.dot(attn, w_cols, preferred_element_type=F32)
    own_lines = count * cols // 128
    part = part.reshape(count, own_lines, 8).transpose(1, 0, 2)
    high, low = halves(part.reshape(own_lines, 128))
    got = exchange(to_all(jnp.concatenate([high, low, fresh], axis=0), blocks), BLK)
    fresh = got[:, 2 * own_lines :].reshape(ny, nz, 2, pair, HEAD_DIM).transpose(2, 3, 1, 0, 4)
    fresh = fresh.reshape(2, 1, count, width_k)

    expert = block * w_gate.shape[1] // EXPERT_UNITS
    expert_in, share, mixed = routed(expert, got, hidden[0], router.T, routes[0].T)
    sent = expert_payload(expert_in, share, w_gate, w_up, w_down)
    got = exchange(sent.reshape(blocks, 2 * own_lines, 128), BLK)

    piece = jnp.sum(got[:, :own_lines].astype(F32) + got[:, own_lines : 2 * own_lines].astype(F32), axis=0)
    mixed_piece = lax.dynamic_index_in_dim(mixed.reshape(blocks, own_lines, 128), block, 0, False)
    mixed_piece = lax.optimization_barrier(mixed_piece)
    piece = (mixed_piece + piece).astype(BF16)
    piece = jnp.concatenate([piece, jnp.zeros((1, 128), BF16)], axis=0)
    everyone = blocks * lax.axis_size("batch")
    got = exchange(jnp.broadcast_to(piece[None], (everyone,) + piece.shape), ("batch",) + BLK)
    outgoing = lax.optimization_barrier(got[:, :own_lines].astype(F32).reshape(-1, width))
    final_in = rms(outgoing).astype(BF16)
    stream_logits = jnp.dot(final_in, w_vocab, preferred_element_type=F32).astype(BF16)
    stream = lax.axis_index("guide")
    half_rows = stream_logits.shape[0] // 2
    both = lax.all_gather(stream_logits, "guide", axis=0, tiled=False)
    both = lax.dynamic_slice_in_dim(both, stream * half_rows, half_rows, 1).astype(F32)
    cond, uncond = both[0], both[1]
    group_count = weight_index.shape[0]
    level_count = guidance_levels.shape[0]
    in_group = (group_ids[:, None] == jnp.arange(group_count)[None, :]).astype(F32)
    level_pick = (weight_index[:, None] == jnp.arange(level_count)[None, :]).astype(F32)
    group_weight = jnp.sum(level_pick * guidance_levels[None, :], axis=1)
    request_weight = jnp.sum(in_group * group_weight[None, :], axis=1)
    weight_rows = lax.dynamic_slice_in_dim(request_weight, stream * half_rows, half_rows, 0)
    logits = uncond + weight_rows[:, None] * (cond - uncond)
    return (logits, fresh[0], fresh[1])


def to_all(lines, number):
    fill = -lines.shape[0] % 8
    lines = jnp.concatenate([lines, jnp.zeros((fill, lines.shape[1]), lines.dtype)], axis=0)
    return jnp.broadcast_to(lines[None], (number,) + lines.shape)


def first_payload_kernel(
    block_ref, hidden_hbm, w_hbm, key_hbm, value_hbm, out_ref, hidden_ref, w_ref, key_ref, value_ref, lines, sems
):
    copies = [
        pltpu.make_async_copy(source, target, sems.at[n])
        for n, (source, target) in enumerate(
            ((hidden_hbm, hidden_ref), (w_hbm, w_ref), (key_hbm, key_ref), (value_hbm, value_ref))
        )
    ]
    for copy in copies:
        copy.start()
    count, width = hidden_ref.shape
    rows, total = w_ref.shape
    span, width_k = key_ref.shape[1:]
    nz = count // 2
    at = lax.broadcasted_iota(jnp.int32, (width, 128), 0) - block_ref[0] * rows
    pick = jnp.where(at == lax.broadcasted_iota(jnp.int32, (width, 128), 1), 1.0, 0.0).astype(BF16)
    copies[0].wait()
    normed = rms(hidden_ref[...].astype(F32)).astype(BF16)
    part = jnp.dot(normed, pick, preferred_element_type=F32)[:, :rows].astype(BF16)
    copies[1].wait()
    qkv = jnp.dot(part, w_ref[...], preferred_element_type=F32)
    low_lane = lax.broadcasted_iota(jnp.int32, (nz, 128), 1) < 64
    heads = (total - 2 * width_k) // 64
    for v in range(total // 128):
        first, second = qkv[:nz, 128 * v : 128 * v + 128], qkv[nz:, 128 * v : 128 * v + 128]
        even = jnp.where(low_lane, first, pltpu.roll(second, 64, 1))
        odd = jnp.where(low_lane, pltpu.roll(first, 64, 1), second)
        for chunk, line in ((2 * v, even), (2 * v + 1, odd)):
            if chunk < heads:
                y, row = chunk // 3, chunk % 3
                high = line.astype(BF16).astype(F32)
                lines[nz * y : nz * y + nz, 5 + row, :] = line - high
            else:
                y, row = (chunk - heads) % 8, 3 + (chunk - heads) // 8
                high = line
            lines[nz * y : nz * y + nz, row, :] = high
    out_ref[:, 2 * span :, :] = lines[...].astype(BF16)
    copies[2].wait()
    copies[3].wait()
    low_lane = lax.broadcasted_iota(jnp.int32, (count, span, 128), 2) < 64
    for m in range(width_k // 128):
        keys = key_ref[:, :, 128 * m : 128 * m + 128].astype(F32)
        values = value_ref[:, :, 128 * m : 128 * m + 128].astype(F32)
        even = jnp.where(low_lane, keys, pltpu.roll(values, 64, 2)).astype(BF16)
        odd = jnp.where(low_lane, pltpu.roll(keys, 64, 2), values).astype(BF16)
        for y, pair in ((2 * m, even), (2 * m + 1, odd)):
            for i in range(count // nz):
                out_ref[nz * y : nz * y + nz, span * i : span * i + span, :] = pair[nz * i : nz * i + nz]


def first_payload(block, hidden, w_qkv, keys, values, blocks):
    span = keys.shape[1]
    return pl.pallas_call(
        first_payload_kernel,
        out_shape=jax.ShapeDtypeStruct((blocks, 2 * span + 8, 128), BF16),
        in_specs=[SMEM] + [HBM] * 4,
        out_specs=VMEM,
        scratch_shapes=[pltpu.VMEM(a.shape, a.dtype) for a in (hidden, w_qkv, keys, values)]
        + [pltpu.VMEM((blocks, 8, 128), F32), pltpu.SemaphoreType.DMA((4,))],
        compiler_params=pltpu.CompilerParams(vmem_limit_bytes=60 << 20),
    )(block.reshape(1), hidden, w_qkv, keys, values)


def route_kernel(
    expert_ref, got_ref, hidden_ref, router_ref, routes_ref, in_ref, share_ref, mixed_ref, held, lines
):
    count, width = hidden_ref.shape
    got = got_ref[...].astype(F32)
    held[...] = got[:, :3] + got[:, 3:6]
    parts = width // 384
    blocks = [held[count * m : count * m + count, i, :] for m in range(parts) for i in range(3)]
    part = jnp.stack(blocks, axis=0)
    row = lax.broadcasted_iota(jnp.int32, part.shape, 1)
    lane = lax.broadcasted_iota(jnp.int32, part.shape, 2) // 8
    step = 1
    while step < count:
        down = pltpu.roll(pltpu.roll(part, count - step, 1), 8 * step, 2)
        back = pltpu.roll(pltpu.roll(part, step, 1), 128 - 8 * step, 2)
        low_row, low_lane = (row & step) == 0, (lane & step) == 0
        part = jnp.where(low_row == low_lane, part, jnp.where(low_row, down, back))
        step *= 2
    hidden = hidden_ref[...].astype(F32)
    total = jnp.zeros((count, 1), F32)
    for n in range(3 * parts):
        block = hidden[:, 128 * n : 128 * n + 128] + part[n]
        total = total + jnp.sum(block * block, axis=1, keepdims=True)
        mixed_ref[:, n // 3, n % 3, :] = block
        lines[:, 128 * n : 128 * n + 128] = block
    expert_in = (lines[...] * lax.rsqrt(total / width + EPS)).astype(BF16)
    in_ref[...] = expert_in
    choice = lax.dot_general(
        router_ref[...], expert_in, (((1,), (1,)), ((), ())), preferred_element_type=F32
    )
    experts = lax.broadcasted_iota(jnp.int32, choice.shape, 0)
    routes = routes_ref[...]
    e1, e2 = routes[0:1], routes[1:2]
    c1 = jnp.sum(jnp.where(experts == e1, choice, 0.0), axis=0, keepdims=True)
    c2 = jnp.sum(jnp.where(experts == e2, choice, 0.0), axis=0, keepdims=True)
    first = 1.0 / (1.0 + jnp.exp(c2 - c1))
    share = jnp.where(e1 == expert_ref[0], first, jnp.where(e2 == expert_ref[0], 1.0 - first, 0.0))
    row = lax.broadcasted_iota(jnp.int32, (count, count), 0)
    column = lax.broadcasted_iota(jnp.int32, (count, count), 1)
    share = jnp.sum(jnp.where(row == column, share, 0.0), axis=1, keepdims=True)
    share_ref[...] = jnp.broadcast_to(share, share_ref.shape)


def routed(expert, got, hidden, router, routes):
    count, width = hidden.shape
    parts = width // 384
    return pl.pallas_call(
        route_kernel,
        out_shape=(
            jax.ShapeDtypeStruct((count, width), BF16),
            jax.ShapeDtypeStruct((count, 128), F32),
            jax.ShapeDtypeStruct((count, parts, 3, 128), F32),
        ),
        in_specs=[SMEM] + [VMEM] * 4,
        out_specs=(VMEM, VMEM, VMEM),
        scratch_shapes=[pltpu.VMEM((got.shape[0], 3, 128), F32), pltpu.VMEM((count, width), F32)],
        compiler_params=pltpu.CompilerParams(vmem_limit_bytes=16 << 20),
    )(expert.reshape(1), got, hidden, router, routes)


def expert_kernel(in_ref, share_ref, gate_ref, up_ref, down_ref, out_ref, lines):
    expert_in = in_ref[...]
    width = expert_in.shape[1]
    gate = jnp.dot(expert_in, gate_ref[...], preferred_element_type=F32)
    upper = jnp.dot(expert_in, up_ref[...], preferred_element_type=F32)
    act = (gate / (1.0 + jnp.exp(-gate)) * upper * share_ref[:, 0:1]).astype(BF16)
    out = jnp.dot(act, down_ref[...], preferred_element_type=F32)
    for n in range(width // 128):
        line = out[:, 128 * n : 128 * n + 128]
        high = line.astype(BF16).astype(F32)
        lines[:, n // 3, n % 3, :] = high
        lines[:, n // 3, 3 + n % 3, :] = line - high
    out_ref[...] = lines[...].astype(BF16)


def expert_payload(expert_in, share, w_gate, w_up, w_down):
    count, width = expert_in.shape
    shape = (count, width // 384, 6, 128)
    return pl.pallas_call(
        expert_kernel,
        out_shape=jax.ShapeDtypeStruct(shape, BF16),
        in_specs=[VMEM] * 5,
        out_specs=VMEM,
        scratch_shapes=[pltpu.VMEM(shape, F32)],
        compiler_params=pltpu.CompilerParams(vmem_limit_bytes=16 << 20),
    )(expert_in, share, w_gate, w_up, w_down)


def solution(mesh):
    guide, blk, batch = (mesh.shape[a] for a in ("guide", "blk", "batch"))
    ny = KV_HEADS
    mesh = Mesh(mesh.devices.reshape(guide, ny, blk // ny, batch), ("guide",) + BLK + ("batch",))
    placed = (
        P("guide", "batch", None),
        P(BLK, None),
        P("guide", "batch", BLK, None),
        P("guide", "batch", BLK, None),
        P("guide", "batch"),
        P(BLK, None),
        P(),
        P("guide", "batch", None),
        P(None, BLK),
        P(None, BLK),
        P(BLK, None),
        P(None, BLK + ("batch",)),
        P(),
        P(),
        P(),
    )
    return jax.shard_map(
        local,
        mesh=mesh,
        in_specs=placed,
        out_specs=(
            P("guide", BLK + ("batch",)),
            P("guide", "batch", None),
            P("guide", "batch", None),
        ),
        check_vma=False,
    )
```

```python
import jax
import jax.numpy as jnp
from jax import lax
from jax.experimental import pallas as pl
from jax.experimental.pallas import tpu as pltpu
from jax.sharding import Mesh, PartitionSpec as P

HEADS = 24
KV_HEADS = 8
HEAD_DIM = 64
EXPERTS = 16
EXPERT_UNITS = 1024
EPS = 1e-05
F32 = jnp.float32
BF16 = jnp.bfloat16
BLK = ("y", "z")
HBM = pl.BlockSpec(memory_space=pltpu.HBM)
VMEM = pl.BlockSpec(memory_space=pltpu.VMEM)
SMEM = pl.BlockSpec(memory_space=pltpu.SMEM)


def rms(values):
    return values * lax.rsqrt(jnp.mean(values * values, axis=-1, keepdims=True) + EPS)


def exchange(value, axes):
    return lax.all_to_all(value, axes, 0, 0, tiled=True)


def halves(value):
    high = lax.reduce_precision(value, 8, 7)
    return high.astype(BF16), (value - high).astype(BF16)


def local(
    hidden,
    w_qkv,
    key_cache,
    value_cache,
    lengths,
    w_out,
    router,
    routes,
    w_gate,
    w_up,
    w_down,
    w_vocab,
    group_ids,
    weight_index,
    guidance_levels,
):
    group = HEADS // KV_HEADS
    y, z = lax.axis_index("y"), lax.axis_index("z")
    ny, nz = lax.axis_size("y"), lax.axis_size("z")
    blocks = ny * nz
    block = y * nz + z
    count = hidden.shape[1]
    pair = count // nz
    width = hidden.shape[2]
    width_q = HEADS * HEAD_DIM
    width_k = KV_HEADS * HEAD_DIM
    span = key_cache.shape[2]
    sent = first_payload(block, hidden[0], w_qkv, key_cache[0], value_cache[0], blocks)
    got = exchange(sent, BLK)
    cols = width // blocks
    w_rows = w_out.shape[0]
    n_w = -(-w_rows * cols // 128)
    w_blocks = w_out.reshape(w_rows, blocks // count, cols // 8, count, 8).transpose(1, 3, 0, 2, 4)
    w_blocks = w_blocks.reshape(blocks, w_rows * cols)
    w_blocks = jnp.pad(w_blocks, ((0, 0), (0, n_w * 128 - w_rows * cols))).reshape(blocks, n_w, 128)

    n_kv = pair * span
    kv = got[:, :n_kv].reshape(blocks, pair, span, 2 * HEAD_DIM).transpose(1, 0, 2, 3)
    kv = kv.reshape(pair, blocks * span, 2 * HEAD_DIM)
    sums = jnp.sum(got[:, n_kv:].astype(F32), axis=0)
    query = (sums[:group] + sums[group + 2 :]).reshape(group, pair, HEAD_DIM).transpose(1, 0, 2).astype(BF16)
    fresh = sums[group : group + 2].astype(BF16)
    new_k, new_v = fresh[0].reshape(pair, HEAD_DIM), fresh[1].reshape(pair, HEAD_DIM)
    scale = HEAD_DIM ** (-0.5)
    scores = jnp.einsum("ihd,ipd->ihp", query, kv[:, :, :HEAD_DIM], preferred_element_type=F32) * scale
    own = jnp.sum(query.astype(F32) * new_k.astype(F32)[:, None, :], axis=-1) * scale
    lens = lax.dynamic_index_in_dim(lengths[0].reshape(pair, nz), z, 1, False)
    valid = (jnp.arange(blocks * span)[None, :] < lens[:, None])[:, None, :]
    top = jnp.maximum(jnp.max(jnp.where(valid, scores, -1e30), axis=-1), own)
    probs = jnp.exp(jnp.where(valid, scores - top[..., None], -1e30))
    own_prob = jnp.exp(own - top)
    total = jnp.sum(probs, axis=-1) + own_prob
    acc = jnp.einsum("ihp,ipd->ihd", probs.astype(BF16), kv[:, :, HEAD_DIM:], preferred_element_type=F32)
    own_r = lax.reduce_precision(own_prob, 8, 7)
    acc = acc + own_r[..., None] * new_v.astype(F32)[:, None, :]
    attn = (acc / total[..., None]).astype(BF16)
    n_a = pair * group * HEAD_DIM // 128
    attn = jnp.broadcast_to(attn.reshape(1, n_a, 128), (blocks, n_a, 128))
    half_rows = group_ids.shape[0] // 2
    start = lax.axis_index("guide").astype(jnp.uint32) * half_rows
    weight_rows = request_weights(group_ids, weight_index, guidance_levels)
    weight_rows = lax.dynamic_slice(weight_rows, (start,), (half_rows,))
    sent = jnp.concatenate([attn, w_blocks], axis=1)
    sent, fresh, weight_rows, start = lax.optimization_barrier((sent, fresh, weight_rows, start))
    got = exchange(sent, BLK)

    w_cols = got[:, n_a:].reshape(blocks, n_w * 128)[:, : w_rows * cols].reshape(-1, cols)
    attn = got[:, :n_a].reshape(ny, nz, pair, group * HEAD_DIM).transpose(2, 1, 0, 3).reshape(count, width_q)
    part = jnp.dot(attn, w_cols, preferred_element_type=F32)
    own_lines = count * cols // 128
    part = part.reshape(count, own_lines, 8).transpose(1, 0, 2)
    high, low = halves(part.reshape(own_lines, 128))
    got = exchange(to_all(jnp.concatenate([high, low, fresh], axis=0), blocks), BLK)
    parts = width // (own_lines * 128)
    expert = lax.div(block * w_gate.shape[1], EXPERT_UNITS)
    where = jnp.stack([expert, lax.div(block, parts), lax.rem(block, parts)])
    expert_in, share, mixed_piece, fresh_k, fresh_v = routed(
        where, got, hidden[0], router.T, routes[0].T, width_k
    )
    sent = expert_payload(expert_in, share, w_gate, w_up, w_down)
    got = exchange(sent.reshape(blocks, 2 * own_lines, 128), BLK)

    piece = jnp.sum(got[:, :own_lines].astype(F32) + got[:, own_lines : 2 * own_lines].astype(F32), axis=0)
    piece = (mixed_piece + piece).astype(BF16)
    piece = jnp.concatenate([piece, jnp.zeros((1, 128), BF16)], axis=0)
    everyone = blocks * lax.axis_size("batch")
    got = exchange(jnp.broadcast_to(piece[None], (everyone,) + piece.shape), ("batch",) + BLK)
    outgoing = lax.optimization_barrier(got[:, :own_lines].astype(F32).reshape(-1, width))
    final_in = rms(outgoing).astype(BF16)
    stream_logits = jnp.dot(final_in, w_vocab, preferred_element_type=F32).astype(BF16)
    both = lax.all_gather(stream_logits, "guide", axis=0, tiled=False)
    zero = jnp.zeros((), start.dtype)
    both = lax.dynamic_slice(both, (zero, start, zero), (2, half_rows, both.shape[2])).astype(F32)
    cond, uncond = both[0], both[1]
    logits = uncond + weight_rows[:, None] * (cond - uncond)
    return (logits, fresh_k[None], fresh_v[None])


def request_weights(group_ids, weight_index, guidance_levels):
    group_count = weight_index.shape[0]
    level_count = guidance_levels.shape[0]
    in_group = (group_ids[:, None] == jnp.arange(group_count)[None, :]).astype(F32)
    level_pick = (weight_index[:, None] == jnp.arange(level_count)[None, :]).astype(F32)
    group_weight = jnp.sum(level_pick * guidance_levels[None, :], axis=1)
    return jnp.sum(in_group * group_weight[None, :], axis=1)


def to_all(lines, number):
    fill = -lines.shape[0] % 8
    lines = jnp.concatenate([lines, jnp.zeros((fill, lines.shape[1]), lines.dtype)], axis=0)
    return jnp.broadcast_to(lines[None], (number,) + lines.shape)


def first_payload_kernel(
    block_ref, hidden_hbm, w_hbm, key_hbm, value_hbm, out_ref, hidden_ref, w_ref, key_ref, value_ref, lines, sems
):
    copies = [
        pltpu.make_async_copy(source, target, sems.at[n])
        for n, (source, target) in enumerate(
            ((hidden_hbm, hidden_ref), (w_hbm, w_ref), (key_hbm, key_ref), (value_hbm, value_ref))
        )
    ]
    for copy in copies:
        copy.start()
    count, width = hidden_ref.shape
    rows, total = w_ref.shape
    span, width_k = key_ref.shape[1:]
    nz = count // 2
    at = lax.broadcasted_iota(jnp.int32, (width, 128), 0) - block_ref[0] * rows
    pick = jnp.where(at == lax.broadcasted_iota(jnp.int32, (width, 128), 1), 1.0, 0.0).astype(BF16)
    copies[0].wait()
    normed = rms(hidden_ref[...].astype(F32)).astype(BF16)
    part = jnp.dot(normed, pick, preferred_element_type=F32)[:, :rows].astype(BF16)
    copies[1].wait()
    qkv = jnp.dot(part, w_ref[...], preferred_element_type=F32)
    low_lane = lax.broadcasted_iota(jnp.int32, (nz, 128), 1) < 64
    heads = (total - 2 * width_k) // 64
    for v in range(total // 128):
        first, second = qkv[:nz, 128 * v : 128 * v + 128], qkv[nz:, 128 * v : 128 * v + 128]
        even = jnp.where(low_lane, first, pltpu.roll(second, 64, 1))
        odd = jnp.where(low_lane, pltpu.roll(first, 64, 1), second)
        for chunk, line in ((2 * v, even), (2 * v + 1, odd)):
            if chunk < heads:
                y, row = chunk // 3, chunk % 3
                high = line.astype(BF16).astype(F32)
                lines[nz * y : nz * y + nz, 5 + row, :] = line - high
            else:
                y, row = (chunk - heads) % 8, 3 + (chunk - heads) // 8
                high = line
            lines[nz * y : nz * y + nz, row, :] = high
    out_ref[:, 2 * span :, :] = lines[...].astype(BF16)
    copies[2].wait()
    copies[3].wait()
    low_lane = lax.broadcasted_iota(jnp.int32, (count, span, 128), 2) < 64
    for m in range(width_k // 128):
        keys = key_ref[:, :, 128 * m : 128 * m + 128].astype(F32)
        values = value_ref[:, :, 128 * m : 128 * m + 128].astype(F32)
        even = jnp.where(low_lane, keys, pltpu.roll(values, 64, 2)).astype(BF16)
        odd = jnp.where(low_lane, pltpu.roll(keys, 64, 2), values).astype(BF16)
        for y, pair in ((2 * m, even), (2 * m + 1, odd)):
            for i in range(count // nz):
                out_ref[nz * y : nz * y + nz, span * i : span * i + span, :] = pair[nz * i : nz * i + nz]


def first_payload(block, hidden, w_qkv, keys, values, blocks):
    span = keys.shape[1]
    return pl.pallas_call(
        first_payload_kernel,
        out_shape=jax.ShapeDtypeStruct((blocks, 2 * span + 8, 128), BF16),
        in_specs=[SMEM] + [HBM] * 4,
        out_specs=VMEM,
        scratch_shapes=[pltpu.VMEM(a.shape, a.dtype) for a in (hidden, w_qkv, keys, values)]
        + [pltpu.VMEM((blocks, 8, 128), F32), pltpu.SemaphoreType.DMA((4,))],
        compiler_params=pltpu.CompilerParams(vmem_limit_bytes=60 << 20),
    )(block.reshape(1), hidden, w_qkv, keys, values)


def route_kernel(
    where_ref,
    got_ref,
    hidden_ref,
    router_ref,
    routes_ref,
    in_ref,
    share_ref,
    piece_ref,
    key_ref,
    value_ref,
    held,
    lines,
    mixed_ref,
):
    count, width = hidden_ref.shape
    got = got_ref[...].astype(F32)
    held[:, :3, :] = got[:, :3] + got[:, 3:6]
    held[:, 3:, :] = got[:, 6:]
    half = count // 2
    low_lane = lax.broadcasted_iota(jnp.int32, (half, 128), 1) < 64
    for n, out_ref in ((3, key_ref), (4, value_ref)):
        for v in range(out_ref.shape[1] // 128):
            even = held[2 * half * v : 2 * half * v + half, n, :]
            odd = held[2 * half * v + half : 2 * half * v + 2 * half, n, :]
            first = jnp.where(low_lane, even, pltpu.roll(odd, 64, 1))
            second = jnp.where(low_lane, pltpu.roll(even, 64, 1), odd)
            both = jnp.concatenate([first, second], axis=0)
            out_ref[:, 128 * v : 128 * v + 128] = both.astype(BF16)
    parts = width // 384
    blocks = [held[count * m : count * m + count, i, :] for m in range(parts) for i in range(3)]
    part = jnp.stack(blocks, axis=0)
    row = lax.broadcasted_iota(jnp.int32, part.shape, 1)
    lane = lax.broadcasted_iota(jnp.int32, part.shape, 2) // 8
    step = 1
    while step < count:
        down = pltpu.roll(pltpu.roll(part, count - step, 1), 8 * step, 2)
        back = pltpu.roll(pltpu.roll(part, step, 1), 128 - 8 * step, 2)
        low_row, low_lane = (row & step) == 0, (lane & step) == 0
        part = jnp.where(low_row == low_lane, part, jnp.where(low_row, down, back))
        step *= 2
    hidden = hidden_ref[...].astype(F32)
    total = jnp.zeros((count, 1), F32)
    for n in range(3 * parts):
        block = hidden[:, 128 * n : 128 * n + 128] + part[n]
        total = total + jnp.sum(block * block, axis=1, keepdims=True)
        mixed_ref[:, n // 3, n % 3, :] = block
        lines[:, 128 * n : 128 * n + 128] = block
    expert_in = (lines[...] * lax.rsqrt(total / width + EPS)).astype(BF16)
    in_ref[...] = expert_in
    piece_ref[...] = mixed_ref[where_ref[1], where_ref[2]]
    choice = lax.dot_general(
        router_ref[...], expert_in, (((1,), (1,)), ((), ())), preferred_element_type=F32
    )
    experts = lax.broadcasted_iota(jnp.int32, choice.shape, 0)
    routes = routes_ref[...]
    e1, e2 = routes[0:1], routes[1:2]
    c1 = jnp.sum(jnp.where(experts == e1, choice, 0.0), axis=0, keepdims=True)
    c2 = jnp.sum(jnp.where(experts == e2, choice, 0.0), axis=0, keepdims=True)
    first = 1.0 / (1.0 + jnp.exp(c2 - c1))
    share = jnp.where(e1 == where_ref[0], first, jnp.where(e2 == where_ref[0], 1.0 - first, 0.0))
    row = lax.broadcasted_iota(jnp.int32, (count, count), 0)
    column = lax.broadcasted_iota(jnp.int32, (count, count), 1)
    share = jnp.sum(jnp.where(row == column, share, 0.0), axis=1, keepdims=True)
    share_ref[...] = jnp.broadcast_to(share, share_ref.shape)


def routed(where, got, hidden, router, routes, width_k):
    count, width = hidden.shape
    parts = width // 384
    return pl.pallas_call(
        route_kernel,
        out_shape=(
            jax.ShapeDtypeStruct((count, width), BF16),
            jax.ShapeDtypeStruct((count, 128), F32),
            jax.ShapeDtypeStruct((3, 128), F32),
            jax.ShapeDtypeStruct((count, width_k), BF16),
            jax.ShapeDtypeStruct((count, width_k), BF16),
        ),
        in_specs=[SMEM] + [VMEM] * 4,
        out_specs=(VMEM,) * 5,
        scratch_shapes=[
            pltpu.VMEM((got.shape[0], 5, 128), F32),
            pltpu.VMEM((count, width), F32),
            pltpu.VMEM((count, parts, 3, 128), F32),
        ],
        compiler_params=pltpu.CompilerParams(vmem_limit_bytes=16 << 20),
    )(where, got, hidden, router, routes)


def expert_kernel(in_ref, share_ref, gate_ref, up_ref, down_ref, out_ref, lines):
    expert_in = in_ref[...]
    width = expert_in.shape[1]
    gate = jnp.dot(expert_in, gate_ref[...], preferred_element_type=F32)
    upper = jnp.dot(expert_in, up_ref[...], preferred_element_type=F32)
    act = (gate / (1.0 + jnp.exp(-gate)) * upper * share_ref[:, 0:1]).astype(BF16)
    out = jnp.dot(act, down_ref[...], preferred_element_type=F32)
    for n in range(width // 128):
        line = out[:, 128 * n : 128 * n + 128]
        high = line.astype(BF16).astype(F32)
        lines[:, n // 3, n % 3, :] = high
        lines[:, n // 3, 3 + n % 3, :] = line - high
    out_ref[...] = lines[...].astype(BF16)


def expert_payload(expert_in, share, w_gate, w_up, w_down):
    count, width = expert_in.shape
    shape = (count, width // 384, 6, 128)
    return pl.pallas_call(
        expert_kernel,
        out_shape=jax.ShapeDtypeStruct(shape, BF16),
        in_specs=[VMEM] * 5,
        out_specs=VMEM,
        scratch_shapes=[pltpu.VMEM(shape, F32)],
        compiler_params=pltpu.CompilerParams(vmem_limit_bytes=16 << 20),
    )(expert_in, share, w_gate, w_up, w_down)


def solution(mesh):
    guide, blk, batch = (mesh.shape[a] for a in ("guide", "blk", "batch"))
    ny = KV_HEADS
    mesh = Mesh(mesh.devices.reshape(guide, ny, blk // ny, batch), ("guide",) + BLK + ("batch",))
    placed = (
        P("guide", "batch", None),
        P(BLK, None),
        P("guide", "batch", BLK, None),
        P("guide", "batch", BLK, None),
        P("guide", "batch"),
        P(BLK, None),
        P(),
        P("guide", "batch", None),
        P(None, BLK),
        P(None, BLK),
        P(BLK, None),
        P(None, BLK + ("batch",)),
        P(),
        P(),
        P(),
    )
    return jax.shard_map(
        local,
        mesh=mesh,
        in_specs=placed,
        out_specs=(
            P("guide", BLK + ("batch",)),
            P("guide", "batch", None),
            P("guide", "batch", None),
        ),
        check_vma=False,
    )
```

```python
import jax
import jax.numpy as jnp
from jax import lax
from jax.experimental import pallas as pl
from jax.experimental.pallas import tpu as pltpu
from jax.sharding import Mesh, PartitionSpec as P

HEADS = 24
KV_HEADS = 8
HEAD_DIM = 64
EXPERTS = 16
EXPERT_UNITS = 1024
EPS = 1e-05
F32 = jnp.float32
BF16 = jnp.bfloat16
BLK = ("y", "z")
HBM = pl.BlockSpec(memory_space=pltpu.HBM)
VMEM = pl.BlockSpec(memory_space=pltpu.VMEM)
SMEM = pl.BlockSpec(memory_space=pltpu.SMEM)


def rms(values):
    return values * lax.rsqrt(jnp.mean(values * values, axis=-1, keepdims=True) + EPS)


def exchange(value, axes):
    return lax.all_to_all(value, axes, 0, 0, tiled=True)


def halves(value):
    high = lax.reduce_precision(value, 8, 7)
    return high.astype(BF16), (value - high).astype(BF16)


def local(
    hidden,
    w_qkv,
    key_cache,
    value_cache,
    lengths,
    w_out,
    router,
    routes,
    w_gate,
    w_up,
    w_down,
    w_vocab,
    group_ids,
    weight_index,
    guidance_levels,
):
    group = HEADS // KV_HEADS
    y, z = lax.axis_index("y"), lax.axis_index("z")
    ny, nz = lax.axis_size("y"), lax.axis_size("z")
    blocks = ny * nz
    block = y * nz + z
    count = hidden.shape[1]
    pair = count // nz
    width = hidden.shape[2]
    width_q = HEADS * HEAD_DIM
    width_k = KV_HEADS * HEAD_DIM
    span = key_cache.shape[2]
    sent = first_payload(block, hidden[0], w_qkv, key_cache[0], value_cache[0], blocks)
    got = exchange(sent, BLK)
    cols = width // blocks
    w_rows = w_out.shape[0]
    n_w = -(-w_rows * cols // 128)
    w_blocks = w_out.reshape(w_rows, blocks // count, cols // 8, count, 8).transpose(1, 3, 0, 2, 4)
    w_blocks = w_blocks.reshape(blocks, w_rows * cols)
    w_blocks = jnp.pad(w_blocks, ((0, 0), (0, n_w * 128 - w_rows * cols))).reshape(blocks, n_w, 128)

    n_kv = pair * span
    kv = got[:, :n_kv].reshape(blocks, pair, span, 2 * HEAD_DIM).transpose(1, 0, 2, 3)
    kv = kv.reshape(pair, blocks * span, 2 * HEAD_DIM)
    sums = jnp.sum(got[:, n_kv:].astype(F32), axis=0)
    query = (sums[:group] + sums[group + 2 :]).reshape(group, pair, HEAD_DIM).transpose(1, 0, 2).astype(BF16)
    fresh = sums[group : group + 2].astype(BF16)
    new_k, new_v = fresh[0].reshape(pair, HEAD_DIM), fresh[1].reshape(pair, HEAD_DIM)
    scale = HEAD_DIM ** (-0.5)
    scores = jnp.einsum("ihd,ipd->ihp", query, kv[:, :, :HEAD_DIM], preferred_element_type=F32) * scale
    own = jnp.sum(query.astype(F32) * new_k.astype(F32)[:, None, :], axis=-1) * scale
    lens = lax.dynamic_index_in_dim(lengths[0].reshape(pair, nz), z, 1, False)
    valid = (jnp.arange(blocks * span)[None, :] < lens[:, None])[:, None, :]
    top = jnp.maximum(jnp.max(jnp.where(valid, scores, -1e30), axis=-1), own)
    probs = jnp.exp(jnp.where(valid, scores - top[..., None], -1e30))
    own_prob = jnp.exp(own - top)
    total = jnp.sum(probs, axis=-1) + own_prob
    acc = jnp.einsum("ihp,ipd->ihd", probs.astype(BF16), kv[:, :, HEAD_DIM:], preferred_element_type=F32)
    own_r = lax.reduce_precision(own_prob, 8, 7)
    acc = acc + own_r[..., None] * new_v.astype(F32)[:, None, :]
    attn = (acc / total[..., None]).astype(BF16)
    n_a = pair * group * HEAD_DIM // 128
    attn = jnp.broadcast_to(attn.reshape(1, n_a, 128), (blocks, n_a, 128))
    half_rows = group_ids.shape[0] // 2
    stream = lax.axis_index("guide")
    weight_rows = request_weights(group_ids, weight_index, guidance_levels)
    weight_rows = lax.dynamic_slice(weight_rows, (stream.astype(jnp.uint32) * half_rows,), (half_rows,))
    weight_rows = jnp.broadcast_to(weight_rows[:, None], (half_rows, w_vocab.shape[1]))
    parts = width // 384
    expert = lax.div(block * w_gate.shape[1], EXPERT_UNITS)
    where = jnp.stack([expert, lax.div(block, parts), lax.rem(block, parts)])
    sent = jnp.concatenate([attn, w_blocks], axis=1)
    sent, fresh, weight_rows, stream, where = lax.optimization_barrier((sent, fresh, weight_rows, stream, where))
    got = exchange(sent, BLK)

    w_cols = got[:, n_a:].reshape(blocks, n_w * 128)[:, : w_rows * cols].reshape(-1, cols)
    attn = got[:, :n_a].reshape(ny, nz, pair, group * HEAD_DIM).transpose(2, 1, 0, 3).reshape(count, width_q)
    part = jnp.dot(attn, w_cols, preferred_element_type=F32)
    own_lines = count * cols // 128
    part = part.reshape(count, own_lines, 8).transpose(1, 0, 2)
    high, low = halves(part.reshape(own_lines, 128))
    got = exchange(to_all(jnp.concatenate([high, low, fresh], axis=0), blocks), BLK)
    expert_in, share, mixed_piece, fresh_k, fresh_v = routed(
        where, got, hidden[0], router.T, routes[0].T, width_k
    )
    sent = expert_payload(expert_in, share, w_gate, w_up, w_down)
    got = exchange(sent.reshape(blocks, 2 * own_lines, 128), BLK)

    piece = jnp.sum(got[:, :own_lines].astype(F32) + got[:, own_lines : 2 * own_lines].astype(F32), axis=0)
    piece = (mixed_piece + piece).astype(BF16)
    piece = jnp.concatenate([piece, jnp.zeros((1, 128), BF16)], axis=0)
    everyone = blocks * lax.axis_size("batch")
    got = exchange(jnp.broadcast_to(piece[None], (everyone,) + piece.shape), ("batch",) + BLK)
    outgoing = lax.optimization_barrier(got[:, :own_lines].astype(F32).reshape(-1, width))
    final_in = rms(outgoing).astype(BF16)
    stream_logits = jnp.dot(final_in, w_vocab, preferred_element_type=F32).astype(BF16)
    both = lax.all_gather(stream_logits, "guide", axis=0, tiled=False)
    return last_outputs(stream, both, weight_rows, fresh_k, fresh_v)


def last_kernel(stream_ref, both_ref, weight_ref, key_in, value_in, logits_ref, key_ref, value_ref):
    half_rows = logits_ref.shape[0]
    first = stream_ref[0] == 0
    cond = jnp.where(first, both_ref[0, :half_rows], both_ref[0, half_rows:]).astype(F32)
    uncond = jnp.where(first, both_ref[1, :half_rows], both_ref[1, half_rows:]).astype(F32)
    logits_ref[...] = uncond + weight_ref[...] * (cond - uncond)
    key_ref[0] = key_in[...].astype(BF16)
    value_ref[0] = value_in[...].astype(BF16)


def last_outputs(stream, both, weight_rows, fresh_k, fresh_v):
    shape = weight_rows.shape
    return pl.pallas_call(
        last_kernel,
        out_shape=(
            jax.ShapeDtypeStruct(shape, F32),
            jax.ShapeDtypeStruct((1,) + fresh_k.shape, BF16),
            jax.ShapeDtypeStruct((1,) + fresh_v.shape, BF16),
        ),
        in_specs=[SMEM] + [VMEM] * 4,
        out_specs=(VMEM,) * 3,
        compiler_params=pltpu.CompilerParams(vmem_limit_bytes=16 << 20),
    )(stream.reshape(1), both, weight_rows, fresh_k, fresh_v)


def request_weights(group_ids, weight_index, guidance_levels):
    group_count = weight_index.shape[0]
    level_count = guidance_levels.shape[0]
    in_group = (group_ids[:, None] == jnp.arange(group_count)[None, :]).astype(F32)
    level_pick = (weight_index[:, None] == jnp.arange(level_count)[None, :]).astype(F32)
    group_weight = jnp.sum(level_pick * guidance_levels[None, :], axis=1)
    return jnp.sum(in_group * group_weight[None, :], axis=1)


def to_all(lines, number):
    fill = -lines.shape[0] % 8
    lines = jnp.concatenate([lines, jnp.zeros((fill, lines.shape[1]), lines.dtype)], axis=0)
    return jnp.broadcast_to(lines[None], (number,) + lines.shape)


def first_payload_kernel(
    block_ref, hidden_hbm, w_hbm, key_hbm, value_hbm, out_ref, hidden_ref, w_ref, key_ref, value_ref, lines, sems
):
    copies = [
        pltpu.make_async_copy(source, target, sems.at[n])
        for n, (source, target) in enumerate(
            ((hidden_hbm, hidden_ref), (w_hbm, w_ref), (key_hbm, key_ref), (value_hbm, value_ref))
        )
    ]
    for copy in copies:
        copy.start()
    count, width = hidden_ref.shape
    rows, total = w_ref.shape
    span, width_k = key_ref.shape[1:]
    nz = count // 2
    at = lax.broadcasted_iota(jnp.int32, (width, 128), 0) - block_ref[0] * rows
    pick = jnp.where(at == lax.broadcasted_iota(jnp.int32, (width, 128), 1), 1.0, 0.0).astype(BF16)
    copies[0].wait()
    normed = rms(hidden_ref[...].astype(F32)).astype(BF16)
    part = jnp.dot(normed, pick, preferred_element_type=F32)[:, :rows].astype(BF16)
    copies[1].wait()
    qkv = jnp.dot(part, w_ref[...], preferred_element_type=F32)
    low_lane = lax.broadcasted_iota(jnp.int32, (nz, 128), 1) < 64
    heads = (total - 2 * width_k) // 64
    for v in range(total // 128):
        first, second = qkv[:nz, 128 * v : 128 * v + 128], qkv[nz:, 128 * v : 128 * v + 128]
        even = jnp.where(low_lane, first, pltpu.roll(second, 64, 1))
        odd = jnp.where(low_lane, pltpu.roll(first, 64, 1), second)
        for chunk, line in ((2 * v, even), (2 * v + 1, odd)):
            if chunk < heads:
                y, row = chunk // 3, chunk % 3
                high = line.astype(BF16).astype(F32)
                lines[nz * y : nz * y + nz, 5 + row, :] = line - high
            else:
                y, row = (chunk - heads) % 8, 3 + (chunk - heads) // 8
                high = line
            lines[nz * y : nz * y + nz, row, :] = high
    out_ref[:, 2 * span :, :] = lines[...].astype(BF16)
    copies[2].wait()
    copies[3].wait()
    low_lane = lax.broadcasted_iota(jnp.int32, (count, span, 128), 2) < 64
    for m in range(width_k // 128):
        keys = key_ref[:, :, 128 * m : 128 * m + 128].astype(F32)
        values = value_ref[:, :, 128 * m : 128 * m + 128].astype(F32)
        even = jnp.where(low_lane, keys, pltpu.roll(values, 64, 2)).astype(BF16)
        odd = jnp.where(low_lane, pltpu.roll(keys, 64, 2), values).astype(BF16)
        for y, pair in ((2 * m, even), (2 * m + 1, odd)):
            for i in range(count // nz):
                out_ref[nz * y : nz * y + nz, span * i : span * i + span, :] = pair[nz * i : nz * i + nz]


def first_payload(block, hidden, w_qkv, keys, values, blocks):
    span = keys.shape[1]
    return pl.pallas_call(
        first_payload_kernel,
        out_shape=jax.ShapeDtypeStruct((blocks, 2 * span + 8, 128), BF16),
        in_specs=[SMEM] + [HBM] * 4,
        out_specs=VMEM,
        scratch_shapes=[pltpu.VMEM(a.shape, a.dtype) for a in (hidden, w_qkv, keys, values)]
        + [pltpu.VMEM((blocks, 8, 128), F32), pltpu.SemaphoreType.DMA((4,))],
        compiler_params=pltpu.CompilerParams(vmem_limit_bytes=60 << 20),
    )(block.reshape(1), hidden, w_qkv, keys, values)


def route_kernel(
    where_ref,
    got_ref,
    hidden_ref,
    router_ref,
    routes_ref,
    in_ref,
    share_ref,
    piece_ref,
    key_ref,
    value_ref,
    held,
    lines,
    mixed_ref,
):
    count, width = hidden_ref.shape
    got = got_ref[...].astype(F32)
    held[:, :3, :] = got[:, :3] + got[:, 3:6]
    held[:, 3:, :] = got[:, 6:]
    half = count // 2
    low_lane = lax.broadcasted_iota(jnp.int32, (half, 128), 1) < 64
    for n, out_ref in ((3, key_ref), (4, value_ref)):
        for v in range(out_ref.shape[1] // 128):
            even = held[2 * half * v : 2 * half * v + half, n, :]
            odd = held[2 * half * v + half : 2 * half * v + 2 * half, n, :]
            first = jnp.where(low_lane, even, pltpu.roll(odd, 64, 1))
            second = jnp.where(low_lane, pltpu.roll(even, 64, 1), odd)
            out_ref[:, 128 * v : 128 * v + 128] = jnp.concatenate([first, second], axis=0)
    parts = width // 384
    blocks = [held[count * m : count * m + count, i, :] for m in range(parts) for i in range(3)]
    part = jnp.stack(blocks, axis=0)
    row = lax.broadcasted_iota(jnp.int32, part.shape, 1)
    lane = lax.broadcasted_iota(jnp.int32, part.shape, 2) // 8
    step = 1
    while step < count:
        down = pltpu.roll(pltpu.roll(part, count - step, 1), 8 * step, 2)
        back = pltpu.roll(pltpu.roll(part, step, 1), 128 - 8 * step, 2)
        low_row, low_lane = (row & step) == 0, (lane & step) == 0
        part = jnp.where(low_row == low_lane, part, jnp.where(low_row, down, back))
        step *= 2
    hidden = hidden_ref[...].astype(F32)
    total = jnp.zeros((count, 1), F32)
    for n in range(3 * parts):
        block = hidden[:, 128 * n : 128 * n + 128] + part[n]
        total = total + jnp.sum(block * block, axis=1, keepdims=True)
        mixed_ref[:, n // 3, n % 3, :] = block
        lines[:, 128 * n : 128 * n + 128] = block
    expert_in = (lines[...] * lax.rsqrt(total / width + EPS)).astype(BF16)
    in_ref[...] = expert_in
    piece_ref[...] = mixed_ref[where_ref[1], where_ref[2]]
    choice = lax.dot_general(
        router_ref[...], expert_in, (((1,), (1,)), ((), ())), preferred_element_type=F32
    )
    experts = lax.broadcasted_iota(jnp.int32, choice.shape, 0)
    routes = routes_ref[...]
    e1, e2 = routes[0:1], routes[1:2]
    c1 = jnp.sum(jnp.where(experts == e1, choice, 0.0), axis=0, keepdims=True)
    c2 = jnp.sum(jnp.where(experts == e2, choice, 0.0), axis=0, keepdims=True)
    first = 1.0 / (1.0 + jnp.exp(c2 - c1))
    share = jnp.where(e1 == where_ref[0], first, jnp.where(e2 == where_ref[0], 1.0 - first, 0.0))
    row = lax.broadcasted_iota(jnp.int32, (count, count), 0)
    column = lax.broadcasted_iota(jnp.int32, (count, count), 1)
    share = jnp.sum(jnp.where(row == column, share, 0.0), axis=1, keepdims=True)
    share_ref[...] = jnp.broadcast_to(share, share_ref.shape)


def routed(where, got, hidden, router, routes, width_k):
    count, width = hidden.shape
    parts = width // 384
    return pl.pallas_call(
        route_kernel,
        out_shape=(
            jax.ShapeDtypeStruct((count, width), BF16),
            jax.ShapeDtypeStruct((count, 128), F32),
            jax.ShapeDtypeStruct((3, 128), F32),
            jax.ShapeDtypeStruct((count, width_k), F32),
            jax.ShapeDtypeStruct((count, width_k), F32),
        ),
        in_specs=[SMEM] + [VMEM] * 4,
        out_specs=(VMEM,) * 5,
        scratch_shapes=[
            pltpu.VMEM((got.shape[0], 5, 128), F32),
            pltpu.VMEM((count, width), F32),
            pltpu.VMEM((count, parts, 3, 128), F32),
        ],
        compiler_params=pltpu.CompilerParams(vmem_limit_bytes=16 << 20),
    )(where, got, hidden, router, routes)


def expert_kernel(in_ref, share_ref, gate_ref, up_ref, down_ref, out_ref, lines):
    expert_in = in_ref[...]
    width = expert_in.shape[1]
    gate = jnp.dot(expert_in, gate_ref[...], preferred_element_type=F32)
    upper = jnp.dot(expert_in, up_ref[...], preferred_element_type=F32)
    act = (gate / (1.0 + jnp.exp(-gate)) * upper * share_ref[:, 0:1]).astype(BF16)
    out = jnp.dot(act, down_ref[...], preferred_element_type=F32)
    for n in range(width // 128):
        line = out[:, 128 * n : 128 * n + 128]
        high = line.astype(BF16).astype(F32)
        lines[:, n // 3, n % 3, :] = high
        lines[:, n // 3, 3 + n % 3, :] = line - high
    out_ref[...] = lines[...].astype(BF16)


def expert_payload(expert_in, share, w_gate, w_up, w_down):
    count, width = expert_in.shape
    shape = (count, width // 384, 6, 128)
    return pl.pallas_call(
        expert_kernel,
        out_shape=jax.ShapeDtypeStruct(shape, BF16),
        in_specs=[VMEM] * 5,
        out_specs=VMEM,
        scratch_shapes=[pltpu.VMEM(shape, F32)],
        compiler_params=pltpu.CompilerParams(vmem_limit_bytes=16 << 20),
    )(expert_in, share, w_gate, w_up, w_down)


def solution(mesh):
    guide, blk, batch = (mesh.shape[a] for a in ("guide", "blk", "batch"))
    ny = KV_HEADS
    mesh = Mesh(mesh.devices.reshape(guide, ny, blk // ny, batch), ("guide",) + BLK + ("batch",))
    placed = (
        P("guide", "batch", None),
        P(BLK, None),
        P("guide", "batch", BLK, None),
        P("guide", "batch", BLK, None),
        P("guide", "batch"),
        P(BLK, None),
        P(),
        P("guide", "batch", None),
        P(None, BLK),
        P(None, BLK),
        P(BLK, None),
        P(None, BLK + ("batch",)),
        P(),
        P(),
        P(),
    )
    return jax.shard_map(
        local,
        mesh=mesh,
        in_specs=placed,
        out_specs=(
            P("guide", BLK + ("batch",)),
            P("guide", "batch", None),
            P("guide", "batch", None),
        ),
        check_vma=False,
    )
```

```python
import jax
import jax.numpy as jnp
from jax import lax
from jax.experimental import pallas as pl
from jax.experimental.pallas import tpu as pltpu
from jax.sharding import Mesh, PartitionSpec as P

HEADS = 24
KV_HEADS = 8
HEAD_DIM = 64
EXPERTS = 16
EXPERT_UNITS = 1024
EPS = 1e-05
F32 = jnp.float32
BF16 = jnp.bfloat16
BLK = ("y", "z")
HBM = pl.BlockSpec(memory_space=pltpu.HBM)
VMEM = pl.BlockSpec(memory_space=pltpu.VMEM)
SMEM = pl.BlockSpec(memory_space=pltpu.SMEM)


def rms(values):
    return values * lax.rsqrt(jnp.mean(values * values, axis=-1, keepdims=True) + EPS)


def exchange(value, axes):
    return lax.all_to_all(value, axes, 0, 0, tiled=True)


def halves(value):
    high = lax.reduce_precision(value, 8, 7)
    return high.astype(BF16), (value - high).astype(BF16)


def local(
    hidden,
    w_qkv,
    key_cache,
    value_cache,
    lengths,
    w_out,
    router,
    routes,
    w_gate,
    w_up,
    w_down,
    w_vocab,
    group_ids,
    weight_index,
    guidance_levels,
):
    group = HEADS // KV_HEADS
    y, z = lax.axis_index("y"), lax.axis_index("z")
    ny, nz = lax.axis_size("y"), lax.axis_size("z")
    blocks = ny * nz
    block = y * nz + z
    count = hidden.shape[1]
    pair = count // nz
    width = hidden.shape[2]
    width_q = HEADS * HEAD_DIM
    width_k = KV_HEADS * HEAD_DIM
    span = key_cache.shape[2]
    sent = first_payload(block, hidden[0], w_qkv, key_cache[0], value_cache[0], blocks)
    got = exchange(sent, BLK)
    cols = width // blocks
    w_rows = w_out.shape[0]
    n_w = -(-w_rows * cols // 128)
    w_blocks = w_out.reshape(w_rows, blocks // count, cols // 8, count, 8).transpose(1, 3, 0, 2, 4)
    w_blocks = w_blocks.reshape(blocks, w_rows * cols)
    w_blocks = jnp.pad(w_blocks, ((0, 0), (0, n_w * 128 - w_rows * cols))).reshape(blocks, n_w, 128)

    n_a = pair * group * HEAD_DIM // 128
    half_rows = group_ids.shape[0] // 2
    stream = lax.axis_index("guide")
    weight_rows = request_weights(group_ids, weight_index, guidance_levels)
    weight_rows = lax.dynamic_slice(weight_rows, (stream.astype(jnp.uint32) * half_rows,), (half_rows,))
    weight_rows = jnp.broadcast_to(weight_rows[:, None], (half_rows, w_vocab.shape[1]))
    parts = width // 384
    expert = lax.div(block * w_gate.shape[1], EXPERT_UNITS)
    where = jnp.stack([expert, lax.div(block, parts), lax.rem(block, parts), z])
    where = jnp.concatenate([where, lengths.reshape(count)])
    got, weight_rows, stream, where = lax.optimization_barrier((got, weight_rows, stream, where))
    sent, fresh = attended(where, got, w_blocks)
    got = exchange(sent, BLK)

    w_cols = got[:, n_a:].reshape(blocks, n_w * 128)[:, : w_rows * cols].reshape(-1, cols)
    attn = got[:, :n_a].reshape(ny, nz, group, pair, HEAD_DIM).transpose(3, 1, 0, 2, 4).reshape(count, width_q)
    part = jnp.dot(attn, w_cols, preferred_element_type=F32)
    own_lines = count * cols // 128
    part = part.reshape(count, own_lines, 8).transpose(1, 0, 2)
    high, low = halves(part.reshape(own_lines, 128))
    got = exchange(to_all(jnp.concatenate([high, low], axis=0), blocks), BLK)
    expert_in, share, mixed_piece = routed(where, got, hidden[0], router.T, routes[0].T)
    sent = expert_payload(expert_in, share, fresh, w_gate, w_up, w_down)
    got = exchange(sent.reshape(blocks, 2 * own_lines + 2, 128), BLK)
    fresh = got

    piece = jnp.sum(got[:, :own_lines].astype(F32) + got[:, own_lines : 2 * own_lines].astype(F32), axis=0)
    piece = (mixed_piece + piece).astype(BF16)
    piece = jnp.concatenate([piece, jnp.zeros((1, 128), BF16)], axis=0)
    everyone = blocks * lax.axis_size("batch")
    got = exchange(jnp.broadcast_to(piece[None], (everyone,) + piece.shape), ("batch",) + BLK)
    outgoing = lax.optimization_barrier(got[:, :own_lines].astype(F32).reshape(-1, width))
    final_in = rms(outgoing).astype(BF16)
    stream_logits = jnp.dot(final_in, w_vocab, preferred_element_type=F32).astype(BF16)
    both = lax.all_gather(stream_logits, "guide", axis=0, tiled=False)
    return last_outputs(stream, both, weight_rows, fresh, count, width_k)


def last_kernel(stream_ref, both_ref, weight_ref, fresh_ref, logits_ref, key_ref, value_ref, held):
    half_rows = logits_ref.shape[0]
    first = stream_ref[0] == 0
    cond = jnp.where(first, both_ref[0, :half_rows], both_ref[0, half_rows:]).astype(F32)
    uncond = jnp.where(first, both_ref[1, :half_rows], both_ref[1, half_rows:]).astype(F32)
    logits_ref[...] = uncond + weight_ref[...] * (cond - uncond)
    held[...] = fresh_ref[:, 6:, :].astype(F32)
    half = key_ref.shape[1] // 2
    low_lane = lax.broadcasted_iota(jnp.int32, (half, 128), 1) < 64
    for n, out_ref in ((0, key_ref), (1, value_ref)):
        for v in range(out_ref.shape[2] // 128):
            even = held[2 * half * v : 2 * half * v + half, n, :]
            odd = held[2 * half * v + half : 2 * half * v + 2 * half, n, :]
            first = jnp.where(low_lane, even, pltpu.roll(odd, 64, 1))
            second = jnp.where(low_lane, pltpu.roll(even, 64, 1), odd)
            both = jnp.concatenate([first, second], axis=0)
            out_ref[0, :, 128 * v : 128 * v + 128] = both.astype(BF16)


def last_outputs(stream, both, weight_rows, fresh, count, width_k):
    return pl.pallas_call(
        last_kernel,
        out_shape=(
            jax.ShapeDtypeStruct(weight_rows.shape, F32),
            jax.ShapeDtypeStruct((1, count, width_k), BF16),
            jax.ShapeDtypeStruct((1, count, width_k), BF16),
        ),
        in_specs=[SMEM] + [VMEM] * 3,
        out_specs=(VMEM,) * 3,
        scratch_shapes=[pltpu.VMEM((fresh.shape[0], 2, 128), F32)],
        compiler_params=pltpu.CompilerParams(vmem_limit_bytes=16 << 20),
    )(stream.reshape(1), both, weight_rows, fresh)


def attention_kernel(where_ref, got_ref, w_ref, out_ref, fresh_ref, lines):
    blocks, rows, lanes = got_ref.shape
    span = (rows - 8) // 2
    sums = jnp.sum(got_ref[:, 2 * span :, :].astype(F32), axis=0)
    fresh = sums[3:5].astype(BF16)
    fresh_ref[...] = fresh
    fresh = fresh.astype(F32)
    group = HEADS // KV_HEADS
    query = (sums[:group] + sums[group + 2 :]).astype(BF16).astype(F32)
    query = jnp.concatenate([query, jnp.zeros((8 - group, lanes), F32)], axis=0)
    low = lax.broadcasted_iota(jnp.int32, (8, lanes), 1) < HEAD_DIM
    position = lax.broadcasted_iota(jnp.int32, (8, blocks * span), 1)
    scale = HEAD_DIM ** (-0.5)
    results = []
    for i in range(2):
        cache = got_ref[:, span * i : span * i + span, :].reshape(blocks * span, lanes)
        here = jnp.where(low, query if i == 0 else pltpu.roll(query, HEAD_DIM, 1), 0.0)
        flipped = jnp.concatenate([fresh, jnp.zeros((6, lanes), F32)], axis=0)
        flipped = pltpu.roll(flipped, HEAD_DIM, 1)
        new_k = fresh[0:1] if i == 0 else flipped[0:1]
        new_v = flipped[1:2] if i == 0 else fresh[1:2]
        scores = lax.dot_general(
            here.astype(BF16), cache, (((1,), (1,)), ((), ())), preferred_element_type=F32
        )
        scores = scores * scale
        own = jnp.sum(here * new_k, axis=1, keepdims=True) * scale
        valid = position < where_ref[4 + where_ref[3] + 8 * i]
        top = jnp.maximum(jnp.max(jnp.where(valid, scores, -1e30), axis=1, keepdims=True), own)
        probs = jnp.exp(jnp.where(valid, scores - top, -1e30))
        own_prob = jnp.exp(own - top)
        total = jnp.sum(probs, axis=1, keepdims=True) + own_prob
        acc = jnp.dot(probs.astype(BF16), cache, preferred_element_type=F32)
        acc = acc + own_prob.astype(BF16).astype(F32) * new_v
        results.append(acc / total)
    attn = jnp.where(low, pltpu.roll(results[0], HEAD_DIM, 1), results[1])
    lines[:, :group, :] = jnp.broadcast_to(attn[None, :group], (blocks, group, lanes))
    lines[:, group:, :] = w_ref[...].astype(F32)
    out_ref[...] = lines[...].astype(BF16)


def attended(where, got, w_blocks):
    blocks = got.shape[0]
    return pl.pallas_call(
        attention_kernel,
        out_shape=(
            jax.ShapeDtypeStruct((blocks, 8, 128), BF16),
            jax.ShapeDtypeStruct((2, 128), BF16),
        ),
        in_specs=[SMEM] + [VMEM] * 2,
        out_specs=(VMEM,) * 2,
        scratch_shapes=[pltpu.VMEM((blocks, 8, 128), F32)],
        compiler_params=pltpu.CompilerParams(vmem_limit_bytes=16 << 20),
    )(where, got, w_blocks)


def request_weights(group_ids, weight_index, guidance_levels):
    group_count = weight_index.shape[0]
    level_count = guidance_levels.shape[0]
    in_group = (group_ids[:, None] == jnp.arange(group_count)[None, :]).astype(F32)
    level_pick = (weight_index[:, None] == jnp.arange(level_count)[None, :]).astype(F32)
    group_weight = jnp.sum(level_pick * guidance_levels[None, :], axis=1)
    return jnp.sum(in_group * group_weight[None, :], axis=1)


def to_all(lines, number):
    return jnp.broadcast_to(lines[None], (number,) + lines.shape)


def first_payload_kernel(
    block_ref, hidden_hbm, w_hbm, key_hbm, value_hbm, out_ref, hidden_ref, w_ref, key_ref, value_ref, lines, sems
):
    copies = [
        pltpu.make_async_copy(source, target, sems.at[n])
        for n, (source, target) in enumerate(
            ((hidden_hbm, hidden_ref), (w_hbm, w_ref), (key_hbm, key_ref), (value_hbm, value_ref))
        )
    ]
    for copy in copies:
        copy.start()
    count, width = hidden_ref.shape
    rows, total = w_ref.shape
    span, width_k = key_ref.shape[1:]
    nz = count // 2
    at = lax.broadcasted_iota(jnp.int32, (width, 128), 0) - block_ref[0] * rows
    pick = jnp.where(at == lax.broadcasted_iota(jnp.int32, (width, 128), 1), 1.0, 0.0).astype(BF16)
    copies[0].wait()
    normed = rms(hidden_ref[...].astype(F32)).astype(BF16)
    part = jnp.dot(normed, pick, preferred_element_type=F32)[:, :rows].astype(BF16)
    copies[1].wait()
    qkv = jnp.dot(part, w_ref[...], preferred_element_type=F32)
    low_lane = lax.broadcasted_iota(jnp.int32, (nz, 128), 1) < 64
    heads = (total - 2 * width_k) // 64
    for v in range(total // 128):
        first, second = qkv[:nz, 128 * v : 128 * v + 128], qkv[nz:, 128 * v : 128 * v + 128]
        even = jnp.where(low_lane, first, pltpu.roll(second, 64, 1))
        odd = jnp.where(low_lane, pltpu.roll(first, 64, 1), second)
        for chunk, line in ((2 * v, even), (2 * v + 1, odd)):
            if chunk < heads:
                y, row = chunk // 3, chunk % 3
                high = line.astype(BF16).astype(F32)
                lines[nz * y : nz * y + nz, 5 + row, :] = line - high
            else:
                y, row = (chunk - heads) % 8, 3 + (chunk - heads) // 8
                high = line
            lines[nz * y : nz * y + nz, row, :] = high
    out_ref[:, 2 * span :, :] = lines[...].astype(BF16)
    copies[2].wait()
    copies[3].wait()
    low_lane = lax.broadcasted_iota(jnp.int32, (count, span, 128), 2) < 64
    for m in range(width_k // 128):
        keys = key_ref[:, :, 128 * m : 128 * m + 128].astype(F32)
        values = value_ref[:, :, 128 * m : 128 * m + 128].astype(F32)
        even = jnp.where(low_lane, keys, pltpu.roll(values, 64, 2)).astype(BF16)
        odd = jnp.where(low_lane, pltpu.roll(keys, 64, 2), values).astype(BF16)
        for y, pair in ((2 * m, even), (2 * m + 1, odd)):
            for i in range(count // nz):
                out_ref[nz * y : nz * y + nz, span * i : span * i + span, :] = pair[nz * i : nz * i + nz]


def first_payload(block, hidden, w_qkv, keys, values, blocks):
    span = keys.shape[1]
    return pl.pallas_call(
        first_payload_kernel,
        out_shape=jax.ShapeDtypeStruct((blocks, 2 * span + 8, 128), BF16),
        in_specs=[SMEM] + [HBM] * 4,
        out_specs=VMEM,
        scratch_shapes=[pltpu.VMEM(a.shape, a.dtype) for a in (hidden, w_qkv, keys, values)]
        + [pltpu.VMEM((blocks, 8, 128), F32), pltpu.SemaphoreType.DMA((4,))],
        compiler_params=pltpu.CompilerParams(vmem_limit_bytes=60 << 20),
    )(block.reshape(1), hidden, w_qkv, keys, values)


def route_kernel(
    where_ref,
    got_ref,
    hidden_ref,
    router_ref,
    routes_ref,
    in_ref,
    share_ref,
    piece_ref,
    held,
    lines,
    mixed_ref,
):
    count, width = hidden_ref.shape
    got = got_ref[...].astype(F32)
    held[...] = got[:, :3] + got[:, 3:6]
    parts = width // 384
    blocks = [held[count * m : count * m + count, i, :] for m in range(parts) for i in range(3)]
    part = jnp.stack(blocks, axis=0)
    row = lax.broadcasted_iota(jnp.int32, part.shape, 1)
    lane = lax.broadcasted_iota(jnp.int32, part.shape, 2) // 8
    step = 1
    while step < count:
        down = pltpu.roll(pltpu.roll(part, count - step, 1), 8 * step, 2)
        back = pltpu.roll(pltpu.roll(part, step, 1), 128 - 8 * step, 2)
        low_row, low_lane = (row & step) == 0, (lane & step) == 0
        part = jnp.where(low_row == low_lane, part, jnp.where(low_row, down, back))
        step *= 2
    hidden = hidden_ref[...].astype(F32)
    total = jnp.zeros((count, 1), F32)
    for n in range(3 * parts):
        block = hidden[:, 128 * n : 128 * n + 128] + part[n]
        total = total + jnp.sum(block * block, axis=1, keepdims=True)
        mixed_ref[:, n // 3, n % 3, :] = block
        lines[:, 128 * n : 128 * n + 128] = block
    expert_in = (lines[...] * lax.rsqrt(total / width + EPS)).astype(BF16)
    in_ref[...] = expert_in
    piece_ref[...] = mixed_ref[where_ref[1], where_ref[2]]
    choice = lax.dot_general(
        router_ref[...], expert_in, (((1,), (1,)), ((), ())), preferred_element_type=F32
    )
    experts = lax.broadcasted_iota(jnp.int32, choice.shape, 0)
    routes = routes_ref[...]
    e1, e2 = routes[0:1], routes[1:2]
    c1 = jnp.sum(jnp.where(experts == e1, choice, 0.0), axis=0, keepdims=True)
    c2 = jnp.sum(jnp.where(experts == e2, choice, 0.0), axis=0, keepdims=True)
    first = 1.0 / (1.0 + jnp.exp(c2 - c1))
    share = jnp.where(e1 == where_ref[0], first, jnp.where(e2 == where_ref[0], 1.0 - first, 0.0))
    row = lax.broadcasted_iota(jnp.int32, (count, count), 0)
    column = lax.broadcasted_iota(jnp.int32, (count, count), 1)
    share = jnp.sum(jnp.where(row == column, share, 0.0), axis=1, keepdims=True)
    share_ref[...] = jnp.broadcast_to(share, share_ref.shape)


def routed(where, got, hidden, router, routes):
    count, width = hidden.shape
    parts = width // 384
    return pl.pallas_call(
        route_kernel,
        out_shape=(
            jax.ShapeDtypeStruct((count, width), BF16),
            jax.ShapeDtypeStruct((count, 128), F32),
            jax.ShapeDtypeStruct((3, 128), F32),
        ),
        in_specs=[SMEM] + [VMEM] * 4,
        out_specs=(VMEM,) * 3,
        scratch_shapes=[
            pltpu.VMEM((got.shape[0], 3, 128), F32),
            pltpu.VMEM((count, width), F32),
            pltpu.VMEM((count, parts, 3, 128), F32),
        ],
        compiler_params=pltpu.CompilerParams(vmem_limit_bytes=16 << 20),
    )(where, got, hidden, router, routes)


def expert_kernel(in_ref, share_ref, fresh_ref, gate_ref, up_ref, down_ref, out_ref, lines):
    expert_in = in_ref[...]
    width = expert_in.shape[1]
    gate = jnp.dot(expert_in, gate_ref[...], preferred_element_type=F32)
    upper = jnp.dot(expert_in, up_ref[...], preferred_element_type=F32)
    act = (gate / (1.0 + jnp.exp(-gate)) * upper * share_ref[:, 0:1]).astype(BF16)
    out = jnp.dot(act, down_ref[...], preferred_element_type=F32)
    for n in range(width // 128):
        line = out[:, 128 * n : 128 * n + 128]
        high = line.astype(BF16).astype(F32)
        lines[:, n // 3, n % 3, :] = high
        lines[:, n // 3, 3 + n % 3, :] = line - high
    fresh = fresh_ref[...].astype(F32)
    lines[:, :, 6:, :] = jnp.broadcast_to(fresh[None, None], lines.shape[:2] + fresh.shape)
    out_ref[...] = lines[...].astype(BF16)


def expert_payload(expert_in, share, fresh, w_gate, w_up, w_down):
    count, width = expert_in.shape
    shape = (count, width // 384, 8, 128)
    return pl.pallas_call(
        expert_kernel,
        out_shape=jax.ShapeDtypeStruct(shape, BF16),
        in_specs=[VMEM] * 6,
        out_specs=VMEM,
        scratch_shapes=[pltpu.VMEM(shape, F32)],
        compiler_params=pltpu.CompilerParams(vmem_limit_bytes=16 << 20),
    )(expert_in, share, fresh, w_gate, w_up, w_down)


def solution(mesh):
    guide, blk, batch = (mesh.shape[a] for a in ("guide", "blk", "batch"))
    ny = KV_HEADS
    mesh = Mesh(mesh.devices.reshape(guide, ny, blk // ny, batch), ("guide",) + BLK + ("batch",))
    placed = (
        P("guide", "batch", None),
        P(BLK, None),
        P("guide", "batch", BLK, None),
        P("guide", "batch", BLK, None),
        P("guide", "batch"),
        P(BLK, None),
        P(),
        P("guide", "batch", None),
        P(None, BLK),
        P(None, BLK),
        P(BLK, None),
        P(None, BLK + ("batch",)),
        P(),
        P(),
        P(),
    )
    return jax.shard_map(
        local,
        mesh=mesh,
        in_specs=placed,
        out_specs=(
            P("guide", BLK + ("batch",)),
            P("guide", "batch", None),
            P("guide", "batch", None),
        ),
        check_vma=False,
    )
```

```python
import jax
import jax.numpy as jnp
from jax import lax
from jax.experimental import pallas as pl
from jax.experimental.pallas import tpu as pltpu
from jax.sharding import Mesh, PartitionSpec as P

HEADS = 24
KV_HEADS = 8
HEAD_DIM = 64
EXPERTS = 16
EXPERT_UNITS = 1024
EPS = 1e-05
F32 = jnp.float32
BF16 = jnp.bfloat16
BLK = ("y", "z")
HBM = pl.BlockSpec(memory_space=pltpu.HBM)
VMEM = pl.BlockSpec(memory_space=pltpu.VMEM)
SMEM = pl.BlockSpec(memory_space=pltpu.SMEM)


def rms(values):
    return values * lax.rsqrt(jnp.mean(values * values, axis=-1, keepdims=True) + EPS)


def exchange(value, axes):
    return lax.all_to_all(value, axes, 0, 0, tiled=True)


def halves(value):
    high = lax.reduce_precision(value, 8, 7)
    return high.astype(BF16), (value - high).astype(BF16)


def local(
    hidden,
    w_qkv,
    key_cache,
    value_cache,
    lengths,
    w_out,
    router,
    routes,
    w_gate,
    w_up,
    w_down,
    w_vocab,
    group_ids,
    weight_index,
    guidance_levels,
):
    group = HEADS // KV_HEADS
    y, z = lax.axis_index("y"), lax.axis_index("z")
    ny, nz = lax.axis_size("y"), lax.axis_size("z")
    blocks = ny * nz
    block = y * nz + z
    count = hidden.shape[1]
    pair = count // nz
    width = hidden.shape[2]
    width_q = HEADS * HEAD_DIM
    width_k = KV_HEADS * HEAD_DIM
    span = key_cache.shape[2]
    sent = first_payload(block, hidden[0], w_qkv, key_cache[0], value_cache[0], blocks)
    got = exchange(sent, BLK)
    cols = width // blocks
    w_rows = w_out.shape[0]
    w_blocks = jnp.pad(w_out, ((0, 25 - w_rows), (0, 0)))
    w_blocks = w_blocks.reshape(5, 5, blocks // count, cols // 8, count, 8).transpose(2, 4, 1, 0, 3, 5)
    w_blocks = jnp.pad(w_blocks.reshape(blocks, 5, 5 * cols), ((0, 0), (0, 0), (0, 128 - 5 * cols)))

    half_rows = group_ids.shape[0] // 2
    stream = lax.axis_index("guide")
    weight_rows = request_weights(group_ids, weight_index, guidance_levels)
    weight_rows = lax.dynamic_slice(weight_rows, (stream.astype(jnp.uint32) * half_rows,), (half_rows,))
    weight_rows = jnp.broadcast_to(weight_rows[:, None], (half_rows, w_vocab.shape[1]))
    parts = width // 384
    expert = lax.div(block * w_gate.shape[1], EXPERT_UNITS)
    where = jnp.stack([expert, lax.div(block, parts), lax.rem(block, parts), z])
    where = jnp.concatenate([where, lengths.reshape(count)])
    got, weight_rows, stream, where = lax.optimization_barrier((got, weight_rows, stream, where))
    sent, fresh = attended(where, got, w_blocks)
    got = exchange(sent, BLK)

    own_lines = count * cols // 128
    got = exchange(projected(got, count, w_rows, width_q), BLK)

    expert_in, share, mixed_piece = routed(where, got, hidden[0], router.T, routes[0].T)
    sent = expert_payload(expert_in, share, fresh, w_gate, w_up, w_down)
    got = exchange(sent.reshape(blocks, 2 * own_lines + 2, 128), BLK)
    fresh = got

    piece = jnp.sum(got[:, :own_lines].astype(F32) + got[:, own_lines : 2 * own_lines].astype(F32), axis=0)
    piece = (mixed_piece + piece).astype(BF16)
    piece = jnp.concatenate([piece, jnp.zeros((1, 128), BF16)], axis=0)
    everyone = blocks * lax.axis_size("batch")
    got = exchange(jnp.broadcast_to(piece[None], (everyone,) + piece.shape), ("batch",) + BLK)
    outgoing = lax.optimization_barrier(got[:, :own_lines].astype(F32).reshape(-1, width))
    final_in = rms(outgoing).astype(BF16)
    stream_logits = jnp.dot(final_in, w_vocab, preferred_element_type=F32).astype(BF16)
    both = lax.all_gather(stream_logits, "guide", axis=0, tiled=False)
    return last_outputs(stream, both, weight_rows, fresh, count, width_k)


def last_kernel(stream_ref, both_ref, weight_ref, fresh_ref, logits_ref, key_ref, value_ref, held):
    half_rows = logits_ref.shape[0]
    first = stream_ref[0] == 0
    cond = jnp.where(first, both_ref[0, :half_rows], both_ref[0, half_rows:]).astype(F32)
    uncond = jnp.where(first, both_ref[1, :half_rows], both_ref[1, half_rows:]).astype(F32)
    logits_ref[...] = uncond + weight_ref[...] * (cond - uncond)
    held[...] = fresh_ref[:, 6:, :].astype(F32)
    half = key_ref.shape[1] // 2
    low_lane = lax.broadcasted_iota(jnp.int32, (half, 128), 1) < 64
    for n, out_ref in ((0, key_ref), (1, value_ref)):
        for v in range(out_ref.shape[2] // 128):
            even = held[2 * half * v : 2 * half * v + half, n, :]
            odd = held[2 * half * v + half : 2 * half * v + 2 * half, n, :]
            first = jnp.where(low_lane, even, pltpu.roll(odd, 64, 1))
            second = jnp.where(low_lane, pltpu.roll(even, 64, 1), odd)
            both = jnp.concatenate([first, second], axis=0)
            out_ref[0, :, 128 * v : 128 * v + 128] = both.astype(BF16)


def last_outputs(stream, both, weight_rows, fresh, count, width_k):
    return pl.pallas_call(
        last_kernel,
        out_shape=(
            jax.ShapeDtypeStruct(weight_rows.shape, F32),
            jax.ShapeDtypeStruct((1, count, width_k), BF16),
            jax.ShapeDtypeStruct((1, count, width_k), BF16),
        ),
        in_specs=[SMEM] + [VMEM] * 3,
        out_specs=(VMEM,) * 3,
        scratch_shapes=[pltpu.VMEM((fresh.shape[0], 2, 128), F32)],
        compiler_params=pltpu.CompilerParams(vmem_limit_bytes=16 << 20),
    )(stream.reshape(1), both, weight_rows, fresh)


def project_kernel(got_ref, out_ref, held, rows_ref, attn_ref):
    held[...] = got_ref[...].astype(F32)
    rows = rows_ref.shape[1]
    w = held[:, 3:, :]
    for g in range(5):
        here = min(5, rows - 5 * g)
        turned = w if g == 0 else pltpu.roll(w, 128 - 24 * g, 2)
        rows_ref[:, 5 * g : 5 * g + here, :] = turned[:, :here, :]
    half = attn_ref.shape[0] // 2
    low = lax.broadcasted_iota(jnp.int32, (half, 128), 1) < 64
    for v in range(attn_ref.shape[1] // 128):
        (y, h), (y2, h2) = divmod(2 * v, 3), divmod(2 * v + 1, 3)
        even = held[8 * y : 8 * y + 8, h, :]
        odd = held[8 * y2 : 8 * y2 + 8, h2, :]
        attn_ref[:half, 128 * v : 128 * v + 128] = jnp.where(low, even, pltpu.roll(odd, 64, 1))
        attn_ref[half:, 128 * v : 128 * v + 128] = jnp.where(low, pltpu.roll(even, 64, 1), odd)
    w = rows_ref[...].reshape(-1, 128).astype(BF16)
    part = jnp.dot(attn_ref[...].astype(BF16), w, preferred_element_type=F32)
    row = lax.broadcasted_iota(jnp.int32, part.shape, 0)
    lane = lax.broadcasted_iota(jnp.int32, part.shape, 1)
    highs, lows = [], []
    for i in range(3):
        group = part if i == 0 else pltpu.roll(part, 128 - 8 * i, 1)
        group = jnp.where(lane < 8, group, 0.0)
        for shift in (8, 16, 32, 64):
            group = group + pltpu.roll(group, shift, 1)
        line = jnp.sum(jnp.where(lane // 8 == row, group, 0.0), axis=0, keepdims=True)
        high = line.astype(BF16).astype(F32)
        highs.append(high)
        lows.append(line - high)
    lines = jnp.concatenate(highs + lows, axis=0)
    out_ref[...] = jnp.broadcast_to(lines[None], out_ref.shape).astype(BF16)


def projected(got, count, w_rows, width_q):
    blocks = got.shape[0]
    return pl.pallas_call(
        project_kernel,
        out_shape=jax.ShapeDtypeStruct((blocks, 6, 128), BF16),
        in_specs=[VMEM],
        out_specs=VMEM,
        scratch_shapes=[
            pltpu.VMEM((blocks, 8, 128), F32),
            pltpu.VMEM((blocks, w_rows, 128), F32),
            pltpu.VMEM((count, width_q), F32),
        ],
        compiler_params=pltpu.CompilerParams(vmem_limit_bytes=16 << 20),
    )(got)


def attention_kernel(where_ref, got_ref, w_ref, out_ref, fresh_ref, lines):
    blocks, rows, lanes = got_ref.shape
    span = (rows - 8) // 2
    sums = jnp.sum(got_ref[:, 2 * span :, :].astype(F32), axis=0)
    fresh = sums[3:5].astype(BF16)
    fresh_ref[...] = fresh
    fresh = fresh.astype(F32)
    group = HEADS // KV_HEADS
    query = (sums[:group] + sums[group + 2 :]).astype(BF16).astype(F32)
    query = jnp.concatenate([query, jnp.zeros((8 - group, lanes), F32)], axis=0)
    low = lax.broadcasted_iota(jnp.int32, (8, lanes), 1) < HEAD_DIM
    position = lax.broadcasted_iota(jnp.int32, (8, blocks * span), 1)
    scale = HEAD_DIM ** (-0.5)
    results = []
    for i in range(2):
        cache = got_ref[:, span * i : span * i + span, :].reshape(blocks * span, lanes)
        here = jnp.where(low, query if i == 0 else pltpu.roll(query, HEAD_DIM, 1), 0.0)
        flipped = jnp.concatenate([fresh, jnp.zeros((6, lanes), F32)], axis=0)
        flipped = pltpu.roll(flipped, HEAD_DIM, 1)
        new_k = fresh[0:1] if i == 0 else flipped[0:1]
        new_v = flipped[1:2] if i == 0 else fresh[1:2]
        scores = lax.dot_general(
            here.astype(BF16), cache, (((1,), (1,)), ((), ())), preferred_element_type=F32
        )
        scores = scores * scale
        own = jnp.sum(here * new_k, axis=1, keepdims=True) * scale
        valid = position < where_ref[4 + where_ref[3] + 8 * i]
        top = jnp.maximum(jnp.max(jnp.where(valid, scores, -1e30), axis=1, keepdims=True), own)
        probs = jnp.exp(jnp.where(valid, scores - top, -1e30))
        own_prob = jnp.exp(own - top)
        total = jnp.sum(probs, axis=1, keepdims=True) + own_prob
        acc = jnp.dot(probs.astype(BF16), cache, preferred_element_type=F32)
        acc = acc + own_prob.astype(BF16).astype(F32) * new_v
        results.append(acc / total)
    attn = jnp.where(low, pltpu.roll(results[0], HEAD_DIM, 1), results[1])
    lines[:, :group, :] = jnp.broadcast_to(attn[None, :group], (blocks, group, lanes))
    lines[:, group:, :] = w_ref[...].astype(F32)
    out_ref[...] = lines[...].astype(BF16)


def attended(where, got, w_blocks):
    blocks = got.shape[0]
    return pl.pallas_call(
        attention_kernel,
        out_shape=(
            jax.ShapeDtypeStruct((blocks, 8, 128), BF16),
            jax.ShapeDtypeStruct((2, 128), BF16),
        ),
        in_specs=[SMEM] + [VMEM] * 2,
        out_specs=(VMEM,) * 2,
        scratch_shapes=[pltpu.VMEM((blocks, 8, 128), F32)],
        compiler_params=pltpu.CompilerParams(vmem_limit_bytes=16 << 20),
    )(where, got, w_blocks)


def request_weights(group_ids, weight_index, guidance_levels):
    group_count = weight_index.shape[0]
    level_count = guidance_levels.shape[0]
    in_group = (group_ids[:, None] == jnp.arange(group_count)[None, :]).astype(F32)
    level_pick = (weight_index[:, None] == jnp.arange(level_count)[None, :]).astype(F32)
    group_weight = jnp.sum(level_pick * guidance_levels[None, :], axis=1)
    return jnp.sum(in_group * group_weight[None, :], axis=1)


def first_payload_kernel(
    block_ref, hidden_hbm, w_hbm, key_hbm, value_hbm, out_ref, hidden_ref, w_ref, key_ref, value_ref, lines, sems
):
    copies = [
        pltpu.make_async_copy(source, target, sems.at[n])
        for n, (source, target) in enumerate(
            ((hidden_hbm, hidden_ref), (w_hbm, w_ref), (key_hbm, key_ref), (value_hbm, value_ref))
        )
    ]
    for copy in copies:
        copy.start()
    count, width = hidden_ref.shape
    rows, total = w_ref.shape
    span, width_k = key_ref.shape[1:]
    nz = count // 2
    at = lax.broadcasted_iota(jnp.int32, (width, 128), 0) - block_ref[0] * rows
    pick = jnp.where(at == lax.broadcasted_iota(jnp.int32, (width, 128), 1), 1.0, 0.0).astype(BF16)
    copies[0].wait()
    normed = rms(hidden_ref[...].astype(F32)).astype(BF16)
    part = jnp.dot(normed, pick, preferred_element_type=F32)[:, :rows].astype(BF16)
    copies[1].wait()
    qkv = jnp.dot(part, w_ref[...], preferred_element_type=F32)
    low_lane = lax.broadcasted_iota(jnp.int32, (nz, 128), 1) < 64
    heads = (total - 2 * width_k) // 64
    for v in range(total // 128):
        first, second = qkv[:nz, 128 * v : 128 * v + 128], qkv[nz:, 128 * v : 128 * v + 128]
        even = jnp.where(low_lane, first, pltpu.roll(second, 64, 1))
        odd = jnp.where(low_lane, pltpu.roll(first, 64, 1), second)
        for chunk, line in ((2 * v, even), (2 * v + 1, odd)):
            if chunk < heads:
                y, row = chunk // 3, chunk % 3
                high = line.astype(BF16).astype(F32)
                lines[nz * y : nz * y + nz, 5 + row, :] = line - high
            else:
                y, row = (chunk - heads) % 8, 3 + (chunk - heads) // 8
                high = line
            lines[nz * y : nz * y + nz, row, :] = high
    out_ref[:, 2 * span :, :] = lines[...].astype(BF16)
    copies[2].wait()
    copies[3].wait()
    low_lane = lax.broadcasted_iota(jnp.int32, (count, span, 128), 2) < 64
    for m in range(width_k // 128):
        keys = key_ref[:, :, 128 * m : 128 * m + 128].astype(F32)
        values = value_ref[:, :, 128 * m : 128 * m + 128].astype(F32)
        even = jnp.where(low_lane, keys, pltpu.roll(values, 64, 2)).astype(BF16)
        odd = jnp.where(low_lane, pltpu.roll(keys, 64, 2), values).astype(BF16)
        for y, pair in ((2 * m, even), (2 * m + 1, odd)):
            for i in range(count // nz):
                out_ref[nz * y : nz * y + nz, span * i : span * i + span, :] = pair[nz * i : nz * i + nz]


def first_payload(block, hidden, w_qkv, keys, values, blocks):
    span = keys.shape[1]
    return pl.pallas_call(
        first_payload_kernel,
        out_shape=jax.ShapeDtypeStruct((blocks, 2 * span + 8, 128), BF16),
        in_specs=[SMEM] + [HBM] * 4,
        out_specs=VMEM,
        scratch_shapes=[pltpu.VMEM(a.shape, a.dtype) for a in (hidden, w_qkv, keys, values)]
        + [pltpu.VMEM((blocks, 8, 128), F32), pltpu.SemaphoreType.DMA((4,))],
        compiler_params=pltpu.CompilerParams(vmem_limit_bytes=60 << 20),
    )(block.reshape(1), hidden, w_qkv, keys, values)


def route_kernel(
    where_ref,
    got_ref,
    hidden_ref,
    router_ref,
    routes_ref,
    in_ref,
    share_ref,
    piece_ref,
    held,
    lines,
    mixed_ref,
):
    count, width = hidden_ref.shape
    got = got_ref[...].astype(F32)
    held[...] = got[:, :3] + got[:, 3:6]
    parts = width // 384
    blocks = [held[count * m : count * m + count, i, :] for m in range(parts) for i in range(3)]
    part = jnp.stack(blocks, axis=0)
    row = lax.broadcasted_iota(jnp.int32, part.shape, 1)
    lane = lax.broadcasted_iota(jnp.int32, part.shape, 2) // 8
    step = 1
    while step < count:
        down = pltpu.roll(pltpu.roll(part, count - step, 1), 8 * step, 2)
        back = pltpu.roll(pltpu.roll(part, step, 1), 128 - 8 * step, 2)
        low_row, low_lane = (row & step) == 0, (lane & step) == 0
        part = jnp.where(low_row == low_lane, part, jnp.where(low_row, down, back))
        step *= 2
    hidden = hidden_ref[...].astype(F32)
    total = jnp.zeros((count, 1), F32)
    for n in range(3 * parts):
        block = hidden[:, 128 * n : 128 * n + 128] + part[n]
        total = total + jnp.sum(block * block, axis=1, keepdims=True)
        mixed_ref[:, n // 3, n % 3, :] = block
        lines[:, 128 * n : 128 * n + 128] = block
    expert_in = (lines[...] * lax.rsqrt(total / width + EPS)).astype(BF16)
    in_ref[...] = expert_in
    piece_ref[...] = mixed_ref[where_ref[1], where_ref[2]]
    choice = lax.dot_general(
        router_ref[...], expert_in, (((1,), (1,)), ((), ())), preferred_element_type=F32
    )
    experts = lax.broadcasted_iota(jnp.int32, choice.shape, 0)
    routes = routes_ref[...]
    e1, e2 = routes[0:1], routes[1:2]
    c1 = jnp.sum(jnp.where(experts == e1, choice, 0.0), axis=0, keepdims=True)
    c2 = jnp.sum(jnp.where(experts == e2, choice, 0.0), axis=0, keepdims=True)
    first = 1.0 / (1.0 + jnp.exp(c2 - c1))
    share = jnp.where(e1 == where_ref[0], first, jnp.where(e2 == where_ref[0], 1.0 - first, 0.0))
    row = lax.broadcasted_iota(jnp.int32, (count, count), 0)
    column = lax.broadcasted_iota(jnp.int32, (count, count), 1)
    share = jnp.sum(jnp.where(row == column, share, 0.0), axis=1, keepdims=True)
    share_ref[...] = jnp.broadcast_to(share, share_ref.shape)


def routed(where, got, hidden, router, routes):
    count, width = hidden.shape
    parts = width // 384
    return pl.pallas_call(
        route_kernel,
        out_shape=(
            jax.ShapeDtypeStruct((count, width), BF16),
            jax.ShapeDtypeStruct((count, 128), F32),
            jax.ShapeDtypeStruct((3, 128), F32),
        ),
        in_specs=[SMEM] + [VMEM] * 4,
        out_specs=(VMEM,) * 3,
        scratch_shapes=[
            pltpu.VMEM((got.shape[0], 3, 128), F32),
            pltpu.VMEM((count, width), F32),
            pltpu.VMEM((count, parts, 3, 128), F32),
        ],
        compiler_params=pltpu.CompilerParams(vmem_limit_bytes=16 << 20),
    )(where, got, hidden, router, routes)


def expert_kernel(in_ref, share_ref, fresh_ref, gate_ref, up_ref, down_ref, out_ref, lines):
    expert_in = in_ref[...]
    width = expert_in.shape[1]
    gate = jnp.dot(expert_in, gate_ref[...], preferred_element_type=F32)
    upper = jnp.dot(expert_in, up_ref[...], preferred_element_type=F32)
    act = (gate / (1.0 + jnp.exp(-gate)) * upper * share_ref[:, 0:1]).astype(BF16)
    out = jnp.dot(act, down_ref[...], preferred_element_type=F32)
    for n in range(width // 128):
        line = out[:, 128 * n : 128 * n + 128]
        high = line.astype(BF16).astype(F32)
        lines[:, n // 3, n % 3, :] = high
        lines[:, n // 3, 3 + n % 3, :] = line - high
    fresh = fresh_ref[...].astype(F32)
    lines[:, :, 6:, :] = jnp.broadcast_to(fresh[None, None], lines.shape[:2] + fresh.shape)
    out_ref[...] = lines[...].astype(BF16)


def expert_payload(expert_in, share, fresh, w_gate, w_up, w_down):
    count, width = expert_in.shape
    shape = (count, width // 384, 8, 128)
    return pl.pallas_call(
        expert_kernel,
        out_shape=jax.ShapeDtypeStruct(shape, BF16),
        in_specs=[VMEM] * 6,
        out_specs=VMEM,
        scratch_shapes=[pltpu.VMEM(shape, F32)],
        compiler_params=pltpu.CompilerParams(vmem_limit_bytes=16 << 20),
    )(expert_in, share, fresh, w_gate, w_up, w_down)


def solution(mesh):
    guide, blk, batch = (mesh.shape[a] for a in ("guide", "blk", "batch"))
    ny = KV_HEADS
    mesh = Mesh(mesh.devices.reshape(guide, ny, blk // ny, batch), ("guide",) + BLK + ("batch",))
    placed = (
        P("guide", "batch", None),
        P(BLK, None),
        P("guide", "batch", BLK, None),
        P("guide", "batch", BLK, None),
        P("guide", "batch"),
        P(BLK, None),
        P(),
        P("guide", "batch", None),
        P(None, BLK),
        P(None, BLK),
        P(BLK, None),
        P(None, BLK + ("batch",)),
        P(),
        P(),
        P(),
    )
    return jax.shard_map(
        local,
        mesh=mesh,
        in_specs=placed,
        out_specs=(
            P("guide", BLK + ("batch",)),
            P("guide", "batch", None),
            P("guide", "batch", None),
        ),
        check_vma=False,
    )
```

```python
import jax
import jax.numpy as jnp
from jax import lax
from jax.experimental import pallas as pl
from jax.experimental.pallas import tpu as pltpu
from jax.sharding import Mesh, PartitionSpec as P

HEADS = 24
KV_HEADS = 8
HEAD_DIM = 64
EXPERTS = 16
EXPERT_UNITS = 1024
EPS = 1e-05
F32 = jnp.float32
BF16 = jnp.bfloat16
BLK = ("y", "z")
HBM = pl.BlockSpec(memory_space=pltpu.HBM)
VMEM = pl.BlockSpec(memory_space=pltpu.VMEM)
SMEM = pl.BlockSpec(memory_space=pltpu.SMEM)


def rms(values):
    return values * lax.rsqrt(jnp.mean(values * values, axis=-1, keepdims=True) + EPS)


def exchange(value, axes):
    return lax.all_to_all(value, axes, 0, 0, tiled=True)


def halves(value):
    high = lax.reduce_precision(value, 8, 7)
    return high.astype(BF16), (value - high).astype(BF16)


def local(
    hidden,
    w_qkv,
    key_cache,
    value_cache,
    lengths,
    w_out,
    router,
    routes,
    w_gate,
    w_up,
    w_down,
    w_vocab,
    group_ids,
    weight_index,
    guidance_levels,
):
    group = HEADS // KV_HEADS
    y, z = lax.axis_index("y"), lax.axis_index("z")
    ny, nz = lax.axis_size("y"), lax.axis_size("z")
    blocks = ny * nz
    block = y * nz + z
    count = hidden.shape[1]
    pair = count // nz
    width = hidden.shape[2]
    width_q = HEADS * HEAD_DIM
    width_k = KV_HEADS * HEAD_DIM
    span = key_cache.shape[2]
    sent = first_payload(block, hidden[0], w_qkv, key_cache[0], value_cache[0], blocks)
    got = exchange(sent, BLK)
    cols = width // blocks
    w_rows = w_out.shape[0]
    w_blocks = jnp.pad(w_out, ((0, 25 - w_rows), (0, 0)))
    w_blocks = w_blocks.reshape(5, 5, blocks // count, cols // 8, count, 8).transpose(2, 4, 1, 0, 3, 5)
    w_blocks = jnp.pad(w_blocks.reshape(blocks, 5, 5 * cols), ((0, 0), (0, 0), (0, 128 - 5 * cols)))

    half_rows = group_ids.shape[0] // 2
    stream = lax.axis_index("guide")
    weight_rows = request_weights(group_ids, weight_index, guidance_levels)
    weight_rows = lax.dynamic_slice(weight_rows, (stream.astype(jnp.uint32) * half_rows,), (half_rows,))
    weight_rows = jnp.broadcast_to(weight_rows[:, None], (half_rows, w_vocab.shape[1]))
    parts = width // 384
    expert = lax.div(block * w_gate.shape[1], EXPERT_UNITS)
    where = jnp.stack([expert, lax.div(block, parts), lax.rem(block, parts), z])
    where = jnp.concatenate([where, lengths.reshape(count)])
    got, weight_rows, stream, where = lax.optimization_barrier((got, weight_rows, stream, where))
    sent, fresh = attended(where, got, w_blocks)
    got = exchange(sent, BLK)

    own_lines = count * cols // 128
    got = exchange(projected(got, count, w_rows, width_q), BLK)

    expert_in, share, mixed_piece = routed(where, got, hidden[0], router.T, routes[0].T)
    sent = expert_payload(expert_in, share, fresh, w_gate, w_up, w_down)
    got = exchange(sent.reshape(blocks, 2 * own_lines + 2, 128), BLK)
    fresh = got

    piece = jnp.sum(got[:, :own_lines].astype(F32) + got[:, own_lines : 2 * own_lines].astype(F32), axis=0)
    piece = (mixed_piece + piece).astype(BF16)
    piece = jnp.concatenate([piece, jnp.zeros((1, 128), BF16)], axis=0)
    everyone = blocks * lax.axis_size("batch")
    got = exchange(jnp.broadcast_to(piece[None], (everyone,) + piece.shape), ("batch",) + BLK)
    outgoing = lax.optimization_barrier(got[:, :own_lines].astype(F32).reshape(-1, width))
    final_in = rms(outgoing).astype(BF16)
    stream_logits = jnp.dot(final_in, w_vocab, preferred_element_type=F32).astype(BF16)
    both = lax.all_gather(stream_logits, "guide", axis=0, tiled=False)
    return last_outputs(stream, both, weight_rows, fresh, count, width_k)


def last_kernel(stream_ref, both_ref, weight_ref, fresh_ref, logits_ref, key_ref, value_ref, held):
    half_rows = logits_ref.shape[0]
    first = stream_ref[0] == 0
    cond = jnp.where(first, both_ref[0, :half_rows], both_ref[0, half_rows:]).astype(F32)
    uncond = jnp.where(first, both_ref[1, :half_rows], both_ref[1, half_rows:]).astype(F32)
    logits_ref[...] = uncond + weight_ref[...] * (cond - uncond)
    held[...] = fresh_ref[:, 6:, :].astype(F32)
    half = key_ref.shape[1] // 2
    low_lane = lax.broadcasted_iota(jnp.int32, (half, 128), 1) < 64
    for n, out_ref in ((0, key_ref), (1, value_ref)):
        for v in range(out_ref.shape[2] // 128):
            even = held[2 * half * v : 2 * half * v + half, n, :]
            odd = held[2 * half * v + half : 2 * half * v + 2 * half, n, :]
            first = jnp.where(low_lane, even, pltpu.roll(odd, 64, 1))
            second = jnp.where(low_lane, pltpu.roll(even, 64, 1), odd)
            both = jnp.concatenate([first, second], axis=0)
            out_ref[0, :, 128 * v : 128 * v + 128] = both.astype(BF16)


def last_outputs(stream, both, weight_rows, fresh, count, width_k):
    return pl.pallas_call(
        last_kernel,
        out_shape=(
            jax.ShapeDtypeStruct(weight_rows.shape, F32),
            jax.ShapeDtypeStruct((1, count, width_k), BF16),
            jax.ShapeDtypeStruct((1, count, width_k), BF16),
        ),
        in_specs=[SMEM] + [VMEM] * 3,
        out_specs=(VMEM,) * 3,
        scratch_shapes=[pltpu.VMEM((fresh.shape[0], 2, 128), F32)],
        compiler_params=pltpu.CompilerParams(vmem_limit_bytes=16 << 20),
    )(stream.reshape(1), both, weight_rows, fresh)


def project_kernel(got_ref, out_ref, held, rows_ref, attn_ref):
    held[...] = got_ref[...].astype(F32)
    rows = rows_ref.shape[1]
    w = held[:, 3:, :]
    for g in range(5):
        here = min(5, rows - 5 * g)
        turned = w if g == 0 else pltpu.roll(w, 128 - 24 * g, 2)
        rows_ref[:, 5 * g : 5 * g + here, :] = turned[:, :here, :]
    half = attn_ref.shape[0] // 2
    low = lax.broadcasted_iota(jnp.int32, (half, 128), 1) < 64
    for v in range(attn_ref.shape[1] // 128):
        (y, h), (y2, h2) = divmod(2 * v, 3), divmod(2 * v + 1, 3)
        even = held[8 * y : 8 * y + 8, h, :]
        odd = held[8 * y2 : 8 * y2 + 8, h2, :]
        attn_ref[:half, 128 * v : 128 * v + 128] = jnp.where(low, even, pltpu.roll(odd, 64, 1))
        attn_ref[half:, 128 * v : 128 * v + 128] = jnp.where(low, pltpu.roll(even, 64, 1), odd)
    w = rows_ref[...].reshape(-1, 128).astype(BF16)
    part = jnp.dot(attn_ref[...].astype(BF16), w, preferred_element_type=F32)
    row = lax.broadcasted_iota(jnp.int32, part.shape, 0)
    lane = lax.broadcasted_iota(jnp.int32, part.shape, 1)
    highs, lows = [], []
    for i in range(3):
        group = part if i == 0 else pltpu.roll(part, 128 - 8 * i, 1)
        group = jnp.where(lane < 8, group, 0.0)
        for shift in (8, 16, 32, 64):
            group = group + pltpu.roll(group, shift, 1)
        line = jnp.sum(jnp.where(lane // 8 == row, group, 0.0), axis=0, keepdims=True)
        high = line.astype(BF16).astype(F32)
        highs.append(high)
        lows.append(line - high)
    lines = jnp.concatenate(highs + lows, axis=0)
    out_ref[...] = jnp.broadcast_to(lines[None], out_ref.shape).astype(BF16)


def projected(got, count, w_rows, width_q):
    blocks = got.shape[0]
    return pl.pallas_call(
        project_kernel,
        out_shape=jax.ShapeDtypeStruct((blocks, 6, 128), BF16),
        in_specs=[VMEM],
        out_specs=VMEM,
        scratch_shapes=[
            pltpu.VMEM((blocks, 8, 128), F32),
            pltpu.VMEM((blocks, w_rows, 128), F32),
            pltpu.VMEM((count, width_q), F32),
        ],
        compiler_params=pltpu.CompilerParams(vmem_limit_bytes=16 << 20),
    )(got)


def attention_kernel(where_ref, got_ref, w_ref, out_ref, fresh_ref, lines):
    blocks, rows, lanes = got_ref.shape
    span = (rows - 8) // 2
    sums = jnp.sum(got_ref[:, 2 * span :, :].astype(F32), axis=0)
    fresh = sums[3:5].astype(BF16)
    fresh_ref[...] = fresh
    fresh = fresh.astype(F32)
    group = HEADS // KV_HEADS
    query = (sums[:group] + sums[group + 2 :]).astype(BF16).astype(F32)
    query = jnp.concatenate([query, jnp.zeros((8 - group, lanes), F32)], axis=0)
    low = lax.broadcasted_iota(jnp.int32, (8, lanes), 1) < HEAD_DIM
    position = lax.broadcasted_iota(jnp.int32, (8, blocks * span), 1)
    scale = HEAD_DIM ** (-0.5)
    results = []
    for i in range(2):
        cache = got_ref[:, span * i : span * i + span, :].reshape(blocks * span, lanes)
        here = jnp.where(low, query if i == 0 else pltpu.roll(query, HEAD_DIM, 1), 0.0)
        flipped = jnp.concatenate([fresh, jnp.zeros((6, lanes), F32)], axis=0)
        flipped = pltpu.roll(flipped, HEAD_DIM, 1)
        new_k = fresh[0:1] if i == 0 else flipped[0:1]
        new_v = flipped[1:2] if i == 0 else fresh[1:2]
        scores = lax.dot_general(
            here.astype(BF16), cache, (((1,), (1,)), ((), ())), preferred_element_type=F32
        )
        scores = scores * scale
        own = jnp.sum(here * new_k, axis=1, keepdims=True) * scale
        valid = position < where_ref[4 + where_ref[3] + 8 * i]
        top = jnp.maximum(jnp.max(jnp.where(valid, scores, -1e30), axis=1, keepdims=True), own)
        probs = jnp.exp(jnp.where(valid, scores - top, -1e30))
        own_prob = jnp.exp(own - top)
        total = jnp.sum(probs, axis=1, keepdims=True) + own_prob
        acc = jnp.dot(probs.astype(BF16), cache, preferred_element_type=F32)
        acc = acc + own_prob.astype(BF16).astype(F32) * new_v
        results.append(acc / total)
    attn = jnp.where(low, pltpu.roll(results[0], HEAD_DIM, 1), results[1])
    lines[:, :group, :] = jnp.broadcast_to(attn[None, :group], (blocks, group, lanes))
    lines[:, group:, :] = w_ref[...].astype(F32)
    out_ref[...] = lines[...].astype(BF16)


def attended(where, got, w_blocks):
    blocks = got.shape[0]
    return pl.pallas_call(
        attention_kernel,
        out_shape=(
            jax.ShapeDtypeStruct((blocks, 8, 128), BF16),
            jax.ShapeDtypeStruct((2, 128), BF16),
        ),
        in_specs=[SMEM] + [VMEM] * 2,
        out_specs=(VMEM,) * 2,
        scratch_shapes=[pltpu.VMEM((blocks, 8, 128), F32)],
        compiler_params=pltpu.CompilerParams(vmem_limit_bytes=16 << 20),
    )(where, got, w_blocks)


def request_weights(group_ids, weight_index, guidance_levels):
    group_count = weight_index.shape[0]
    level_count = guidance_levels.shape[0]
    in_group = (group_ids[:, None] == jnp.arange(group_count)[None, :]).astype(F32)
    level_pick = (weight_index[:, None] == jnp.arange(level_count)[None, :]).astype(F32)
    group_weight = jnp.sum(level_pick * guidance_levels[None, :], axis=1)
    return jnp.sum(in_group * group_weight[None, :], axis=1)


def first_payload_kernel(
    block_ref,
    hidden_hbm,
    w_hbm,
    key_hbm,
    value_hbm,
    out_hbm,
    hidden_ref,
    w_ref,
    key_ref,
    value_ref,
    lines,
    out_ref,
    sems,
    out_sems,
):
    copies = [
        pltpu.make_async_copy(source, target, sems.at[n])
        for n, (source, target) in enumerate(
            ((hidden_hbm, hidden_ref), (w_hbm, w_ref), (key_hbm, key_ref), (value_hbm, value_ref))
        )
    ]
    for copy in copies:
        copy.start()
    count, width = hidden_ref.shape
    rows, total = w_ref.shape
    span, width_k = key_ref.shape[1:]
    nz = count // 2
    at = lax.broadcasted_iota(jnp.int32, (width, 128), 0) - block_ref[0] * rows
    pick = jnp.where(at == lax.broadcasted_iota(jnp.int32, (width, 128), 1), 1.0, 0.0).astype(BF16)
    copies[0].wait()
    normed = rms(hidden_ref[...].astype(F32)).astype(BF16)
    part = jnp.dot(normed, pick, preferred_element_type=F32)[:, :rows].astype(BF16)
    copies[1].wait()
    qkv = jnp.dot(part, w_ref[...], preferred_element_type=F32)
    low_lane = lax.broadcasted_iota(jnp.int32, (nz, 128), 1) < 64
    heads = (total - 2 * width_k) // 64
    for v in range(total // 128):
        first, second = qkv[:nz, 128 * v : 128 * v + 128], qkv[nz:, 128 * v : 128 * v + 128]
        even = jnp.where(low_lane, first, pltpu.roll(second, 64, 1))
        odd = jnp.where(low_lane, pltpu.roll(first, 64, 1), second)
        for chunk, line in ((2 * v, even), (2 * v + 1, odd)):
            if chunk < heads:
                y, row = chunk // 3, chunk % 3
                high = line.astype(BF16).astype(F32)
                lines[nz * y : nz * y + nz, 5 + row, :] = line - high
            else:
                y, row = (chunk - heads) % 8, 3 + (chunk - heads) // 8
                high = line
            lines[nz * y : nz * y + nz, row, :] = high
    out_ref[:, 2 * span :, :] = lines[...].astype(BF16)
    copies[2].wait()
    copies[3].wait()
    writes = []
    low_lane = lax.broadcasted_iota(jnp.int32, (count, span, 128), 2) < 64
    for m in range(width_k // 128):
        keys = key_ref[:, :, 128 * m : 128 * m + 128].astype(F32)
        values = value_ref[:, :, 128 * m : 128 * m + 128].astype(F32)
        even = jnp.where(low_lane, keys, pltpu.roll(values, 64, 2)).astype(BF16)
        odd = jnp.where(low_lane, pltpu.roll(keys, 64, 2), values).astype(BF16)
        for y, pair in ((2 * m, even), (2 * m + 1, odd)):
            for i in range(count // nz):
                out_ref[nz * y : nz * y + nz, span * i : span * i + span, :] = pair[nz * i : nz * i + nz]
        piece = pl.ds(2 * nz * m, 2 * nz)
        writes.append(pltpu.make_async_copy(out_ref.at[piece], out_hbm.at[piece], out_sems.at[m]))
        writes[-1].start()
    for write in writes:
        write.wait()


def first_payload(block, hidden, w_qkv, keys, values, blocks):
    span = keys.shape[1]
    return pl.pallas_call(
        first_payload_kernel,
        out_shape=jax.ShapeDtypeStruct((blocks, 2 * span + 8, 128), BF16),
        in_specs=[SMEM] + [HBM] * 4,
        out_specs=HBM,
        scratch_shapes=[pltpu.VMEM(a.shape, a.dtype) for a in (hidden, w_qkv, keys, values)]
        + [
            pltpu.VMEM((blocks, 8, 128), F32),
            pltpu.VMEM((blocks, 2 * span + 8, 128), BF16),
            pltpu.SemaphoreType.DMA((4,)),
            pltpu.SemaphoreType.DMA((keys.shape[2] // 128,)),
        ],
        compiler_params=pltpu.CompilerParams(vmem_limit_bytes=60 << 20),
    )(block.reshape(1), hidden, w_qkv, keys, values)


def route_kernel(
    where_ref,
    got_ref,
    hidden_ref,
    router_ref,
    routes_ref,
    in_ref,
    share_ref,
    piece_ref,
    held,
    lines,
    mixed_ref,
):
    count, width = hidden_ref.shape
    got = got_ref[...].astype(F32)
    held[...] = got[:, :3] + got[:, 3:6]
    parts = width // 384
    blocks = [held[count * m : count * m + count, i, :] for m in range(parts) for i in range(3)]
    part = jnp.stack(blocks, axis=0)
    row = lax.broadcasted_iota(jnp.int32, part.shape, 1)
    lane = lax.broadcasted_iota(jnp.int32, part.shape, 2) // 8
    step = 1
    while step < count:
        down = pltpu.roll(pltpu.roll(part, count - step, 1), 8 * step, 2)
        back = pltpu.roll(pltpu.roll(part, step, 1), 128 - 8 * step, 2)
        low_row, low_lane = (row & step) == 0, (lane & step) == 0
        part = jnp.where(low_row == low_lane, part, jnp.where(low_row, down, back))
        step *= 2
    hidden = hidden_ref[...].astype(F32)
    total = jnp.zeros((count, 1), F32)
    for n in range(3 * parts):
        block = hidden[:, 128 * n : 128 * n + 128] + part[n]
        total = total + jnp.sum(block * block, axis=1, keepdims=True)
        mixed_ref[:, n // 3, n % 3, :] = block
        lines[:, 128 * n : 128 * n + 128] = block
    expert_in = (lines[...] * lax.rsqrt(total / width + EPS)).astype(BF16)
    in_ref[...] = expert_in
    piece_ref[...] = mixed_ref[where_ref[1], where_ref[2]]
    choice = lax.dot_general(
        router_ref[...], expert_in, (((1,), (1,)), ((), ())), preferred_element_type=F32
    )
    experts = lax.broadcasted_iota(jnp.int32, choice.shape, 0)
    routes = routes_ref[...]
    e1, e2 = routes[0:1], routes[1:2]
    c1 = jnp.sum(jnp.where(experts == e1, choice, 0.0), axis=0, keepdims=True)
    c2 = jnp.sum(jnp.where(experts == e2, choice, 0.0), axis=0, keepdims=True)
    first = 1.0 / (1.0 + jnp.exp(c2 - c1))
    share = jnp.where(e1 == where_ref[0], first, jnp.where(e2 == where_ref[0], 1.0 - first, 0.0))
    row = lax.broadcasted_iota(jnp.int32, (count, count), 0)
    column = lax.broadcasted_iota(jnp.int32, (count, count), 1)
    share = jnp.sum(jnp.where(row == column, share, 0.0), axis=1, keepdims=True)
    share_ref[...] = jnp.broadcast_to(share, share_ref.shape)


def routed(where, got, hidden, router, routes):
    count, width = hidden.shape
    parts = width // 384
    return pl.pallas_call(
        route_kernel,
        out_shape=(
            jax.ShapeDtypeStruct((count, width), BF16),
            jax.ShapeDtypeStruct((count, 128), F32),
            jax.ShapeDtypeStruct((3, 128), F32),
        ),
        in_specs=[SMEM] + [VMEM] * 4,
        out_specs=(VMEM,) * 3,
        scratch_shapes=[
            pltpu.VMEM((got.shape[0], 3, 128), F32),
            pltpu.VMEM((count, width), F32),
            pltpu.VMEM((count, parts, 3, 128), F32),
        ],
        compiler_params=pltpu.CompilerParams(vmem_limit_bytes=16 << 20),
    )(where, got, hidden, router, routes)


def expert_kernel(in_ref, share_ref, fresh_ref, gate_ref, up_ref, down_ref, out_ref, lines):
    expert_in = in_ref[...]
    width = expert_in.shape[1]
    gate = jnp.dot(expert_in, gate_ref[...], preferred_element_type=F32)
    upper = jnp.dot(expert_in, up_ref[...], preferred_element_type=F32)
    act = (gate / (1.0 + jnp.exp(-gate)) * upper * share_ref[:, 0:1]).astype(BF16)
    out = jnp.dot(act, down_ref[...], preferred_element_type=F32)
    for n in range(width // 128):
        line = out[:, 128 * n : 128 * n + 128]
        high = line.astype(BF16).astype(F32)
        lines[:, n // 3, n % 3, :] = high
        lines[:, n // 3, 3 + n % 3, :] = line - high
    fresh = fresh_ref[...].astype(F32)
    lines[:, :, 6:, :] = jnp.broadcast_to(fresh[None, None], lines.shape[:2] + fresh.shape)
    out_ref[...] = lines[...].astype(BF16)


def expert_payload(expert_in, share, fresh, w_gate, w_up, w_down):
    count, width = expert_in.shape
    shape = (count, width // 384, 8, 128)
    return pl.pallas_call(
        expert_kernel,
        out_shape=jax.ShapeDtypeStruct(shape, BF16),
        in_specs=[VMEM] * 6,
        out_specs=VMEM,
        scratch_shapes=[pltpu.VMEM(shape, F32)],
        compiler_params=pltpu.CompilerParams(vmem_limit_bytes=16 << 20),
    )(expert_in, share, fresh, w_gate, w_up, w_down)


def solution(mesh):
    guide, blk, batch = (mesh.shape[a] for a in ("guide", "blk", "batch"))
    ny = KV_HEADS
    mesh = Mesh(mesh.devices.reshape(guide, ny, blk // ny, batch), ("guide",) + BLK + ("batch",))
    placed = (
        P("guide", "batch", None),
        P(BLK, None),
        P("guide", "batch", BLK, None),
        P("guide", "batch", BLK, None),
        P("guide", "batch"),
        P(BLK, None),
        P(),
        P("guide", "batch", None),
        P(None, BLK),
        P(None, BLK),
        P(BLK, None),
        P(None, BLK + ("batch",)),
        P(),
        P(),
        P(),
    )
    return jax.shard_map(
        local,
        mesh=mesh,
        in_specs=placed,
        out_specs=(
            P("guide", BLK + ("batch",)),
            P("guide", "batch", None),
            P("guide", "batch", None),
        ),
        check_vma=False,
    )
```

```python
import jax
import jax.numpy as jnp
from jax import lax
from jax.experimental import pallas as pl
from jax.experimental.pallas import tpu as pltpu
from jax.sharding import Mesh, PartitionSpec as P

HEADS = 24
KV_HEADS = 8
HEAD_DIM = 64
EXPERTS = 16
EXPERT_UNITS = 1024
EPS = 1e-05
F32 = jnp.float32
BF16 = jnp.bfloat16
BLK = ("y", "z")
HBM = pl.BlockSpec(memory_space=pltpu.HBM)
VMEM = pl.BlockSpec(memory_space=pltpu.VMEM)
SMEM = pl.BlockSpec(memory_space=pltpu.SMEM)


def rms(values):
    return values * lax.rsqrt(jnp.mean(values * values, axis=-1, keepdims=True) + EPS)


def exchange(value, axes):
    return lax.all_to_all(value, axes, 0, 0, tiled=True)


def halves(value):
    high = lax.reduce_precision(value, 8, 7)
    return high.astype(BF16), (value - high).astype(BF16)


def local(
    hidden,
    w_qkv,
    key_cache,
    value_cache,
    lengths,
    w_out,
    router,
    routes,
    w_gate,
    w_up,
    w_down,
    w_vocab,
    group_ids,
    weight_index,
    guidance_levels,
):
    group = HEADS // KV_HEADS
    y, z = lax.axis_index("y"), lax.axis_index("z")
    ny, nz = lax.axis_size("y"), lax.axis_size("z")
    blocks = ny * nz
    block = y * nz + z
    count = hidden.shape[1]
    pair = count // nz
    width = hidden.shape[2]
    width_q = HEADS * HEAD_DIM
    width_k = KV_HEADS * HEAD_DIM
    span = key_cache.shape[2]
    sent = first_payload(block, hidden[0], w_qkv, key_cache[0], value_cache[0], blocks)
    got = exchange(sent, BLK)
    cols = width // blocks
    w_rows = w_out.shape[0]
    w_blocks = jnp.pad(w_out, ((0, 25 - w_rows), (0, 0)))
    w_blocks = w_blocks.reshape(5, 5, blocks // count, cols // 8, count, 8).transpose(2, 4, 1, 0, 3, 5)
    w_blocks = jnp.pad(w_blocks.reshape(blocks, 5, 5 * cols), ((0, 0), (0, 0), (0, 128 - 5 * cols)))

    half_rows = group_ids.shape[0] // 2
    stream = lax.axis_index("guide")
    weight_rows = request_weights(group_ids, weight_index, guidance_levels)
    weight_rows = lax.dynamic_slice(weight_rows, (stream.astype(jnp.uint32) * half_rows,), (half_rows,))
    weight_rows = jnp.broadcast_to(weight_rows[:, None], (half_rows, w_vocab.shape[1]))
    parts = width // 384
    expert = lax.div(block * w_gate.shape[1], EXPERT_UNITS)
    where = jnp.stack([expert, lax.div(block, parts), lax.rem(block, parts), z])
    where = jnp.concatenate([where, lengths.reshape(count)])
    got, weight_rows, stream, where = lax.optimization_barrier((got, weight_rows, stream, where))
    sent, fresh = attended(where, got, w_blocks)
    got = exchange(sent, BLK)

    own_lines = count * cols // 128
    got = exchange(projected(got, count, w_rows, width_q), BLK)

    expert_in, share, mixed_piece = routed(where, got, hidden[0], router.T, routes[0].T)
    sent = expert_payload(expert_in, share, fresh, w_gate, w_up, w_down)
    got = exchange(sent.reshape(blocks, 2 * own_lines + 2, 128), BLK)
    fresh = got

    piece = jnp.sum(got[:, :own_lines].astype(F32) + got[:, own_lines : 2 * own_lines].astype(F32), axis=0)
    piece = (mixed_piece + piece).astype(BF16)
    everyone = blocks * lax.axis_size("batch")
    got = exchange(jnp.broadcast_to(piece[None], (everyone,) + piece.shape), ("batch",) + BLK)
    outgoing = lax.optimization_barrier(got[:, :own_lines].astype(F32).reshape(-1, width))
    final_in = rms(outgoing).astype(BF16)
    stream_logits = jnp.dot(final_in, w_vocab, preferred_element_type=F32).astype(BF16)
    both = lax.all_gather(stream_logits, "guide", axis=0, tiled=False)
    return last_outputs(stream, both, weight_rows, fresh, count, width_k)


def last_kernel(stream_ref, both_ref, weight_ref, fresh_ref, logits_ref, key_ref, value_ref, held):
    half_rows = logits_ref.shape[0]
    first = stream_ref[0] == 0
    cond = jnp.where(first, both_ref[0, :half_rows], both_ref[0, half_rows:]).astype(F32)
    uncond = jnp.where(first, both_ref[1, :half_rows], both_ref[1, half_rows:]).astype(F32)
    logits_ref[...] = uncond + weight_ref[...] * (cond - uncond)
    held[...] = fresh_ref[:, 6:, :].astype(F32)
    half = key_ref.shape[1] // 2
    low_lane = lax.broadcasted_iota(jnp.int32, (half, 128), 1) < 64
    for n, out_ref in ((0, key_ref), (1, value_ref)):
        for v in range(out_ref.shape[2] // 128):
            even = held[2 * half * v : 2 * half * v + half, n, :]
            odd = held[2 * half * v + half : 2 * half * v + 2 * half, n, :]
            first = jnp.where(low_lane, even, pltpu.roll(odd, 64, 1))
            second = jnp.where(low_lane, pltpu.roll(even, 64, 1), odd)
            both = jnp.concatenate([first, second], axis=0)
            out_ref[0, :, 128 * v : 128 * v + 128] = both.astype(BF16)


def last_outputs(stream, both, weight_rows, fresh, count, width_k):
    return pl.pallas_call(
        last_kernel,
        out_shape=(
            jax.ShapeDtypeStruct(weight_rows.shape, F32),
            jax.ShapeDtypeStruct((1, count, width_k), BF16),
            jax.ShapeDtypeStruct((1, count, width_k), BF16),
        ),
        in_specs=[SMEM] + [VMEM] * 3,
        out_specs=(VMEM,) * 3,
        scratch_shapes=[pltpu.VMEM((fresh.shape[0], 2, 128), F32)],
        compiler_params=pltpu.CompilerParams(vmem_limit_bytes=16 << 20),
    )(stream.reshape(1), both, weight_rows, fresh)


def project_kernel(got_ref, out_ref, held, rows_ref, attn_ref):
    held[...] = got_ref[...].astype(F32)
    rows = rows_ref.shape[1]
    w = held[:, 3:, :]
    for g in range(5):
        here = min(5, rows - 5 * g)
        turned = w if g == 0 else pltpu.roll(w, 128 - 24 * g, 2)
        rows_ref[:, 5 * g : 5 * g + here, :] = turned[:, :here, :]
    half = attn_ref.shape[0] // 2
    low = lax.broadcasted_iota(jnp.int32, (half, 128), 1) < 64
    for v in range(attn_ref.shape[1] // 128):
        (y, h), (y2, h2) = divmod(2 * v, 3), divmod(2 * v + 1, 3)
        even = held[8 * y : 8 * y + 8, h, :]
        odd = held[8 * y2 : 8 * y2 + 8, h2, :]
        attn_ref[:half, 128 * v : 128 * v + 128] = jnp.where(low, even, pltpu.roll(odd, 64, 1))
        attn_ref[half:, 128 * v : 128 * v + 128] = jnp.where(low, pltpu.roll(even, 64, 1), odd)
    w = rows_ref[...].reshape(-1, 128).astype(BF16)
    part = jnp.dot(attn_ref[...].astype(BF16), w, preferred_element_type=F32)
    row = lax.broadcasted_iota(jnp.int32, part.shape, 0)
    lane = lax.broadcasted_iota(jnp.int32, part.shape, 1)
    highs, lows = [], []
    for i in range(3):
        group = part if i == 0 else pltpu.roll(part, 128 - 8 * i, 1)
        group = jnp.where(lane < 8, group, 0.0)
        for shift in (8, 16, 32, 64):
            group = group + pltpu.roll(group, shift, 1)
        line = jnp.sum(jnp.where(lane // 8 == row, group, 0.0), axis=0, keepdims=True)
        high = line.astype(BF16).astype(F32)
        highs.append(high)
        lows.append(line - high)
    lines = jnp.concatenate(highs + lows, axis=0)
    out_ref[...] = jnp.broadcast_to(lines[None], out_ref.shape).astype(BF16)


def projected(got, count, w_rows, width_q):
    blocks = got.shape[0]
    return pl.pallas_call(
        project_kernel,
        out_shape=jax.ShapeDtypeStruct((blocks, 6, 128), BF16),
        in_specs=[VMEM],
        out_specs=VMEM,
        scratch_shapes=[
            pltpu.VMEM((blocks, 8, 128), F32),
            pltpu.VMEM((blocks, w_rows, 128), F32),
            pltpu.VMEM((count, width_q), F32),
        ],
        compiler_params=pltpu.CompilerParams(vmem_limit_bytes=16 << 20),
    )(got)


def attention_kernel(where_ref, got_ref, w_ref, out_ref, fresh_ref, lines):
    blocks, rows, lanes = got_ref.shape
    span = (rows - 8) // 2
    sums = jnp.sum(got_ref[:, 2 * span :, :].astype(F32), axis=0)
    fresh = sums[3:5].astype(BF16)
    fresh_ref[...] = fresh
    fresh = fresh.astype(F32)
    group = HEADS // KV_HEADS
    query = (sums[:group] + sums[group + 2 :]).astype(BF16).astype(F32)
    query = jnp.concatenate([query, jnp.zeros((8 - group, lanes), F32)], axis=0)
    low = lax.broadcasted_iota(jnp.int32, (8, lanes), 1) < HEAD_DIM
    position = lax.broadcasted_iota(jnp.int32, (8, blocks * span), 1)
    scale = HEAD_DIM ** (-0.5)
    results = []
    for i in range(2):
        cache = got_ref[:, span * i : span * i + span, :].reshape(blocks * span, lanes)
        here = jnp.where(low, query if i == 0 else pltpu.roll(query, HEAD_DIM, 1), 0.0)
        flipped = jnp.concatenate([fresh, jnp.zeros((6, lanes), F32)], axis=0)
        flipped = pltpu.roll(flipped, HEAD_DIM, 1)
        new_k = fresh[0:1] if i == 0 else flipped[0:1]
        new_v = flipped[1:2] if i == 0 else fresh[1:2]
        scores = lax.dot_general(
            here.astype(BF16), cache, (((1,), (1,)), ((), ())), preferred_element_type=F32
        )
        scores = scores * scale
        own = jnp.sum(here * new_k, axis=1, keepdims=True) * scale
        valid = position < where_ref[4 + where_ref[3] + 8 * i]
        top = jnp.maximum(jnp.max(jnp.where(valid, scores, -1e30), axis=1, keepdims=True), own)
        probs = jnp.exp(jnp.where(valid, scores - top, -1e30))
        own_prob = jnp.exp(own - top)
        total = jnp.sum(probs, axis=1, keepdims=True) + own_prob
        acc = jnp.dot(probs.astype(BF16), cache, preferred_element_type=F32)
        acc = acc + own_prob.astype(BF16).astype(F32) * new_v
        results.append(acc / total)
    attn = jnp.where(low, pltpu.roll(results[0], HEAD_DIM, 1), results[1])
    lines[:, :group, :] = jnp.broadcast_to(attn[None, :group], (blocks, group, lanes))
    lines[:, group:, :] = w_ref[...].astype(F32)
    out_ref[...] = lines[...].astype(BF16)


def attended(where, got, w_blocks):
    blocks = got.shape[0]
    return pl.pallas_call(
        attention_kernel,
        out_shape=(
            jax.ShapeDtypeStruct((blocks, 8, 128), BF16),
            jax.ShapeDtypeStruct((2, 128), BF16),
        ),
        in_specs=[SMEM] + [VMEM] * 2,
        out_specs=(VMEM,) * 2,
        scratch_shapes=[pltpu.VMEM((blocks, 8, 128), F32)],
        compiler_params=pltpu.CompilerParams(vmem_limit_bytes=16 << 20),
    )(where, got, w_blocks)


def request_weights(group_ids, weight_index, guidance_levels):
    group_count = weight_index.shape[0]
    level_count = guidance_levels.shape[0]
    in_group = (group_ids[:, None] == jnp.arange(group_count)[None, :]).astype(F32)
    level_pick = (weight_index[:, None] == jnp.arange(level_count)[None, :]).astype(F32)
    group_weight = jnp.sum(level_pick * guidance_levels[None, :], axis=1)
    return jnp.sum(in_group * group_weight[None, :], axis=1)


def first_payload_kernel(
    block_ref,
    hidden_hbm,
    w_hbm,
    key_hbm,
    value_hbm,
    out_hbm,
    hidden_ref,
    w_ref,
    key_ref,
    value_ref,
    lines,
    out_ref,
    sems,
    out_sems,
):
    copies = [
        pltpu.make_async_copy(source, target, sems.at[n])
        for n, (source, target) in enumerate(
            ((hidden_hbm, hidden_ref), (w_hbm, w_ref), (key_hbm, key_ref), (value_hbm, value_ref))
        )
    ]
    for copy in copies:
        copy.start()
    count, width = hidden_ref.shape
    rows, total = w_ref.shape
    span, width_k = key_ref.shape[1:]
    nz = count // 2
    at = lax.broadcasted_iota(jnp.int32, (width, 128), 0) - block_ref[0] * rows
    pick = jnp.where(at == lax.broadcasted_iota(jnp.int32, (width, 128), 1), 1.0, 0.0).astype(BF16)
    copies[0].wait()
    normed = rms(hidden_ref[...].astype(F32)).astype(BF16)
    part = jnp.dot(normed, pick, preferred_element_type=F32)[:, :rows].astype(BF16)
    copies[1].wait()
    qkv = jnp.dot(part, w_ref[...], preferred_element_type=F32)
    low_lane = lax.broadcasted_iota(jnp.int32, (nz, 128), 1) < 64
    heads = (total - 2 * width_k) // 64
    for v in range(total // 128):
        first, second = qkv[:nz, 128 * v : 128 * v + 128], qkv[nz:, 128 * v : 128 * v + 128]
        even = jnp.where(low_lane, first, pltpu.roll(second, 64, 1))
        odd = jnp.where(low_lane, pltpu.roll(first, 64, 1), second)
        for chunk, line in ((2 * v, even), (2 * v + 1, odd)):
            if chunk < heads:
                y, row = chunk // 3, chunk % 3
                high = line.astype(BF16).astype(F32)
                lines[nz * y : nz * y + nz, 5 + row, :] = line - high
            else:
                y, row = (chunk - heads) % 8, 3 + (chunk - heads) // 8
                high = line
            lines[nz * y : nz * y + nz, row, :] = high
    out_ref[:, 2 * span :, :] = lines[...].astype(BF16)
    copies[2].wait()
    copies[3].wait()
    writes = []
    low_lane = lax.broadcasted_iota(jnp.int32, (count, span, 128), 2) < 64
    for m in range(width_k // 128):
        keys = key_ref[:, :, 128 * m : 128 * m + 128].astype(F32)
        values = value_ref[:, :, 128 * m : 128 * m + 128].astype(F32)
        even = jnp.where(low_lane, keys, pltpu.roll(values, 64, 2)).astype(BF16)
        odd = jnp.where(low_lane, pltpu.roll(keys, 64, 2), values).astype(BF16)
        for y, pair in ((2 * m, even), (2 * m + 1, odd)):
            for i in range(count // nz):
                out_ref[nz * y : nz * y + nz, span * i : span * i + span, :] = pair[nz * i : nz * i + nz]
        piece = pl.ds(2 * nz * m, 2 * nz)
        writes.append(pltpu.make_async_copy(out_ref.at[piece], out_hbm.at[piece], out_sems.at[m]))
        writes[-1].start()
    for write in writes:
        write.wait()


def first_payload(block, hidden, w_qkv, keys, values, blocks):
    span = keys.shape[1]
    return pl.pallas_call(
        first_payload_kernel,
        out_shape=jax.ShapeDtypeStruct((blocks, 2 * span + 8, 128), BF16),
        in_specs=[SMEM] + [HBM] * 4,
        out_specs=HBM,
        scratch_shapes=[pltpu.VMEM(a.shape, a.dtype) for a in (hidden, w_qkv, keys, values)]
        + [
            pltpu.VMEM((blocks, 8, 128), F32),
            pltpu.VMEM((blocks, 2 * span + 8, 128), BF16),
            pltpu.SemaphoreType.DMA((4,)),
            pltpu.SemaphoreType.DMA((keys.shape[2] // 128,)),
        ],
        compiler_params=pltpu.CompilerParams(vmem_limit_bytes=60 << 20),
    )(block.reshape(1), hidden, w_qkv, keys, values)


def route_kernel(
    where_ref,
    got_ref,
    hidden_ref,
    router_ref,
    routes_ref,
    in_ref,
    share_ref,
    piece_ref,
    held,
    lines,
    mixed_ref,
):
    count, width = hidden_ref.shape
    got = got_ref[...].astype(F32)
    held[...] = got[:, :3] + got[:, 3:6]
    parts = width // 384
    blocks = [held[count * m : count * m + count, i, :] for m in range(parts) for i in range(3)]
    part = jnp.stack(blocks, axis=0)
    row = lax.broadcasted_iota(jnp.int32, part.shape, 1)
    lane = lax.broadcasted_iota(jnp.int32, part.shape, 2) // 8
    step = 1
    while step < count:
        down = pltpu.roll(pltpu.roll(part, count - step, 1), 8 * step, 2)
        back = pltpu.roll(pltpu.roll(part, step, 1), 128 - 8 * step, 2)
        low_row, low_lane = (row & step) == 0, (lane & step) == 0
        part = jnp.where(low_row == low_lane, part, jnp.where(low_row, down, back))
        step *= 2
    hidden = hidden_ref[...].astype(F32)
    total = jnp.zeros((count, 1), F32)
    for n in range(3 * parts):
        block = hidden[:, 128 * n : 128 * n + 128] + part[n]
        total = total + jnp.sum(block * block, axis=1, keepdims=True)
        mixed_ref[:, n // 3, n % 3, :] = block
        lines[:, 128 * n : 128 * n + 128] = block
    expert_in = (lines[...] * lax.rsqrt(total / width + EPS)).astype(BF16)
    in_ref[...] = expert_in
    piece_ref[...] = mixed_ref[where_ref[1], where_ref[2]]
    choice = lax.dot_general(
        router_ref[...], expert_in, (((1,), (1,)), ((), ())), preferred_element_type=F32
    )
    experts = lax.broadcasted_iota(jnp.int32, choice.shape, 0)
    routes = routes_ref[...]
    e1, e2 = routes[0:1], routes[1:2]
    c1 = jnp.sum(jnp.where(experts == e1, choice, 0.0), axis=0, keepdims=True)
    c2 = jnp.sum(jnp.where(experts == e2, choice, 0.0), axis=0, keepdims=True)
    first = 1.0 / (1.0 + jnp.exp(c2 - c1))
    share = jnp.where(e1 == where_ref[0], first, jnp.where(e2 == where_ref[0], 1.0 - first, 0.0))
    row = lax.broadcasted_iota(jnp.int32, (count, count), 0)
    column = lax.broadcasted_iota(jnp.int32, (count, count), 1)
    share = jnp.sum(jnp.where(row == column, share, 0.0), axis=1, keepdims=True)
    share_ref[...] = jnp.broadcast_to(share, share_ref.shape)


def routed(where, got, hidden, router, routes):
    count, width = hidden.shape
    parts = width // 384
    return pl.pallas_call(
        route_kernel,
        out_shape=(
            jax.ShapeDtypeStruct((count, width), BF16),
            jax.ShapeDtypeStruct((count, 128), F32),
            jax.ShapeDtypeStruct((3, 128), F32),
        ),
        in_specs=[SMEM] + [VMEM] * 4,
        out_specs=(VMEM,) * 3,
        scratch_shapes=[
            pltpu.VMEM((got.shape[0], 3, 128), F32),
            pltpu.VMEM((count, width), F32),
            pltpu.VMEM((count, parts, 3, 128), F32),
        ],
        compiler_params=pltpu.CompilerParams(vmem_limit_bytes=16 << 20),
    )(where, got, hidden, router, routes)


def expert_kernel(in_ref, share_ref, fresh_ref, gate_ref, up_ref, down_ref, out_ref, lines):
    expert_in = in_ref[...]
    width = expert_in.shape[1]
    gate = jnp.dot(expert_in, gate_ref[...], preferred_element_type=F32)
    upper = jnp.dot(expert_in, up_ref[...], preferred_element_type=F32)
    act = (gate / (1.0 + jnp.exp(-gate)) * upper * share_ref[:, 0:1]).astype(BF16)
    out = jnp.dot(act, down_ref[...], preferred_element_type=F32)
    for n in range(width // 128):
        line = out[:, 128 * n : 128 * n + 128]
        high = line.astype(BF16).astype(F32)
        lines[:, n // 3, n % 3, :] = high
        lines[:, n // 3, 3 + n % 3, :] = line - high
    fresh = fresh_ref[...].astype(F32)
    lines[:, :, 6:, :] = jnp.broadcast_to(fresh[None, None], lines.shape[:2] + fresh.shape)
    out_ref[...] = lines[...].astype(BF16)


def expert_payload(expert_in, share, fresh, w_gate, w_up, w_down):
    count, width = expert_in.shape
    shape = (count, width // 384, 8, 128)
    return pl.pallas_call(
        expert_kernel,
        out_shape=jax.ShapeDtypeStruct(shape, BF16),
        in_specs=[VMEM] * 6,
        out_specs=VMEM,
        scratch_shapes=[pltpu.VMEM(shape, F32)],
        compiler_params=pltpu.CompilerParams(vmem_limit_bytes=16 << 20),
    )(expert_in, share, fresh, w_gate, w_up, w_down)


def solution(mesh):
    guide, blk, batch = (mesh.shape[a] for a in ("guide", "blk", "batch"))
    ny = KV_HEADS
    mesh = Mesh(mesh.devices.reshape(guide, ny, blk // ny, batch), ("guide",) + BLK + ("batch",))
    placed = (
        P("guide", "batch", None),
        P(BLK, None),
        P("guide", "batch", BLK, None),
        P("guide", "batch", BLK, None),
        P("guide", "batch"),
        P(BLK, None),
        P(),
        P("guide", "batch", None),
        P(None, BLK),
        P(None, BLK),
        P(BLK, None),
        P(None, BLK + ("batch",)),
        P(),
        P(),
        P(),
    )
    return jax.shard_map(
        local,
        mesh=mesh,
        in_specs=placed,
        out_specs=(
            P("guide", BLK + ("batch",)),
            P("guide", "batch", None),
            P("guide", "batch", None),
        ),
        check_vma=False,
    )
```
